256 devices in a mesh: lat: 8 (over x, z_hi), lon: 32 (over z_lo, y, core).
Axes of the slice: x: 4, y: 4, z: 8 (z_hi: 2, z_lo: 4; z = z_hi * 4 + z_lo), core: 2. Of those that a mesh axis runs over, the one named last changes fastest.
Arguments:
- fields: bfloat16 [64, 1024, 768], P('lat', 'lon'), may hold values from -60 to 60
- conv_kernel: float32 [3, 3, 768], replicated, may hold values from -1 to 1
- layer_norm_gain: float32 [768], replicated, may hold values from 0.1 to 1.9
- qkv_weight: bfloat16 [768, 2304], replicated, may hold values from -0.21875 to 0.21875
- out_weight: bfloat16 [768, 768], replicated, may hold values from -0.21875 to 0.21875
- score_bias: float32 [24, 64, 64], replicated, may hold values from -4 to 400
- pattern: int32 [8, 32, 256], P('lat', 'lon'), may hold values from 0 to 255, each once within a row
- cotangent: bfloat16 [64, 1024, 768], P('lat', 'lon'), may hold values from -6 to 6
Outputs:
- block_out: bfloat16 [64, 1024, 768], P('lat', 'lon')
- grad_fields: bfloat16 [64, 1024, 768], P('lat', 'lon')
- grad_project: float32 [768, 768], P('lat', 'lon')
- grad_kernel: float32 [3, 3, 768], replicated
- gain_gradient: float32 [768], replicated
The draws below stay inside these ranges and needn't reach their ends.
Inputs may be any that keep to these rules, and one draw needn't show every extreme that they name: pattern[a, b, :] lists each of the 256 cells of block (a, b) once.
All inputs are finite; a program needn't handle non-finite values.
Results may differ from the reference program's by a relative error of at most 0.028.
Values may be sent and summed in bfloat16 or wider, within the bound.
A program may use at most 128 MiB of HBM per device.

```python
import math
import jax
import jax.numpy as jnp
from jax import lax

LAT_DEV = 8
LON_DEV = 32
HEADS = 24
HEAD_DIM = 32
GROUP = 64
D = 768
LATS = 64
LONS = 1024
CELLS_DEV = 256
BLOCKS = 256
SLOTS = 1
TOKENS = 65536
N_LAT = 8
N_LON = 32


def draw_fields(key, part):
    base = jax.random.normal(jax.random.fold_in(key, 11), (LATS, LONS, D), jnp.float32)
    return jnp.clip(base, -6.0, 6.0).astype(jnp.bfloat16)


def draw_score_bias(key, part):
    return jnp.clip(jax.random.normal(jax.random.fold_in(key, 26), (HEADS, GROUP, GROUP), jnp.float32), -4.0, 4.0)


def shard_levels(stream_key, extent, split, low, high):
    factor_of, own = 1.0, jax.random.fold_in(stream_key, 6)
    for axis_at, shards_of in split:
        draws = jnp.exp(jax.random.uniform(jax.random.fold_in(own, axis_at), (shards_of,), jnp.float32, low / len(split), high / len(split)))
        factor_of = factor_of * jnp.repeat(draws, extent[axis_at] // shards_of).reshape([-1 if axis == axis_at else 1 for axis in range(len(extent))])
    return factor_of


def gaussian(own_key, shape, width, limit, split=(), kind=jnp.bfloat16):
    drawn = width * jax.random.normal(own_key, shape, jnp.float32)
    if split:
        drawn = drawn * shard_levels(own_key, shape, split, -0.22, 0.18)
    return jnp.clip(drawn, -limit, limit).astype(kind)


def setup_inputs(seed: int = 0) -> dict:
    arg_keys = jax.random.split(jax.random.key(seed), 9)
    fields = draw_fields(jax.random.fold_in(arg_keys[8], 71), 0)
    conv_kernel = gaussian(arg_keys[1], (3, 3, D), 0.25, 1.0, (), jnp.float32)
    layer_norm_gain = jnp.clip(1.0 + 0.18 * jax.random.normal(arg_keys[2], (D,), jnp.float32), 0.1, 1.9)
    qkv_weight = gaussian(arg_keys[3], (D, 3 * D), D ** -0.5, 0.21875)
    out_weight = gaussian(arg_keys[4], (D, D), D ** -0.5, 0.21875)
    score_bias = draw_score_bias(jax.random.fold_in(arg_keys[8], 71), 0)
    pattern = jax.vmap(lambda own: jax.random.permutation(own, CELLS_DEV))(jax.random.split(arg_keys[6], N_LAT * N_LON)).reshape((N_LAT, N_LON, CELLS_DEV)).astype(jnp.int32)
    cotangent = gaussian(arg_keys[7], (LATS, LONS, D), 1.0, 6.0, ((0, 8), (1, 32)))
    return {"fields": fields, "conv_kernel": conv_kernel, "layer_norm_gain": layer_norm_gain, "qkv_weight": qkv_weight, "out_weight": out_weight, "score_bias": score_bias, "pattern": pattern, "cotangent": cotangent}


epsilon = 1e-05

def spread(field):
    padded = jnp.pad(field, ((1, 1), (0, 0), (0, 0)))
    return jnp.concatenate([padded[:, -1:], padded, padded[:, :1]], axis=1)

def apply_taps(padded, conv_kernel, lat_rows, lon_cols):
    summed = jnp.zeros((lat_rows, lon_cols, padded.shape[2]), jnp.float32)
    for lat_tap in range(3):
        for lon_tap in range(3):
            summed = summed + conv_kernel[lat_tap, lon_tap] * padded[lat_tap:lat_tap + lat_rows, lon_tap:lon_tap + lon_cols]
    return summed

def to_owner(field, pattern):
    chans = field.shape[-1]
    blocked = field.reshape(N_LAT, LAT_DEV, N_LON, LON_DEV, chans).transpose(0, 2, 1, 3, 4)
    blocked = blocked.reshape(N_LAT, N_LON, CELLS_DEV, chans)
    slotted = jnp.take_along_axis(blocked, pattern[..., None], axis=2)
    slotted = slotted.reshape(N_LAT, N_LON, N_LAT, N_LON, SLOTS, chans).transpose(2, 3, 4, 0, 1, 5)
    return slotted.reshape(BLOCKS, CELLS_DEV, chans)

def to_grid(grouped, inverse):
    chans = grouped.shape[-1]
    slotted = grouped.reshape(N_LAT, N_LON, SLOTS, N_LAT, N_LON, chans).transpose(3, 4, 0, 1, 2, 5)
    slotted = slotted.reshape(N_LAT, N_LON, CELLS_DEV, chans)
    blocked = jnp.take_along_axis(slotted, inverse[..., None], axis=2)
    blocked = blocked.reshape(N_LAT, N_LON, LAT_DEV, LON_DEV, chans).transpose(0, 2, 1, 3, 4)
    return blocked.reshape(LATS, LONS, chans)

def attention_probs(queries, key_rows, score_bias):
    scores = jnp.einsum('gihd,gjhd->ghij', queries.astype(jnp.float32), key_rows.astype(jnp.float32))
    scores = scores * HEAD_DIM ** (-0.5) + score_bias[None]
    peak = lax.optimization_barrier(jnp.max(scores, axis=-1, keepdims=True))
    lifted = jnp.exp(scores - peak)
    return lifted / lax.optimization_barrier(jnp.sum(lifted, axis=-1, keepdims=True))

def reference(fields, conv_kernel, layer_norm_gain, qkv_weight, out_weight, score_bias, pattern, cotangent):
    scale_everywhere = 1.0 / math.sqrt(TOKENS)
    head_scale = HEAD_DIM ** (-0.5)
    group_count = CELLS_DEV // GROUP
    fields_f = fields.astype(jnp.float32)
    padded_fields = spread(fields_f)
    state_h = (fields_f + apply_taps(padded_fields, conv_kernel, LATS, LONS)).astype(jnp.bfloat16)
    state_f = state_h.astype(jnp.float32)
    mean_h = lax.optimization_barrier(jnp.mean(state_f, axis=-1, keepdims=True))
    mean_removed = state_f - mean_h
    var_h = lax.optimization_barrier(jnp.mean(mean_removed * mean_removed, axis=-1, keepdims=True))
    inverse_deviation = lax.rsqrt(var_h + epsilon)
    standardized_input = mean_removed * inverse_deviation
    normalized_fields = (standardized_input * layer_norm_gain).astype(jnp.bfloat16)
    inverse = jnp.argsort(pattern, axis=-1).astype(jnp.int32)
    normed_grouped = to_owner(normalized_fields, pattern)
    cot_grouped = to_owner(cotangent, pattern)

    def owner_step(carry, inputs):
        normed_g, cot_g = inputs
        qkv_rows = jnp.dot(normed_g, qkv_weight, preferred_element_type=jnp.float32).astype(jnp.bfloat16)
        split_rows = qkv_rows.reshape(group_count, GROUP, 3, HEADS, HEAD_DIM)
        queries = split_rows[:, :, 0]
        key_rows = split_rows[:, :, 1]
        value_rows = split_rows[:, :, 2]
        probs = attention_probs(queries, key_rows, score_bias)
        probs_low = probs.astype(jnp.bfloat16)
        attended = jnp.einsum('ghij,gjhd->gihd', probs_low.astype(jnp.float32), value_rows.astype(jnp.float32))
        attended = attended.astype(jnp.bfloat16).reshape(CELLS_DEV, D)
        mixed = jnp.dot(attended, out_weight, preferred_element_type=jnp.float32).astype(jnp.bfloat16)
        term = jnp.dot(attended.T, cot_g, preferred_element_type=jnp.float32)
        grad_att = jnp.dot(cot_g, out_weight.T, preferred_element_type=jnp.float32).astype(jnp.bfloat16)
        grad_heads = grad_att.reshape(group_count, GROUP, HEADS, HEAD_DIM).astype(jnp.float32)
        grad_probs = jnp.einsum('gihd,gjhd->ghij', grad_heads, value_rows.astype(jnp.float32))
        grad_scores = probs * (grad_probs - lax.optimization_barrier(jnp.sum(probs * grad_probs, axis=-1, keepdims=True)))
        grad_scores = grad_scores.astype(jnp.bfloat16).astype(jnp.float32)
        grad_query = jnp.einsum('ghij,gjhd->gihd', grad_scores, key_rows.astype(jnp.float32)) * head_scale
        grad_key = jnp.einsum('ghij,gihd->gjhd', grad_scores, queries.astype(jnp.float32)) * head_scale
        grad_value = jnp.einsum('ghij,gihd->gjhd', probs_low.astype(jnp.float32), grad_heads)
        grad_qkv = jnp.stack([grad_query, grad_key, grad_value], axis=2).astype(jnp.bfloat16)
        grad_qkv = grad_qkv.reshape(CELLS_DEV, 3 * D)
        grad_normed_g = jnp.dot(grad_qkv, qkv_weight.T, preferred_element_type=jnp.float32).astype(jnp.bfloat16)
        return (carry + term, (mixed, grad_normed_g))
    term_total, (mixed_all, grad_all) = lax.scan(owner_step, jnp.zeros((D, D), jnp.float32), (normed_grouped, cot_grouped))
    grad_project = term_total * scale_everywhere
    mixed_grid = to_grid(mixed_all, inverse)
    block_out = (state_f + mixed_grid.astype(jnp.float32)).astype(jnp.bfloat16)
    normalized_gradient = to_grid(grad_all, inverse).astype(jnp.float32)
    gain_gradient = lax.optimization_barrier(jnp.sum(normalized_gradient * standardized_input, axis=(0, 1))) * scale_everywhere
    gain_scaled = normalized_gradient * layer_norm_gain
    layer_norm_gradient = inverse_deviation * (gain_scaled - lax.optimization_barrier(jnp.mean(gain_scaled, axis=-1, keepdims=True)) - standardized_input * lax.optimization_barrier(jnp.mean(gain_scaled * standardized_input, axis=-1, keepdims=True)))
    grad_h = (cotangent.astype(jnp.float32) + layer_norm_gradient).astype(jnp.bfloat16)
    grad_hf = grad_h.astype(jnp.float32)
    padded_grad = spread(grad_hf)
    grad_fields = (grad_hf + apply_taps(padded_grad, conv_kernel[::-1, ::-1], LATS, LONS)).astype(jnp.bfloat16)
    kernel_terms = []
    for lat_tap in range(3):
        for lon_tap in range(3):
            kernel_terms.append(lax.optimization_barrier(jnp.sum(padded_fields[lat_tap:lat_tap + LATS, lon_tap:lon_tap + LONS] * grad_hf, axis=(0, 1))))
    grad_kernel = jnp.stack(kernel_terms).reshape(3, 3, D) * scale_everywhere
    return (block_out, grad_fields, grad_project, grad_kernel, gain_gradient)
```

```python
import math

import jax
import jax.numpy as jnp
from jax import lax
from jax.experimental import pallas as pl
from jax.experimental.pallas import tpu as pltpu
from jax.sharding import PartitionSpec as P

MESH = pl.DeviceIdType.MESH
BF = jnp.bfloat16
F32 = jnp.float32
D = 768
EPS = 1e-05
HEAD_SCALE = 32 ** (-0.5)
TOTAL_SCALE = 1.0 / math.sqrt(65536)


def nn(a, b):
    return lax.dot_general(a, b, (((1,), (0,)), ((), ())), preferred_element_type=F32)


def nt(a, b):
    return lax.dot_general(a, b, (((1,), (1,)), ((), ())), preferred_element_type=F32)


def tn(a, b):
    return lax.dot_general(a, b, (((0,), (0,)), ((), ())), preferred_element_type=F32)


def device(x, y, z, c):
    return (x * 2 + z // 4, (z % 4) * 8 + y * 2 + c)


def one_hot(cond):
    return jnp.where(cond, 1.0, 0.0).astype(BF)


def iota2(axis):
    return lax.broadcasted_iota(jnp.int32, (256, 256), axis)


def slot_order(s):
    x, zh, zl, y, c = s >> 6, (s >> 5) & 1, (s >> 3) & 3, (s >> 1) & 3, s & 1
    return x * 64 + y * 16 + zh * 8 + zl * 2 + c


def arrival_order(p):
    x, zh, zl, y, c = p >> 6, (p >> 5) & 1, (p >> 3) & 3, (p >> 1) & 3, p & 1
    return zh * 128 + zl * 32 + c * 16 + x * 4 + y


def kernel(
    fields, cot, taps, gain, pat, wqkv_hbm, wo_hbm, bias_hbm,
    block_out, grad_fields, gp_out, sums_out,
    wqkv, wo, bias, bias_t, w_sem,
    edges, edges_g, rows_in, cols_in, rows_in_g, cols_in_g, halo_s, halo_r, halo_gs, halo_gr,
    shifted, hid, xhat, rstd, work, work2, normed_w,
    perm_out, perm_home, perm_swap, perm_pos, perm_arr,
    c0, c1, c2, c3, n0, n1, n2, n3, g0, g1, g2, g3, m0, m1, m2, m3, a2a_s, a2a_r,
    cot_g, nrm_g, qkv, grad_att, att, gqkv,
    gp0, gp1, gp2, gp3, gp4, gp5, gp6, gp7, gpy_s, gpy_r, gpz_s, gpz_r, gpc_s, gpc_r, gpl_s, gpl_r,
    acc, s0, s1, s2, s3, s4, sum_s, sum_r,
):
    a = lax.axis_index("lat")
    b = lax.axis_index("lon")
    x, zh = a // 2, a % 2
    zl, y, c = b // 8, (b // 2) % 4, b % 2
    z = zh * 4 + zl
    me_b = x * 4 + y
    me_a = z * 2 + c

    def peer_b(k):
        return device(k // 4, k % 4, z, c)

    def peer_a(k):
        return device(x, y, k // 2, k % 2)

    def neighbour(da, db):
        return ((a + da + 8) % 8, (b + db + 32) % 32)

    loads = [
        pltpu.make_async_copy(wqkv_hbm, wqkv, w_sem.at[0]),
        pltpu.make_async_copy(wo_hbm, wo, w_sem.at[1]),
        pltpu.make_async_copy(bias_hbm, bias, w_sem.at[2]),
    ]
    for load in loads:
        load.start()

    bar = pltpu.get_barrier_semaphore()

    def greet(d, carry):
        pl.semaphore_signal(bar, inc=1, device_id=peer_b((me_b + d) % 16), device_id_type=MESH)
        pl.semaphore_signal(bar, inc=1, device_id=peer_a((me_a + d) % 16), device_id_type=MESH)
        return carry

    offsets = [(-1, 0), (1, 0), (0, -1), (0, 1), (-1, -1), (-1, 1), (1, -1), (1, 1)]
    for da, db in offsets:
        pl.semaphore_signal(bar, inc=1, device_id=neighbour(da, db), device_id_type=MESH)
    for d in range(1, 4):
        pl.semaphore_signal(
            bar, inc=1, device_id=device((x + d) % 4, y, (z + 4) % 8, c), device_id_type=MESH
        )
    lax.fori_loop(1, 16, greet, 0)

    row8 = lax.broadcasted_iota(jnp.int32, (8, D), 0)
    row32 = lax.broadcasted_iota(jnp.int32, (32, D), 0)

    def fill_edges(source, dest):
        left = jnp.zeros((8, D), F32)
        right = jnp.zeros((8, D), F32)
        for l in range(8):
            row = source[l].astype(F32)
            left = jnp.where(row8 == l, row[0:1, :], left)
            right = jnp.where(row8 == l, row[31:32, :], right)
        dest[0] = left.astype(BF)
        dest[1] = right.astype(BF)

    def halo_copies(source, edge, rows, cols, ss, rs):
        out = []
        routes = [
            (source.at[0], rows.at[1]), (source.at[7], rows.at[0]),
            (edge.at[0], cols.at[1]), (edge.at[1], cols.at[0]),
            (edge.at[0], cols.at[5]), (edge.at[1], cols.at[4]),
            (edge.at[0], cols.at[3]), (edge.at[1], cols.at[2]),
        ]
        for m, (src, dst) in enumerate(routes):
            out.append(
                pltpu.make_async_remote_copy(
                    src_ref=src, dst_ref=dst, send_sem=ss.at[m], recv_sem=rs.at[m],
                    device_id=neighbour(*offsets[m]), device_id_type=MESH,
                )
            )
        return out

    top_mask = (a > 0).astype(F32)
    bottom_mask = (a < 7).astype(F32)

    def fill_shifted(source, rows, cols):
        for r in range(10):
            if r == 0:
                f = rows[0].astype(F32) * top_mask
                le = cols[2].astype(F32)[7:8, :] * top_mask
                ri = cols[3].astype(F32)[7:8, :] * top_mask
            elif r == 9:
                f = rows[1].astype(F32) * bottom_mask
                le = cols[4].astype(F32)[0:1, :] * bottom_mask
                ri = cols[5].astype(F32)[0:1, :] * bottom_mask
            else:
                f = source[r - 1].astype(F32)
                le = cols[0].astype(F32)[r - 1 : r, :]
                ri = cols[1].astype(F32)[r - 1 : r, :]
            shifted[0, r] = jnp.where(row32 == 0, le, pltpu.roll(f, 1, 0))
            shifted[1, r] = f
            shifted[2, r] = jnp.where(row32 == 31, ri, pltpu.roll(f, 31, 0))

    def exchange(peer, me, src, dst, slot, sends):
        def step(d, carry):
            k = (me + d) % 16
            copy = pltpu.make_async_remote_copy(
                src_ref=src.at[k], dst_ref=dst.at[me] if sends else dst.at[k],
                send_sem=a2a_s.at[slot, d], recv_sem=a2a_r.at[slot, me if sends else k],
                device_id=peer(k), device_id_type=MESH,
            )
            if sends:
                copy.start()
            else:
                copy.wait()
            return carry

        lax.fori_loop(1, 16, step, 0)
        if sends:
            dst[me] = src[me]

    def permute(perm, src, dst):
        for n in range(3):
            cols = slice(n * 256, (n + 1) * 256)
            rows = src[..., cols].reshape(256, 256)
            got = nn(perm[...], rows).astype(BF)
            dst[..., cols] = got.reshape(dst.shape[:-1] + (256,))

    pat_hot = one_hot(iota2(0) == pat[...])
    order_hot = one_hot(iota2(0) == slot_order(iota2(1)))
    perm_out[...] = nt(order_hot, pat_hot).astype(BF)
    perm_home[...] = nt(pat_hot, order_hot).astype(BF)
    perm_swap[...] = one_hot(iota2(1) == (iota2(0) & 15) * 16 + (iota2(0) >> 4))
    perm_pos[...] = one_hot(iota2(1) == arrival_order(iota2(0)))
    perm_arr[...] = one_hot(iota2(0) == arrival_order(iota2(1)))
    fill_edges(fields, edges)
    permute(perm_out, cot, c0)

    pl.semaphore_wait(bar, 41)

    halos = halo_copies(fields, edges, rows_in, cols_in, halo_s, halo_r)
    for copy in halos:
        copy.start()
    exchange(peer_b, me_b, c0, c1, 0, True)

    loads[2].wait()
    for q in range(6):
        bias_t[q] = jnp.transpose(bias[4 * q : 4 * q + 4].reshape(256, 64))

    for copy in halos:
        copy.wait()
    fill_shifted(fields, rows_in, cols_in)
    gain_row = gain[...]

    def conv_row(l, flip):
        out = shifted[1, l + 1]
        for i in range(3):
            for j in range(3):
                t = 8 - (3 * i + j) if flip else 3 * i + j
                out = out + taps[t : t + 1, :] * shifted[j, l + i]
        return out

    def norm_row(l, carry):
        h = conv_row(l, False).astype(BF)
        hid[l] = h
        hf = h.astype(F32)
        mean = jnp.mean(hf, axis=-1, keepdims=True)
        rem = hf - mean
        var = jnp.mean(rem * rem, axis=-1, keepdims=True)
        inv = lax.rsqrt(var + EPS)
        xh = rem * inv
        xhat[l] = xh
        rstd[l] = inv
        normed_w[l] = (xh * gain_row).astype(BF)
        return carry

    lax.fori_loop(0, 8, norm_row, 0)
    permute(perm_out, normed_w, n0)
    exchange(peer_b, me_b, n0, n1, 1, True)

    exchange(peer_b, me_b, c0, c1, 0, False)
    permute(perm_swap, c1, c2)
    exchange(peer_a, me_a, c2, c3, 2, True)
    exchange(peer_b, me_b, n0, n1, 1, False)
    permute(perm_swap, n1, n2)
    exchange(peer_a, me_a, n2, n3, 3, True)

    exchange(peer_a, me_a, c2, c3, 2, False)
    permute(perm_pos, c3, cot_g)
    loads[1].wait()
    for n in range(3):
        cols = slice(n * 256, (n + 1) * 256)
        grad_att[:, cols] = nt(cot_g[...], wo[cols, :]).astype(BF)
    exchange(peer_a, me_a, n2, n3, 3, False)
    permute(perm_pos, n3, nrm_g)
    loads[0].wait()

    def project(n, carry):
        cols = pl.ds(pl.multiple_of(n * 256, 256), 256)
        qkv[:, cols] = nn(nrm_g[...], wqkv[:, cols]).astype(BF)
        return carry

    lax.fori_loop(0, 9, project, 0)

    lane_head = lax.broadcasted_iota(jnp.int32, (64, 128), 1) >> 5

    def spread(v):
        vf = v.astype(F32)
        return jnp.concatenate(
            [jnp.where(lane_head == e, vf, 0.0).astype(BF) for e in range(4)], axis=0
        )

    def gather(v):
        out = jnp.zeros((64, 128), F32)
        for e in range(4):
            out = jnp.where(lane_head == e, v[e * 64 : (e + 1) * 64, :], out)
        return out

    def attend(u, carry):
        q = u % 6
        rows = pl.ds(pl.multiple_of((u // 6) * 64, 64), 64)
        at = pl.multiple_of(q * 128, 128)
        qc = qkv[rows, pl.ds(at, 128)]
        kc = qkv[rows, pl.ds(pl.multiple_of(at + 768, 128), 128)]
        vc = qkv[rows, pl.ds(pl.multiple_of(at + 1536, 128), 128)]
        gc = grad_att[rows, pl.ds(at, 128)]
        q_bd = spread(qc)
        g_bd = spread(gc)
        st = nt(kc, q_bd) * HEAD_SCALE + bias_t[q]
        e = jnp.exp(st - jnp.max(st, axis=0, keepdims=True))
        p = e * (1.0 / jnp.sum(e, axis=0, keepdims=True))
        pb = p.astype(BF)
        att[rows, pl.ds(at, 128)] = gather(tn(pb, vc)).astype(BF)
        dp = nt(vc, g_bd)
        ds = (p * (dp - jnp.sum(p * dp, axis=0, keepdims=True))).astype(BF)
        gqkv[rows, pl.ds(at, 128)] = (gather(tn(ds, kc)) * HEAD_SCALE).astype(BF)
        gqkv[rows, pl.ds(pl.multiple_of(at + 768, 128), 128)] = (nn(ds, q_bd) * HEAD_SCALE).astype(BF)
        gqkv[rows, pl.ds(pl.multiple_of(at + 1536, 128), 128)] = nn(pb, g_bd).astype(BF)
        return carry

    lax.fori_loop(0, 24, attend, 0)

    for n in range(3):
        cols = slice(n * 256, (n + 1) * 256)
        work[:, cols] = nt(gqkv[...], wqkv[cols, :]).astype(BF)
    permute(perm_arr, work, g0)
    exchange(peer_a, me_a, g0, g1, 4, True)
    for n in range(3):
        cols = slice(n * 256, (n + 1) * 256)
        work2[:, cols] = nn(att[...], wo[:, cols]).astype(BF)
    permute(perm_arr, work2, m0)
    exchange(peer_a, me_a, m0, m1, 5, True)

    def outer(n, carry):
        cols = pl.ds(pl.multiple_of(n * 384, 128), 384)
        got = tn(cot_g[:, cols], att[...]).astype(BF)
        gp0[pl.ds(2 * n, 2)] = got.reshape(2, 4, 48, D)
        return carry

    lax.fori_loop(0, 2, outer, 0)

    def gp_y(d, sends):
        k = (y + d) % 4
        copy = pltpu.make_async_remote_copy(
            src_ref=gp0.at[:, k], dst_ref=gp1.at[y] if sends else gp1.at[k],
            send_sem=gpy_s.at[d], recv_sem=gpy_r.at[y if sends else k],
            device_id=device(x, k, z, c), device_id_type=MESH,
        )
        copy.start() if sends else copy.wait()

    def gp_z(d, sends):
        k = (zl + d) % 4
        copy = pltpu.make_async_remote_copy(
            src_ref=gp2.at[k], dst_ref=gp3.at[zl] if sends else gp3.at[k],
            send_sem=gpz_s.at[d], recv_sem=gpz_r.at[zl if sends else k],
            device_id=device(x, y, zh * 4 + k, c), device_id_type=MESH,
        )
        copy.start() if sends else copy.wait()

    def gp_l(d, sends):
        k = (a + d) % 8
        copy = pltpu.make_async_remote_copy(
            src_ref=gp6.at[k], dst_ref=gp7.at[a] if sends else gp7.at[k],
            send_sem=gpl_s.at[d], recv_sem=gpl_r.at[a if sends else k],
            device_id=(k, b), device_id_type=MESH,
        )
        copy.start() if sends else copy.wait()

    for d in range(1, 4):
        gp_y(d, True)
    for k in range(4):
        gp1[y, k] = gp0[k, y]

    exchange(peer_a, me_a, g0, g1, 4, False)
    permute(perm_swap, g1, g2)
    exchange(peer_b, me_b, g2, g3, 6, True)
    exchange(peer_a, me_a, m0, m1, 5, False)
    permute(perm_swap, m1, m2)
    exchange(peer_b, me_b, m2, m3, 7, True)

    exchange(peer_b, me_b, g2, g3, 6, False)
    permute(perm_home, g3, work)
    acc[...] = jnp.zeros_like(acc)

    def norm_back(l, carry):
        ng = work[pl.ds(pl.multiple_of(l * 32, 32), 32), :].astype(F32)
        xh = xhat[l]
        prod = ng * xh
        acc[9] += jnp.sum(prod.reshape(4, 8, D), axis=0)
        u = ng * gain_row
        mu = jnp.mean(u, axis=-1, keepdims=True)
        mux = jnp.mean(prod * gain_row, axis=-1, keepdims=True)
        gh = cot[l].astype(F32) + rstd[l] * (u - mu - xh * mux)
        normed_w[l] = gh.astype(BF)
        return carry

    lax.fori_loop(0, 8, norm_back, 0)
    fill_edges(normed_w, edges_g)
    halos = halo_copies(normed_w, edges_g, rows_in_g, cols_in_g, halo_gs, halo_gr)
    for copy in halos:
        copy.start()

    def tap_sums(l, carry):
        gh = normed_w[l].astype(F32)
        for i in range(3):
            for j in range(3):
                acc[3 * i + j] += jnp.sum((shifted[j, l + i] * gh).reshape(4, 8, D), axis=0)
        return carry

    lax.fori_loop(0, 8, tap_sums, 0)
    for k in range(16):
        if k < 10:
            s0[k] = jnp.sum(acc[k], axis=0, keepdims=True)
        else:
            s0[k] = jnp.zeros((1, D), F32)

    def sums(peer, me, src, dst, slot, whole_src, sends):
        def step(d, carry):
            k = (me + d) % 16
            copy = pltpu.make_async_remote_copy(
                src_ref=src if whole_src else src.at[k], dst_ref=dst.at[me] if sends else dst.at[k],
                send_sem=sum_s.at[slot, d], recv_sem=sum_r.at[slot, me if sends else k],
                device_id=peer(k), device_id_type=MESH,
            )
            if sends:
                copy.start()
            else:
                copy.wait()
            return carry

        lax.fori_loop(1, 16, step, 0)
        if sends:
            dst[me] = src[...] if whole_src else src[me]

    sums(peer_a, me_a, s0, s1, 0, False, True)

    for d in range(1, 4):
        gp_y(d, False)
    for k in range(4):
        total = gp1[0, k].astype(F32)
        for i in range(1, 4):
            total = total + gp1[i, k].astype(F32)
        gp2[k] = total.astype(BF)
    for d in range(1, 4):
        gp_z(d, True)
    gp3[zl] = gp2[zl]

    sums(peer_a, me_a, s0, s1, 0, False, False)
    s2[...] = jnp.sum(s1[...], axis=0)
    sums(peer_b, me_b, s2, s3, 1, True, True)

    exchange(peer_b, me_b, m2, m3, 7, False)
    permute(perm_home, m3, work2)
    for l in range(8):
        block_out[l] = (hid[l].astype(F32) + work2[l * 32 : (l + 1) * 32, :].astype(F32)).astype(BF)

    for copy in halos:
        copy.wait()
    fill_shifted(normed_w, rows_in_g, cols_in_g)

    for d in range(1, 4):
        gp_z(d, False)
    total = gp3[0].astype(F32)
    for i in range(1, 4):
        total = total + gp3[i].astype(F32)
    gp4[...] = total.reshape(2, 24, D)
    core = pltpu.make_async_remote_copy(
        src_ref=gp4.at[1 - c], dst_ref=gp5, send_sem=gpc_s, recv_sem=gpc_r,
        device_id=device(x, y, z, 1 - c), device_id_type=MESH,
    )
    core.start()

    sums(peer_b, me_b, s2, s3, 1, True, False)
    s4[...] = jnp.sum(s3[...], axis=0) * TOTAL_SCALE
    sums(peer_a, me_a, s4, sums_out, 2, True, True)

    def grad_row(l, carry):
        grad_fields[l] = conv_row(l, True).astype(BF)
        return carry

    lax.fori_loop(0, 4, grad_row, 0)
    core.wait()
    total = gp4[c] + gp5[...]
    for i in range(8):
        gp6[i, :, 0:96] = total[:, i * 96 : (i + 1) * 96]
        gp6[i, :, 96:128] = jnp.zeros((24, 32), F32)
    for d in range(1, 8):
        gp_l(d, True)
    gp7[a] = gp6[a]
    lax.fori_loop(4, 8, grad_row, 0)

    for d in range(1, 8):
        gp_l(d, False)
    gp_out[...] = jnp.sum(gp7[...], axis=0) * TOTAL_SCALE
    sums(peer_a, me_a, s4, sums_out, 2, True, False)


def body(
    fields, conv_kernel, layer_norm_gain, qkv_weight, out_weight, score_bias, pattern, cotangent
):
    vm = pl.BlockSpec(memory_space=pltpu.VMEM)
    hbm = pl.BlockSpec(memory_space=pl.ANY)
    dma = pltpu.SemaphoreType.DMA

    def vmem(shape, dtype):
        return pltpu.VMEM(shape, dtype)

    scratch = (
        [vmem((D, 3 * D), BF), vmem((D, D), BF), vmem((24, 64, 64), F32), vmem((6, 64, 256), F32), dma((3,))]
        + [vmem((2, 8, D), BF), vmem((2, 8, D), BF)]
        + [vmem((2, 32, D), BF), vmem((6, 8, D), BF)] * 2
        + [dma((8,))] * 4
        + [vmem((3, 10, 32, D), F32), vmem((8, 32, D), BF), vmem((8, 32, D), F32), vmem((8, 32, 1), F32)]
        + [vmem((256, D), BF)] * 2
        + [vmem((8, 32, D), BF)]
        + [vmem((256, 256), BF)] * 5
        + [vmem((16, 16, D), BF)] * 16
        + [dma((8, 16)), dma((8, 16))]
        + [vmem((256, D), BF), vmem((256, D), BF), vmem((256, 3 * D), BF), vmem((256, D), BF), vmem((256, D), BF), vmem((256, 3 * D), BF)]
        + [vmem((4, 4, 48, D), BF), vmem((4, 4, 48, D), BF), vmem((4, 48, D), BF), vmem((4, 48, D), BF)]
        + [vmem((2, 24, D), F32), vmem((24, D), F32), vmem((8, 24, 128), F32), vmem((8, 24, 128), F32)]
        + [dma((4,)), dma((4,)), dma((4,)), dma((4,)), dma(()), dma(()), dma((8,)), dma((8,))]
        + [vmem((10, 8, D), F32), vmem((16, 1, D), F32), vmem((16, 1, D), F32), vmem((1, D), F32), vmem((16, 1, D), F32), vmem((1, D), F32)]
        + [dma((3, 16)), dma((3, 16))]
    )
    block_out, grad_fields, gp, sums = pl.pallas_call(
        kernel,
        out_shape=(
            jax.ShapeDtypeStruct((8, 32, D), BF),
            jax.ShapeDtypeStruct((8, 32, D), BF),
            jax.ShapeDtypeStruct((24, 128), F32),
            jax.ShapeDtypeStruct((16, 1, D), F32),
        ),
        in_specs=[vm] * 5 + [hbm] * 3,
        out_specs=(vm,) * 4,
        scratch_shapes=scratch,
        name="section",
        compiler_params=pltpu.CompilerParams(
            collective_id=0, has_side_effects=True, vmem_limit_bytes=60 << 20
        ),
    )(
        fields, cotangent, conv_kernel.reshape(9, D), layer_norm_gain.reshape(1, D),
        pattern.reshape(1, 256), qkv_weight, out_weight, score_bias,
    )
    return (
        block_out,
        grad_fields,
        jnp.transpose(gp[:, :96]),
        sums[:9, 0, :].reshape(3, 3, D),
        sums[9, 0, :],
    )


def solution(mesh):
    split = P("lat", "lon", None)
    return jax.shard_map(
        body,
        mesh=mesh,
        in_specs=(split, P(), P(), P(), P(), P(), split, split),
        out_specs=(split, split, P("lat", "lon"), P(), P()),
        check_vma=False,
    )
```

```python
import math

import jax
import jax.numpy as jnp
from jax import lax
from jax.experimental import pallas as pl
from jax.experimental.pallas import tpu as pltpu
from jax.sharding import PartitionSpec as P

MESH = pl.DeviceIdType.MESH
BF = jnp.bfloat16
F32 = jnp.float32
D = 768
EPS = 1e-05
HEAD_SCALE = 32 ** (-0.5)
TOTAL_SCALE = 1.0 / math.sqrt(65536)


def nn(a, b):
    return lax.dot_general(a, b, (((1,), (0,)), ((), ())), preferred_element_type=F32)


def nt(a, b):
    return lax.dot_general(a, b, (((1,), (1,)), ((), ())), preferred_element_type=F32)


def tn(a, b):
    return lax.dot_general(a, b, (((0,), (0,)), ((), ())), preferred_element_type=F32)


def div(a, n):
    return lax.div(a, jnp.int32(n))


def rem(a, n):
    return lax.rem(a, jnp.int32(n))


def device(x, y, z, c):
    return (x * 2 + div(z, 4), rem(z, 4) * 8 + y * 2 + c)


def one_hot(cond):
    return jnp.where(cond, 1.0, 0.0).astype(BF)


def iota2(axis):
    return lax.broadcasted_iota(jnp.int32, (256, 256), axis)


def slot_order(s):
    x, zh, zl, y, c = s >> 6, (s >> 5) & 1, (s >> 3) & 3, (s >> 1) & 3, s & 1
    return x * 64 + y * 16 + zh * 8 + zl * 2 + c


def arrival_order(p):
    x, zh, zl, y, c = p >> 6, (p >> 5) & 1, (p >> 3) & 3, (p >> 1) & 3, p & 1
    return zh * 128 + zl * 32 + c * 16 + x * 4 + y


def kernel(
    fields, cot, taps, gain, pat, wqkv_hbm, wo_hbm, bias_hbm,
    block_out, grad_fields, gp_out, taps_out, gain_out,
    wqkv, wo, bias, bias_t, w_sem,
    edges, edges_g, rows_in, cols_in, rows_in_g, cols_in_g, halo_s, halo_r, halo_gs, halo_gr,
    shifted, hid, xhat, rstd, work, work2, normed_w,
    perm_out, perm_home, perm_swap, perm_pos, perm_arr,
    c0, c1, c2, c3, n0, n1, n2, n3, g0, g1, g2, g3, m0, m1, m2, m3, a2a_s, a2a_r,
    probs, cot_g, nrm_g, qkv, grad_att, att, gqkv,
    gp0, gp1, gp2, gp3, gp4, gp5, gp6, gp7, gpy_s, gpy_r, gpz_s, gpz_r, gpc_s, gpc_r, gpl_s, gpl_r,
    acc, s0, s1, s2, s3, s4, s5, sum_s, sum_r,
):
    a = lax.axis_index("lat")
    b = lax.axis_index("lon")
    x, zh = div(a, 2), rem(a, 2)
    zl, y, c = div(b, 8), rem(div(b, 2), 4), rem(b, 2)
    z = zh * 4 + zl
    me_b = x * 4 + y
    me_a = z * 2 + c

    def peer_b(k):
        return device(div(k, 4), rem(k, 4), z, c)

    def peer_a(k):
        return device(x, y, div(k, 2), rem(k, 2))

    def neighbour(da, db):
        return (rem(a + da + 8, 8), rem(b + db + 32, 32))

    loads = [
        pltpu.make_async_copy(wqkv_hbm, wqkv, w_sem.at[0]),
        pltpu.make_async_copy(wo_hbm, wo, w_sem.at[1]),
        pltpu.make_async_copy(bias_hbm, bias, w_sem.at[2]),
    ]
    for load in loads:
        load.start()

    bar = pltpu.get_barrier_semaphore()

    def greet(d, carry):
        pl.semaphore_signal(bar, inc=1, device_id=peer_b(rem(me_b + d, 16)), device_id_type=MESH)
        pl.semaphore_signal(bar, inc=1, device_id=peer_a(rem(me_a + d, 16)), device_id_type=MESH)
        return carry

    offsets = [(-1, 0), (1, 0), (0, -1), (0, 1), (-1, -1), (-1, 1), (1, -1), (1, 1)]
    for da, db in offsets:
        pl.semaphore_signal(bar, inc=1, device_id=neighbour(da, db), device_id_type=MESH)
    for d in range(1, 4):
        pl.semaphore_signal(
            bar, inc=1, device_id=device(rem(x + d, 4), y, rem(z + 4, 8), c), device_id_type=MESH
        )
    lax.fori_loop(1, 16, greet, 0)

    row8 = lax.broadcasted_iota(jnp.int32, (8, D), 0)
    row32 = lax.broadcasted_iota(jnp.int32, (32, D), 0)

    def fill_edges(source, dest):
        left = jnp.zeros((8, D), F32)
        right = jnp.zeros((8, D), F32)
        for l in range(8):
            row = source[l].astype(F32)
            left = jnp.where(row8 == l, row[0:1, :], left)
            right = jnp.where(row8 == l, row[31:32, :], right)
        dest[0] = left.astype(BF)
        dest[1] = right.astype(BF)

    def halo_copies(source, edge, rows, cols, ss, rs):
        out = []
        routes = [
            (source.at[0], rows.at[1]), (source.at[7], rows.at[0]),
            (edge.at[0], cols.at[1]), (edge.at[1], cols.at[0]),
            (edge.at[0], cols.at[5]), (edge.at[1], cols.at[4]),
            (edge.at[0], cols.at[3]), (edge.at[1], cols.at[2]),
        ]
        for m, (src, dst) in enumerate(routes):
            out.append(
                pltpu.make_async_remote_copy(
                    src_ref=src, dst_ref=dst, send_sem=ss.at[m], recv_sem=rs.at[m],
                    device_id=neighbour(*offsets[m]), device_id_type=MESH,
                )
            )
        return out

    top_mask = (a > 0).astype(F32)
    bottom_mask = (a < 7).astype(F32)

    def fill_shifted(source, rows, cols):
        for r in range(10):
            if r == 0:
                f = rows[0].astype(F32) * top_mask
                le = cols[2].astype(F32)[7:8, :] * top_mask
                ri = cols[3].astype(F32)[7:8, :] * top_mask
            elif r == 9:
                f = rows[1].astype(F32) * bottom_mask
                le = cols[4].astype(F32)[0:1, :] * bottom_mask
                ri = cols[5].astype(F32)[0:1, :] * bottom_mask
            else:
                f = source[r - 1].astype(F32)
                le = cols[0].astype(F32)[r - 1 : r, :]
                ri = cols[1].astype(F32)[r - 1 : r, :]
            shifted[0, r] = jnp.where(row32 == 0, le, pltpu.roll(f, 1, 0))
            shifted[1, r] = f
            shifted[2, r] = jnp.where(row32 == 31, ri, pltpu.roll(f, 31, 0))

    def exchange(peer, me, src, dst, slot, sends):
        def step(d, carry):
            k = rem(me + d, 16)
            copy = pltpu.make_async_remote_copy(
                src_ref=src.at[k], dst_ref=dst.at[me] if sends else dst.at[k],
                send_sem=a2a_s.at[slot, d], recv_sem=a2a_r.at[slot, me if sends else k],
                device_id=peer(k), device_id_type=MESH,
            )
            if sends:
                copy.start()
            else:
                copy.wait()
            return carry

        lax.fori_loop(1, 16, step, 0)
        if sends:
            dst[me] = src[me]

    def permute(perm, src, dst):
        for n in range(3):
            cols = slice(n * 256, (n + 1) * 256)
            rows = src[..., cols].reshape(256, 256)
            got = nn(perm[...], rows).astype(BF)
            dst[..., cols] = got.reshape(dst.shape[:-1] + (256,))

    def permute_out(perm, src, dst, half):
        rows = src[..., half * 384 : (half + 1) * 384].reshape(256, 384)
        dst[half] = nn(perm[...], rows).astype(BF).reshape(16, 16, 384)

    def permute_mid(src, dst, half):
        dst[half] = nn(perm_swap[...], src[half].reshape(256, 384)).astype(BF).reshape(16, 16, 384)

    def permute_in(perm, src, dst, half):
        got = nn(perm[...], src[half].reshape(256, 384)).astype(BF)
        dst[:, half * 384 : (half + 1) * 384] = got

    pat_hot = one_hot(iota2(0) == pat[...])
    order_hot = one_hot(iota2(0) == slot_order(iota2(1)))
    perm_out[...] = nt(order_hot, pat_hot).astype(BF)
    perm_home[...] = nt(pat_hot, order_hot).astype(BF)
    perm_swap[...] = one_hot(iota2(1) == (iota2(0) & 15) * 16 + (iota2(0) >> 4))
    perm_pos[...] = one_hot(iota2(1) == arrival_order(iota2(0)))
    perm_arr[...] = one_hot(iota2(0) == arrival_order(iota2(1)))
    fill_edges(fields, edges)
    permute_out(perm_out, cot, c0, 0)
    permute_out(perm_out, cot, c0, 1)

    pl.semaphore_wait(bar, 41)

    halos = halo_copies(fields, edges, rows_in, cols_in, halo_s, halo_r)
    for copy in halos:
        copy.start()
    exchange(peer_b, me_b, c0.at[0], c1.at[0], 0, True)
    exchange(peer_b, me_b, c0.at[1], c1.at[1], 1, True)

    loads[2].wait()
    for q in range(6):
        bias_t[q] = jnp.transpose(bias[4 * q : 4 * q + 4].reshape(256, 64))

    for copy in halos:
        copy.wait()
    fill_shifted(fields, rows_in, cols_in)
    gain_row = gain[...].reshape(1, D)

    def conv_row(l, flip):
        out = shifted[1, l + 1]
        for i in range(3):
            for j in range(3):
                ti, tj = (2 - i, 2 - j) if flip else (i, j)
                out = out + taps[ti, tj : tj + 1, :] * shifted[j, l + i]
        return out

    def norm_row(l, carry):
        h = conv_row(l, False).astype(BF)
        hid[l] = h
        hf = h.astype(F32)
        mean = jnp.mean(hf, axis=-1, keepdims=True)
        rem = hf - mean
        var = jnp.mean(rem * rem, axis=-1, keepdims=True)
        inv = lax.rsqrt(var + EPS)
        xh = rem * inv
        xhat[l] = xh
        rstd[l] = inv
        normed_w[l] = (xh * gain_row).astype(BF)
        return carry

    lax.fori_loop(0, 8, norm_row, 0)
    permute_out(perm_out, normed_w, n0, 0)
    exchange(peer_b, me_b, n0.at[0], n1.at[0], 2, True)
    permute_out(perm_out, normed_w, n0, 1)
    exchange(peer_b, me_b, n0.at[1], n1.at[1], 3, True)

    exchange(peer_b, me_b, c0.at[0], c1.at[0], 0, False)
    permute_mid(c1, c2, 0)
    exchange(peer_a, me_a, c2.at[0], c3.at[0], 4, True)
    exchange(peer_b, me_b, c0.at[1], c1.at[1], 1, False)
    permute_mid(c1, c2, 1)
    exchange(peer_b, me_b, n0.at[0], n1.at[0], 2, False)
    permute_mid(n1, n2, 0)
    exchange(peer_a, me_a, n2.at[0], n3.at[0], 6, True)
    exchange(peer_b, me_b, n0.at[1], n1.at[1], 3, False)
    permute_mid(n1, n2, 1)
    exchange(peer_a, me_a, n2.at[1], n3.at[1], 7, True)
    exchange(peer_a, me_a, c2.at[1], c3.at[1], 5, True)

    exchange(peer_a, me_a, n2.at[0], n3.at[0], 6, False)
    permute_in(perm_pos, n3, nrm_g, 0)
    exchange(peer_a, me_a, n2.at[1], n3.at[1], 7, False)
    permute_in(perm_pos, n3, nrm_g, 1)
    loads[0].wait()

    def project(n, carry):
        cols = pl.ds(pl.multiple_of(n * 256, 256), 256)
        qkv[:, cols] = nn(nrm_g[...], wqkv[:, cols]).astype(BF)
        return carry

    lax.fori_loop(0, 9, project, 0)

    lane_head = lax.broadcasted_iota(jnp.int32, (64, 128), 1) >> 5

    def spread(v):
        vf = v.astype(F32)
        return jnp.concatenate(
            [jnp.where(lane_head == e, vf, 0.0).astype(BF) for e in range(4)], axis=0
        )

    def gather(v):
        out = jnp.zeros((64, 128), F32)
        for e in range(4):
            out = jnp.where(lane_head == e, v[e * 64 : (e + 1) * 64, :], out)
        return out

    def columns(q, part):
        return pl.ds(pl.multiple_of(q * 128 + part * D, 128), 128)

    def attend(q, carry):
        for g in range(4):
            rows = slice(g * 64, (g + 1) * 64)
            q_bd = spread(qkv[rows, columns(q, 0)])
            st = nt(qkv[rows, columns(q, 1)], q_bd) * HEAD_SCALE + bias_t[q]
            e = jnp.exp(st - jnp.max(st, axis=0, keepdims=True))
            p = e * (1.0 / jnp.sum(e, axis=0, keepdims=True))
            probs[q, g] = p
            att[rows, columns(q, 0)] = gather(tn(p.astype(BF), qkv[rows, columns(q, 2)])).astype(BF)
        return carry

    def attend_back(q, carry):
        for g in range(4):
            rows = slice(g * 64, (g + 1) * 64)
            q_bd = spread(qkv[rows, columns(q, 0)])
            g_bd = spread(grad_att[rows, columns(q, 0)])
            p = probs[q, g]
            dp = nt(qkv[rows, columns(q, 2)], g_bd)
            ds = (p * (dp - jnp.sum(p * dp, axis=0, keepdims=True))).astype(BF)
            dq = gather(tn(ds, qkv[rows, columns(q, 1)])) * HEAD_SCALE
            gqkv[rows, columns(q, 0)] = dq.astype(BF)
            gqkv[rows, columns(q, 1)] = (nn(ds, q_bd) * HEAD_SCALE).astype(BF)
            gqkv[rows, columns(q, 2)] = nn(p.astype(BF), g_bd).astype(BF)
        return carry

    lax.fori_loop(0, 6, attend, 0)

    loads[1].wait()
    for n in range(3):
        cols = slice(n * 256, (n + 1) * 256)
        work2[:, cols] = nn(att[...], wo[:, cols]).astype(BF)
    permute(perm_arr, work2, m0)
    exchange(peer_a, me_a, m0, m1, 8, True)

    for h in range(2):
        exchange(peer_a, me_a, c2.at[h], c3.at[h], 4 + h, False)
        permute_in(perm_pos, c3, cot_g, h)

    def outer(n, carry):
        cols = pl.ds(pl.multiple_of(n * 384, 128), 384)
        got = tn(cot_g[:, cols], att[...]).astype(BF)
        gp0[pl.ds(2 * n, 2)] = got.reshape(2, 4, 48, D)
        return carry

    lax.fori_loop(0, 2, outer, 0)

    def gp_y(d, sends):
        k = rem(y + d, 4)
        copy = pltpu.make_async_remote_copy(
            src_ref=gp0.at[:, k], dst_ref=gp1.at[y] if sends else gp1.at[k],
            send_sem=gpy_s.at[d], recv_sem=gpy_r.at[y if sends else k],
            device_id=device(x, k, z, c), device_id_type=MESH,
        )
        copy.start() if sends else copy.wait()

    def gp_z(d, sends):
        k = rem(zl + d, 4)
        copy = pltpu.make_async_remote_copy(
            src_ref=gp3.at[k], dst_ref=gp4.at[zl] if sends else gp4.at[k],
            send_sem=gpz_s.at[d], recv_sem=gpz_r.at[zl if sends else k],
            device_id=device(x, y, zh * 4 + k, c), device_id_type=MESH,
        )
        copy.start() if sends else copy.wait()

    def gp_l(d, sends):
        k = rem(a + d, 8)
        copy = pltpu.make_async_remote_copy(
            src_ref=gp6.at[k], dst_ref=gp7.at[a] if sends else gp7.at[k],
            send_sem=gpl_s.at[d], recv_sem=gpl_r.at[a if sends else k],
            device_id=(k, b), device_id_type=MESH,
        )
        copy.start() if sends else copy.wait()

    for d in range(1, 4):
        gp_y(d, True)
    for k in range(4):
        gp1[y, k] = gp0[k, y]

    for n in range(3):
        cols = slice(n * 256, (n + 1) * 256)
        grad_att[:, cols] = nt(cot_g[...], wo[cols, :]).astype(BF)

    lax.fori_loop(0, 3, attend_back, 0)
    exchange(peer_a, me_a, m0, m1, 8, False)
    permute(perm_swap, m1, m2)
    exchange(peer_b, me_b, m2, m3, 9, True)
    lax.fori_loop(3, 6, attend_back, 0)

    for half in range(2):
        for n in range(3 * half, 3 * half + 3):
            cols = slice(n * 128, (n + 1) * 128)
            work[:, cols] = nt(gqkv[...], wqkv[cols, :]).astype(BF)
        permute_out(perm_arr, work, g0, half)
        exchange(peer_a, me_a, g0.at[half], g1.at[half], 10 + half, True)

    for d in range(1, 4):
        gp_y(d, False)
    for k in range(4):
        total = gp1[0, k].astype(F32)
        for i in range(1, 4):
            total = total + gp1[i, k].astype(F32)
        gp2[0, k] = total[0:24]
        gp2[1, k] = total[24:48]
    core = pltpu.make_async_remote_copy(
        src_ref=gp2.at[1 - c], dst_ref=gp5, send_sem=gpc_s, recv_sem=gpc_r,
        device_id=device(x, y, z, 1 - c), device_id_type=MESH,
    )
    core.start()

    for half in range(2):
        exchange(peer_a, me_a, g0.at[half], g1.at[half], 10 + half, False)
        permute_mid(g1, g2, half)
        exchange(peer_b, me_b, g2.at[half], g3.at[half], 12 + half, True)

    core.wait()
    for k in range(4):
        gp3[k] = (gp2[c, k] + gp5[k]).astype(BF)
    for d in range(1, 4):
        gp_z(d, True)
    gp4[zl] = gp3[zl]

    exchange(peer_b, me_b, m2, m3, 9, False)
    permute(perm_home, m3, work2)
    for l in range(8):
        block_out[l] = (hid[l].astype(F32) + work2[l * 32 : (l + 1) * 32, :].astype(F32)).astype(BF)

    for half in range(2):
        exchange(peer_b, me_b, g2.at[half], g3.at[half], 12 + half, False)
        permute_in(perm_home, g3, work, half)
    acc[...] = jnp.zeros_like(acc)

    def norm_back(l, carry):
        ng = work[pl.ds(pl.multiple_of(l * 32, 32), 32), :].astype(F32)
        xh = xhat[l]
        prod = ng * xh
        acc[9] += jnp.sum(prod.reshape(4, 8, D), axis=0)
        u = ng * gain_row
        mu = jnp.mean(u, axis=-1, keepdims=True)
        mux = jnp.mean(prod * gain_row, axis=-1, keepdims=True)
        gh = cot[l].astype(F32) + rstd[l] * (u - mu - xh * mux)
        normed_w[l] = gh.astype(BF)
        return carry

    lax.fori_loop(0, 8, norm_back, 0)
    fill_edges(normed_w, edges_g)
    halos = halo_copies(normed_w, edges_g, rows_in_g, cols_in_g, halo_gs, halo_gr)
    for copy in halos:
        copy.start()

    def tap_sums(l, carry):
        gh = normed_w[l].astype(F32)
        for i in range(3):
            for j in range(3):
                acc[3 * i + j] += jnp.sum((shifted[j, l + i] * gh).reshape(4, 8, D), axis=0)
        return carry

    lax.fori_loop(0, 8, tap_sums, 0)
    for k in range(16):
        if k < 10:
            s0[k] = jnp.sum(acc[k], axis=0, keepdims=True)
        else:
            s0[k] = jnp.zeros((1, D), F32)

    def sums(peer, me, src, dst, slot, whole_src, sends):
        def step(d, carry):
            k = rem(me + d, 16)
            copy = pltpu.make_async_remote_copy(
                src_ref=src if whole_src else src.at[k], dst_ref=dst.at[me] if sends else dst.at[k],
                send_sem=sum_s.at[slot, d], recv_sem=sum_r.at[slot, me if sends else k],
                device_id=peer(k), device_id_type=MESH,
            )
            if sends:
                copy.start()
            else:
                copy.wait()
            return carry

        lax.fori_loop(1, 16, step, 0)
        if sends:
            dst[me] = src[...] if whole_src else src[me]

    sums(peer_a, me_a, s0, s1, 0, False, True)

    for d in range(1, 4):
        gp_z(d, False)
    total = gp4[0].astype(F32)
    for i in range(1, 4):
        total = total + gp4[i].astype(F32)
    for i in range(8):
        gp6[i, :, 0:96] = total[:, i * 96 : (i + 1) * 96]
        gp6[i, :, 96:128] = jnp.zeros((24, 32), F32)
    for d in range(1, 8):
        gp_l(d, True)
    gp7[a] = gp6[a]

    for copy in halos:
        copy.wait()
    fill_shifted(normed_w, rows_in_g, cols_in_g)

    def grad_row(l, carry):
        grad_fields[l] = conv_row(l, True).astype(BF)
        return carry

    sums(peer_a, me_a, s0, s1, 0, False, False)
    s2[...] = jnp.sum(s1[...], axis=0)
    sums(peer_b, me_b, s2, s3, 1, True, True)
    lax.fori_loop(0, 6, grad_row, 0)
    sums(peer_b, me_b, s2, s3, 1, True, False)
    s4[...] = jnp.sum(s3[...], axis=0) * TOTAL_SCALE
    sums(peer_a, me_a, s4, s5, 2, True, True)
    lax.fori_loop(6, 8, grad_row, 0)

    for d in range(1, 8):
        gp_l(d, False)
    gp_out[...] = (jnp.sum(gp7[...], axis=0) * TOTAL_SCALE)[:, 0:96]
    sums(peer_a, me_a, s4, s5, 2, True, False)
    for k in range(9):
        taps_out[k // 3, k % 3 : k % 3 + 1, :] = s5[k]
    gain_out[...] = s5[9].reshape(D)


def hand_over(*refs):
    for k in range(5):
        refs[5 + k][...] = refs[k][...]


def body(
    fields, conv_kernel, layer_norm_gain, qkv_weight, out_weight, score_bias, pattern, cotangent
):
    vm = pl.BlockSpec(memory_space=pltpu.VMEM)
    hbm = pl.BlockSpec(memory_space=pl.ANY)
    dma = pltpu.SemaphoreType.DMA

    def vmem(shape, dtype):
        return pltpu.VMEM(shape, dtype)

    scratch = (
        [vmem((D, 3 * D), BF), vmem((D, D), BF), vmem((24, 64, 64), F32), vmem((6, 64, 256), F32), dma((3,))]
        + [vmem((2, 8, D), BF), vmem((2, 8, D), BF)]
        + [vmem((2, 32, D), BF), vmem((6, 8, D), BF)] * 2
        + [dma((8,))] * 4
        + [vmem((3, 10, 32, D), F32), vmem((8, 32, D), BF), vmem((8, 32, D), F32), vmem((8, 32, 1), F32)]
        + [vmem((256, D), BF)] * 2
        + [vmem((8, 32, D), BF)]
        + [vmem((256, 256), BF)] * 5
        + [vmem((2, 16, 16, D // 2), BF)] * 12
        + [vmem((16, 16, D), BF)] * 4
        + [dma((14, 16)), dma((14, 16))]
        + [vmem((6, 4, 64, 256), F32)]
        + [vmem((256, D), BF), vmem((256, D), BF), vmem((256, 3 * D), BF), vmem((256, D), BF), vmem((256, D), BF), vmem((256, 3 * D), BF)]
        + [vmem((4, 4, 48, D), BF), vmem((4, 4, 48, D), BF), vmem((2, 4, 24, D), F32)]
        + [vmem((4, 24, D), BF), vmem((4, 24, D), BF), vmem((4, 24, D), F32)]
        + [vmem((8, 24, 128), F32), vmem((8, 24, 128), F32)]
        + [dma((4,)), dma((4,)), dma((4,)), dma((4,)), dma(()), dma(()), dma((8,)), dma((8,))]
        + [vmem((10, 8, D), F32), vmem((16, 1, D), F32), vmem((16, 1, D), F32), vmem((1, D), F32), vmem((16, 1, D), F32), vmem((1, D), F32), vmem((16, 1, D), F32)]
        + [dma((3, 16)), dma((3, 16))]
    )
    results = (
        jax.ShapeDtypeStruct((8, 32, D), BF),
        jax.ShapeDtypeStruct((8, 32, D), BF),
        jax.ShapeDtypeStruct((24, 96), F32),
        jax.ShapeDtypeStruct((3, 3, D), F32),
        jax.ShapeDtypeStruct((D,), F32),
    )
    out = pl.pallas_call(
        kernel,
        out_shape=results,
        in_specs=[vm] * 5 + [hbm] * 3,
        out_specs=(vm,) * 5,
        scratch_shapes=scratch,
        name="section",
        compiler_params=pltpu.CompilerParams(
            collective_id=0, has_side_effects=True, vmem_limit_bytes=60 << 20
        ),
    )(
        fields, cotangent, conv_kernel, layer_norm_gain,
        pattern.reshape(1, 256), qkv_weight, out_weight, score_bias,
    )
    block_out, grad_fields, gp, taps, gain = pl.pallas_call(
        hand_over, out_shape=results, in_specs=[vm] * 5, out_specs=(vm,) * 5, name="results"
    )(*out)
    return (block_out, grad_fields, jnp.transpose(gp), taps, gain)


def solution(mesh):
    split = P("lat", "lon", None)
    return jax.shard_map(
        body,
        mesh=mesh,
        in_specs=(split, P(), P(), P(), P(), P(), split, split),
        out_specs=(split, split, P("lat", "lon"), P(), P()),
        check_vma=False,
    )
```

```python
import math

import jax
import jax.numpy as jnp
from jax import lax
from jax.experimental import pallas as pl
from jax.experimental.pallas import tpu as pltpu
from jax.sharding import PartitionSpec as P

MESH = pl.DeviceIdType.MESH
BF = jnp.bfloat16
F32 = jnp.float32
D = 768
EPS = 1e-05
HEAD_SCALE = 32 ** (-0.5)
TOTAL_SCALE = 1.0 / math.sqrt(65536)


def nn(a, b):
    return lax.dot_general(a, b, (((1,), (0,)), ((), ())), preferred_element_type=F32)


def nt(a, b):
    return lax.dot_general(a, b, (((1,), (1,)), ((), ())), preferred_element_type=F32)


def tn(a, b):
    return lax.dot_general(a, b, (((0,), (0,)), ((), ())), preferred_element_type=F32)


def div(a, n):
    return lax.div(a, jnp.int32(n))


def rem(a, n):
    return lax.rem(a, jnp.int32(n))


def device(x, y, z, c):
    return (x * 2 + div(z, 4), rem(z, 4) * 8 + y * 2 + c)


def one_hot(cond):
    return jnp.where(cond, 1.0, 0.0).astype(BF)


def iota2(axis):
    return lax.broadcasted_iota(jnp.int32, (256, 256), axis)


def slot_order(s):
    x, zh, zl, y, c = s >> 6, (s >> 5) & 1, (s >> 3) & 3, (s >> 1) & 3, s & 1
    return x * 64 + y * 16 + zh * 8 + zl * 2 + c


def arrival_order(p):
    x, zh, zl, y, c = p >> 6, (p >> 5) & 1, (p >> 3) & 3, (p >> 1) & 3, p & 1
    return zh * 128 + zl * 32 + c * 16 + x * 4 + y


def kernel(
    fields_hbm, cot_hbm, taps_hbm, gain_hbm, pat_hbm, wqkv_hbm, wo_hbm, bias_hbm,
    block_out, grad_fields, gp_out, taps_out, gain_out,
    fields, cot, taps, gain, pat, wqkv, wo, bias, bias_t, w_sem,
    corners, corners_g, corner_in, corner_in_g, edges, edges_g, rows_in, cols_in, rows_in_g, cols_in_g, halo_s, halo_r, halo_gs, halo_gr,
    shifted, hid, xhat, rstd, work, work2, normed_w,
    perm_out, perm_home, perm_swap, perm_pos, perm_arr,
    c0, c1, c2, c3, n0, n1, n2, n3, g0, g1, g2, g3, m0, m1, m2, m3, a2a_s, a2a_r,
    probs, cot_g, nrm_g, qkv, grad_att, att, gqkv,
    gp0, gp1, gp2, gp3, gp4, gp5, gp6, gp7, gpy_s, gpy_r, gpz_s, gpz_r, gpc_s, gpc_r, gpl_s, gpl_r,
    acc, s0, s1, s2, s3, s4, s5, sum_s, sum_r,
):
    a = lax.axis_index("lat")
    b = lax.axis_index("lon")
    x, zh = div(a, 2), rem(a, 2)
    zl, y, c = div(b, 8), rem(div(b, 2), 4), rem(b, 2)
    z = zh * 4 + zl
    me_b = x * 4 + y
    me_a = z * 2 + c

    def peer_b(k):
        return device(div(k, 4), rem(k, 4), z, c)

    def peer_a(k):
        return device(x, y, div(k, 2), rem(k, 2))

    def neighbour(da, db):
        return (rem(a + da + 8, 8), rem(b + db + 32, 32))

    loads = {}
    for i, (name, src, dst) in enumerate(
        (
            ("fields", fields_hbm, fields), ("pat", pat_hbm, pat), ("cot", cot_hbm, cot),
            ("bias", bias_hbm, bias), ("taps", taps_hbm, taps), ("gain", gain_hbm, gain),
            ("wqkv", wqkv_hbm, wqkv), ("wo", wo_hbm, wo),
        )
    ):
        loads[name] = pltpu.make_async_copy(src, dst, w_sem.at[i])
        loads[name].start()

    bar = pltpu.get_barrier_semaphore()

    def greet(d, carry):
        pl.semaphore_signal(bar, inc=1, device_id=peer_b(rem(me_b + d, 16)), device_id_type=MESH)
        pl.semaphore_signal(bar, inc=1, device_id=peer_a(rem(me_a + d, 16)), device_id_type=MESH)
        return carry

    offsets = [(-1, 0), (1, 0), (0, -1), (0, 1), (-1, -1), (-1, 1), (1, -1), (1, 1)]
    for da, db in offsets:
        pl.semaphore_signal(bar, inc=1, device_id=neighbour(da, db), device_id_type=MESH)
    for d in range(1, 4):
        pl.semaphore_signal(
            bar, inc=1, device_id=device(rem(x + d, 4), y, rem(z + 4, 8), c), device_id_type=MESH
        )
    lax.fori_loop(1, 16, greet, 0)

    row8 = lax.broadcasted_iota(jnp.int32, (8, D), 0)
    row32 = lax.broadcasted_iota(jnp.int32, (32, D), 0)

    def fill_edges(source, dest, corner):
        left = jnp.zeros((8, D), F32)
        right = jnp.zeros((8, D), F32)
        for l in range(8):
            row = source[l].astype(F32)
            left = jnp.where(row8 == l, row[0:1, :], left)
            right = jnp.where(row8 == l, row[31:32, :], right)
        dest[0] = left.astype(BF)
        dest[1] = right.astype(BF)
        corner[0] = left[0:1].astype(BF)
        corner[1] = right[0:1].astype(BF)
        corner[2] = left[7:8].astype(BF)
        corner[3] = right[7:8].astype(BF)

    def halo_copies(source, edge, corner, rows, cols, corner_to, ss, rs):
        out = []
        routes = [
            (source.at[0], rows.at[1]), (source.at[7], rows.at[0]),
            (edge.at[0], cols.at[1]), (edge.at[1], cols.at[0]),
            (corner.at[0], corner_to.at[3]), (corner.at[1], corner_to.at[2]),
            (corner.at[2], corner_to.at[1]), (corner.at[3], corner_to.at[0]),
        ]
        for m, (src, dst) in enumerate(routes):
            out.append(
                pltpu.make_async_remote_copy(
                    src_ref=src, dst_ref=dst, send_sem=ss.at[m], recv_sem=rs.at[m],
                    device_id=neighbour(*offsets[m]), device_id_type=MESH,
                )
            )
        return out

    top_mask = (a > 0).astype(F32)
    bottom_mask = (a < 7).astype(F32)

    def fill_shifted(source, rows, cols, corner):
        for r in range(10):
            if r == 0:
                f = rows[0].astype(F32) * top_mask
                le = corner[0].astype(F32) * top_mask
                ri = corner[1].astype(F32) * top_mask
            elif r == 9:
                f = rows[1].astype(F32) * bottom_mask
                le = corner[2].astype(F32) * bottom_mask
                ri = corner[3].astype(F32) * bottom_mask
            else:
                f = source[r - 1].astype(F32)
                le = cols[0].astype(F32)[r - 1 : r, :]
                ri = cols[1].astype(F32)[r - 1 : r, :]
            shifted[0, r] = jnp.where(row32 == 0, le, pltpu.roll(f, 1, 0))
            shifted[1, r] = f
            shifted[2, r] = jnp.where(row32 == 31, ri, pltpu.roll(f, 31, 0))

    def exchange(peer, me, src, dst, slot, sends):
        def step(d, carry):
            k = rem(me + d, 16)
            copy = pltpu.make_async_remote_copy(
                src_ref=src.at[k], dst_ref=dst.at[me] if sends else dst.at[k],
                send_sem=a2a_s.at[slot, d], recv_sem=a2a_r.at[slot, me if sends else k],
                device_id=peer(k), device_id_type=MESH,
            )
            if sends:
                copy.start()
            else:
                copy.wait()
            return carry

        lax.fori_loop(1, 16, step, 0)
        if sends:
            dst[me] = src[me]

    def permute(perm, src, dst):
        for n in range(3):
            cols = slice(n * 256, (n + 1) * 256)
            rows = src[..., cols].reshape(256, 256)
            got = nn(perm[...], rows).astype(BF)
            dst[..., cols] = got.reshape(dst.shape[:-1] + (256,))

    def permute_out(perm, src, dst, half):
        rows = src[..., half * 384 : (half + 1) * 384].reshape(256, 384)
        dst[half] = nn(perm[half], rows).astype(BF).reshape(16, 16, 384)

    def permute_mid(src, dst, half):
        dst[half] = nn(perm_swap[...], src[half].reshape(256, 384)).astype(BF).reshape(16, 16, 384)

    def permute_in(perm, src, dst, half):
        got = nn(perm[half], src[half].reshape(256, 384)).astype(BF)
        dst[:, half * 384 : (half + 1) * 384] = got

    loads["fields"].wait()
    fill_edges(fields, edges, corners)
    pl.semaphore_wait(bar, 41)
    halos = halo_copies(fields, edges, corners, rows_in, cols_in, corner_in, halo_s, halo_r)
    for copy in halos:
        copy.start()

    loads["pat"].wait()
    pat_hot = one_hot(iota2(0) == pat[...])
    for half, first, second in ((0, slot_order, arrival_order), (1, arrival_order, slot_order)):
        order_hot = one_hot(iota2(0) == first(iota2(1)))
        perm_out[half] = nt(order_hot, pat_hot).astype(BF)
        perm_home[half] = nt(pat_hot, order_hot).astype(BF)
        perm_pos[half] = one_hot(iota2(1) == second(iota2(0)))
        perm_arr[half] = one_hot(iota2(0) == second(iota2(1)))
    perm_swap[...] = one_hot(iota2(1) == (iota2(0) & 15) * 16 + (iota2(0) >> 4))
    first_peer = ((peer_b, me_b), (peer_a, me_a))
    second_peer = ((peer_a, me_a), (peer_b, me_b))

    loads["cot"].wait()
    permute_out(perm_out, cot, c0, 0)
    exchange(*first_peer[0], c0.at[0], c1.at[0], 4, True)
    permute_out(perm_out, cot, c0, 1)

    loads["bias"].wait()
    for q in range(6):
        bias_t[q] = jnp.transpose(bias[4 * q : 4 * q + 4].reshape(256, 64))

    for copy in halos:
        copy.wait()
    exchange(*first_peer[1], c0.at[1], c1.at[1], 5, True)
    fill_shifted(fields, rows_in, cols_in, corner_in)
    loads["taps"].wait()
    loads["gain"].wait()
    gain_row = gain[...].reshape(1, D)

    def conv_row(l, flip):
        out = shifted[1, l + 1]
        for i in range(3):
            for j in range(3):
                ti, tj = (2 - i, 2 - j) if flip else (i, j)
                out = out + taps[ti, tj : tj + 1, :] * shifted[j, l + i]
        return out

    def norm_row(l, carry):
        h = conv_row(l, False).astype(BF)
        hid[l] = h
        hf = h.astype(F32)
        mean = jnp.mean(hf, axis=-1, keepdims=True)
        rem = hf - mean
        var = jnp.mean(rem * rem, axis=-1, keepdims=True)
        inv = lax.rsqrt(var + EPS)
        xh = rem * inv
        xhat[l] = xh
        rstd[l] = inv
        normed_w[l] = (xh * gain_row).astype(BF)
        return carry

    lax.fori_loop(0, 8, norm_row, 0)
    for h in range(2):
        permute_out(perm_out, normed_w, n0, h)
        exchange(*first_peer[h], n0.at[h], n1.at[h], h, True)
    for h in range(2):
        exchange(*first_peer[h], c0.at[h], c1.at[h], 4 + h, False)
        permute_mid(c1, c2, h)
    for h in range(2):
        exchange(*first_peer[h], n0.at[h], n1.at[h], h, False)
        permute_mid(n1, n2, h)
        exchange(*second_peer[h], n2.at[h], n3.at[h], 2 + h, True)
    for h in range(2):
        exchange(*second_peer[h], c2.at[h], c3.at[h], 6 + h, True)

    for h in (1, 0):
        exchange(*second_peer[h], n2.at[h], n3.at[h], 2 + h, False)
        permute_in(perm_pos, n3, nrm_g, h)
    loads["wqkv"].wait()

    def project(n, carry):
        cols = pl.ds(pl.multiple_of(n * 256, 256), 256)
        qkv[:, cols] = nn(nrm_g[...], wqkv[:, cols]).astype(BF)
        return carry

    lax.fori_loop(0, 9, project, 0)

    lane_head = lax.broadcasted_iota(jnp.int32, (64, 128), 1) >> 5

    def spread(v):
        vf = v.astype(F32)
        return jnp.concatenate(
            [jnp.where(lane_head == e, vf, 0.0).astype(BF) for e in range(4)], axis=0
        )

    def gather(v):
        out = jnp.zeros((64, 128), F32)
        for e in range(4):
            out = jnp.where(lane_head == e, v[e * 64 : (e + 1) * 64, :], out)
        return out

    def columns(q, part):
        return pl.ds(pl.multiple_of(q * 128 + part * D, 128), 128)

    def attend(q, carry):
        for g in range(4):
            rows = slice(g * 64, (g + 1) * 64)
            q_bd = spread(qkv[rows, columns(q, 0)])
            st = nt(qkv[rows, columns(q, 1)], q_bd) * HEAD_SCALE + bias_t[q]
            e = jnp.exp(st - jnp.max(st, axis=0, keepdims=True))
            p = e * (1.0 / jnp.sum(e, axis=0, keepdims=True))
            probs[q, g] = p
            att[rows, columns(q, 0)] = gather(tn(p.astype(BF), qkv[rows, columns(q, 2)])).astype(BF)
        return carry

    def attend_back(q, carry):
        for g in range(4):
            rows = slice(g * 64, (g + 1) * 64)
            q_bd = spread(qkv[rows, columns(q, 0)])
            g_bd = spread(grad_att[rows, columns(q, 0)])
            p = probs[q, g]
            dp = nt(qkv[rows, columns(q, 2)], g_bd)
            ds = (p * (dp - jnp.sum(p * dp, axis=0, keepdims=True))).astype(BF)
            dq = gather(tn(ds, qkv[rows, columns(q, 1)])) * HEAD_SCALE
            gqkv[rows, columns(q, 0)] = dq.astype(BF)
            gqkv[rows, columns(q, 1)] = (nn(ds, q_bd) * HEAD_SCALE).astype(BF)
            gqkv[rows, columns(q, 2)] = nn(p.astype(BF), g_bd).astype(BF)
        return carry

    lax.fori_loop(0, 6, attend, 0)

    loads["wo"].wait()
    for n in range(3):
        cols = slice(n * 256, (n + 1) * 256)
        work2[:, cols] = nn(att[...], wo[:, cols]).astype(BF)
    permute(perm_arr.at[0], work2, m0)
    exchange(peer_a, me_a, m0, m1, 8, True)

    for h in range(2):
        exchange(*second_peer[h], c2.at[h], c3.at[h], 6 + h, False)
        permute_in(perm_pos, c3, cot_g, h)

    def outer(n, carry):
        cols = pl.ds(pl.multiple_of(n * 384, 128), 384)
        got = tn(cot_g[:, cols], att[...]).astype(BF)
        gp0[pl.ds(2 * n, 2)] = got.reshape(2, 4, 48, D)
        return carry

    lax.fori_loop(0, 2, outer, 0)

    def gp_y(d, sends):
        k = rem(y + d, 4)
        copy = pltpu.make_async_remote_copy(
            src_ref=gp0.at[:, k], dst_ref=gp1.at[y] if sends else gp1.at[k],
            send_sem=gpy_s.at[d], recv_sem=gpy_r.at[y if sends else k],
            device_id=device(x, k, z, c), device_id_type=MESH,
        )
        copy.start() if sends else copy.wait()

    def gp_z(d, sends):
        k = rem(zl + d, 4)
        copy = pltpu.make_async_remote_copy(
            src_ref=gp3.at[k], dst_ref=gp4.at[zl] if sends else gp4.at[k],
            send_sem=gpz_s.at[d], recv_sem=gpz_r.at[zl if sends else k],
            device_id=device(x, y, zh * 4 + k, c), device_id_type=MESH,
        )
        copy.start() if sends else copy.wait()

    def gp_l(d, sends):
        k = rem(a + d, 8)
        copy = pltpu.make_async_remote_copy(
            src_ref=gp6.at[k], dst_ref=gp7.at[a] if sends else gp7.at[k],
            send_sem=gpl_s.at[d], recv_sem=gpl_r.at[a if sends else k],
            device_id=(k, b), device_id_type=MESH,
        )
        copy.start() if sends else copy.wait()

    for d in range(1, 4):
        gp_y(d, True)
    for k in range(4):
        gp1[y, k] = gp0[k, y]

    for n in range(3):
        cols = slice(n * 256, (n + 1) * 256)
        grad_att[:, cols] = nt(cot_g[...], wo[cols, :]).astype(BF)

    lax.fori_loop(0, 6, attend_back, 0)

    for half in range(2):
        for n in range(3 * half, 3 * half + 3):
            cols = slice(n * 128, (n + 1) * 128)
            work[:, cols] = nt(gqkv[...], wqkv[cols, :]).astype(BF)
        permute_out(perm_arr, work, g0, half)
        exchange(*second_peer[half], g0.at[half], g1.at[half], 10 + half, True)

    exchange(peer_a, me_a, m0, m1, 8, False)
    permute(perm_swap, m1, m2)
    exchange(peer_b, me_b, m2, m3, 9, True)

    for d in range(1, 4):
        gp_y(d, False)
    for k in range(4):
        total = gp1[0, k].astype(F32)
        for i in range(1, 4):
            total = total + gp1[i, k].astype(F32)
        gp2[0, k] = total[0:24]
        gp2[1, k] = total[24:48]
    core = pltpu.make_async_remote_copy(
        src_ref=gp2.at[1 - c], dst_ref=gp5, send_sem=gpc_s, recv_sem=gpc_r,
        device_id=device(x, y, z, 1 - c), device_id_type=MESH,
    )
    core.start()

    for half in range(2):
        exchange(*second_peer[half], g0.at[half], g1.at[half], 10 + half, False)
        permute_mid(g1, g2, half)
        exchange(*first_peer[half], g2.at[half], g3.at[half], 12 + half, True)

    core.wait()
    for k in range(4):
        gp3[k] = (gp2[c, k] + gp5[k]).astype(BF)
    for d in range(1, 4):
        gp_z(d, True)
    gp4[zl] = gp3[zl]

    exchange(peer_b, me_b, m2, m3, 9, False)
    permute(perm_home.at[0], m3, work2)
    for l in range(8):
        block_out[l] = (hid[l].astype(F32) + work2[l * 32 : (l + 1) * 32, :].astype(F32)).astype(BF)

    for half in range(2):
        exchange(*first_peer[half], g2.at[half], g3.at[half], 12 + half, False)
        permute_in(perm_home, g3, work, half)
    acc[...] = jnp.zeros_like(acc)

    def norm_back(l, carry):
        ng = work[pl.ds(pl.multiple_of(l * 32, 32), 32), :].astype(F32)
        xh = xhat[l]
        prod = ng * xh
        acc[9] += jnp.sum(prod.reshape(4, 8, D), axis=0)
        u = ng * gain_row
        mu = jnp.mean(u, axis=-1, keepdims=True)
        mux = jnp.mean(prod * gain_row, axis=-1, keepdims=True)
        gh = cot[l].astype(F32) + rstd[l] * (u - mu - xh * mux)
        normed_w[l] = gh.astype(BF)
        return carry

    lax.fori_loop(0, 8, norm_back, 0)
    fill_edges(normed_w, edges_g, corners_g)
    halos = halo_copies(
        normed_w, edges_g, corners_g, rows_in_g, cols_in_g, corner_in_g, halo_gs, halo_gr
    )
    for copy in halos:
        copy.start()

    def tap_sums(l, carry):
        gh = normed_w[l].astype(F32)
        for i in range(3):
            for j in range(3):
                acc[3 * i + j] += jnp.sum((shifted[j, l + i] * gh).reshape(4, 8, D), axis=0)
        return carry

    lax.fori_loop(0, 8, tap_sums, 0)
    for k in range(16):
        if k < 10:
            s0[k] = jnp.sum(acc[k], axis=0, keepdims=True)
        else:
            s0[k] = jnp.zeros((1, D), F32)

    def sums(peer, me, src, dst, slot, whole_src, sends):
        def step(d, carry):
            k = rem(me + d, 16)
            copy = pltpu.make_async_remote_copy(
                src_ref=src if whole_src else src.at[k], dst_ref=dst.at[me] if sends else dst.at[k],
                send_sem=sum_s.at[slot, d], recv_sem=sum_r.at[slot, me if sends else k],
                device_id=peer(k), device_id_type=MESH,
            )
            if sends:
                copy.start()
            else:
                copy.wait()
            return carry

        lax.fori_loop(1, 16, step, 0)
        if sends:
            dst[me] = src[...] if whole_src else src[me]

    sums(peer_a, me_a, s0, s1, 0, False, True)

    sums(peer_a, me_a, s0, s1, 0, False, False)
    s2[...] = jnp.sum(s1[...], axis=0)
    sums(peer_b, me_b, s2, s3, 1, True, True)

    for d in range(1, 4):
        gp_z(d, False)
    total = gp4[0].astype(F32)
    for i in range(1, 4):
        total = total + gp4[i].astype(F32)
    for i in range(8):
        gp6[i, :, 0:96] = total[:, i * 96 : (i + 1) * 96]
        gp6[i, :, 96:128] = jnp.zeros((24, 32), F32)
    for d in range(1, 8):
        gp_l(d, True)
    gp7[a] = gp6[a]

    sums(peer_b, me_b, s2, s3, 1, True, False)
    s4[...] = jnp.sum(s3[...], axis=0) * TOTAL_SCALE
    sums(peer_a, me_a, s4, s5, 2, True, True)

    for copy in halos:
        copy.wait()
    fill_shifted(normed_w, rows_in_g, cols_in_g, corner_in_g)

    def grad_row(l, carry):
        grad_fields[l] = conv_row(l, True).astype(BF)
        return carry

    lax.fori_loop(0, 8, grad_row, 0)

    for d in range(1, 8):
        gp_l(d, False)
    gp_out[...] = (jnp.sum(gp7[...], axis=0) * TOTAL_SCALE)[:, 0:96]
    sums(peer_a, me_a, s4, s5, 2, True, False)
    for k in range(9):
        taps_out[k // 3, k % 3 : k % 3 + 1, :] = s5[k]
    gain_out[...] = s5[9].reshape(D)


def hand_over(*refs):
    for k in range(5):
        refs[5 + k][...] = refs[k][...]


def body(
    fields, conv_kernel, layer_norm_gain, qkv_weight, out_weight, score_bias, pattern, cotangent
):
    vm = pl.BlockSpec(memory_space=pltpu.VMEM)
    hbm = pl.BlockSpec(memory_space=pl.ANY)
    dma = pltpu.SemaphoreType.DMA

    def vmem(shape, dtype):
        return pltpu.VMEM(shape, dtype)

    scratch = (
        [vmem((8, 32, D), BF), vmem((8, 32, D), BF), vmem((3, 3, D), F32), vmem((D,), F32), vmem((1, 256), jnp.int32)]
        + [vmem((D, 3 * D), BF), vmem((D, D), BF), vmem((24, 64, 64), F32), vmem((6, 64, 256), F32), dma((8,))]
        + [vmem((4, 1, D), BF)] * 4
        + [vmem((2, 8, D), BF), vmem((2, 8, D), BF)]
        + [vmem((2, 32, D), BF), vmem((2, 8, D), BF)] * 2
        + [dma((8,))] * 4
        + [vmem((3, 10, 32, D), F32), vmem((8, 32, D), BF), vmem((8, 32, D), F32), vmem((8, 32, 1), F32)]
        + [vmem((256, D), BF)] * 2
        + [vmem((8, 32, D), BF)]
        + [vmem((2, 256, 256), BF)] * 2
        + [vmem((256, 256), BF)]
        + [vmem((2, 256, 256), BF)] * 2
        + [vmem((2, 16, 16, D // 2), BF)] * 12
        + [vmem((16, 16, D), BF)] * 4
        + [dma((14, 16)), dma((14, 16))]
        + [vmem((6, 4, 64, 256), F32)]
        + [vmem((256, D), BF), vmem((256, D), BF), vmem((256, 3 * D), BF), vmem((256, D), BF), vmem((256, D), BF), vmem((256, 3 * D), BF)]
        + [vmem((4, 4, 48, D), BF), vmem((4, 4, 48, D), BF), vmem((2, 4, 24, D), F32)]
        + [vmem((4, 24, D), BF), vmem((4, 24, D), BF), vmem((4, 24, D), F32)]
        + [vmem((8, 24, 128), F32), vmem((8, 24, 128), F32)]
        + [dma((4,)), dma((4,)), dma((4,)), dma((4,)), dma(()), dma(()), dma((8,)), dma((8,))]
        + [vmem((10, 8, D), F32), vmem((16, 1, D), F32), vmem((16, 1, D), F32), vmem((1, D), F32), vmem((16, 1, D), F32), vmem((1, D), F32), vmem((16, 1, D), F32)]
        + [dma((3, 16)), dma((3, 16))]
    )
    results = (
        jax.ShapeDtypeStruct((8, 32, D), BF),
        jax.ShapeDtypeStruct((8, 32, D), BF),
        jax.ShapeDtypeStruct((24, 96), F32),
        jax.ShapeDtypeStruct((3, 3, D), F32),
        jax.ShapeDtypeStruct((D,), F32),
    )
    out = pl.pallas_call(
        kernel,
        out_shape=results,
        in_specs=[hbm] * 8,
        out_specs=(vm,) * 5,
        scratch_shapes=scratch,
        name="section",
        compiler_params=pltpu.CompilerParams(
            collective_id=0, has_side_effects=True, vmem_limit_bytes=60 << 20
        ),
    )(
        fields, cotangent, conv_kernel, layer_norm_gain,
        pattern.reshape(1, 256), qkv_weight, out_weight, score_bias,
    )
    block_out, grad_fields, gp, taps, gain = pl.pallas_call(
        hand_over, out_shape=results, in_specs=[vm] * 5, out_specs=(vm,) * 5, name="results"
    )(*out)
    return (block_out, grad_fields, jnp.transpose(gp), taps, gain)


def solution(mesh):
    split = P("lat", "lon", None)
    return jax.shard_map(
        body,
        mesh=mesh,
        in_specs=(split, P(), P(), P(), P(), P(), split, split),
        out_specs=(split, split, P("lat", "lon"), P(), P()),
        check_vma=False,
    )
```

```python
import math

import jax
import jax.numpy as jnp
from jax import lax
from jax.experimental import pallas as pl
from jax.experimental.pallas import tpu as pltpu
from jax.sharding import PartitionSpec as P

MESH = pl.DeviceIdType.MESH
BF = jnp.bfloat16
F32 = jnp.float32
D = 768
EPS = 1e-05
HEAD_SCALE = 32 ** (-0.5)
TOTAL_SCALE = 1.0 / math.sqrt(65536)


def nn(a, b):
    return lax.dot_general(a, b, (((1,), (0,)), ((), ())), preferred_element_type=F32)


def nt(a, b):
    return lax.dot_general(a, b, (((1,), (1,)), ((), ())), preferred_element_type=F32)


def tn(a, b):
    return lax.dot_general(a, b, (((0,), (0,)), ((), ())), preferred_element_type=F32)


def div(a, n):
    return lax.div(a, jnp.int32(n))


def rem(a, n):
    return lax.rem(a, jnp.int32(n))


def device(x, y, z, c):
    return (x * 2 + div(z, 4), rem(z, 4) * 8 + y * 2 + c)


def one_hot(cond):
    return jnp.where(cond, 1.0, 0.0).astype(BF)


def iota2(axis):
    return lax.broadcasted_iota(jnp.int32, (256, 256), axis)


def slot_order(s):
    x, zh, zl, y, c = s >> 6, (s >> 5) & 1, (s >> 3) & 3, (s >> 1) & 3, s & 1
    return x * 64 + y * 16 + zh * 8 + zl * 2 + c


def arrival_order(p):
    x, zh, zl, y, c = p >> 6, (p >> 5) & 1, (p >> 3) & 3, (p >> 1) & 3, p & 1
    return zh * 128 + zl * 32 + c * 16 + x * 4 + y


def kernel(
    fields_hbm, cot_hbm, taps_hbm, gain_hbm, pat_hbm, wqkv_hbm, wo_hbm, bias_hbm,
    block_out, grad_fields, gp_out, taps_out, gain_out,
    fields, cot, taps, gain, pat, wqkv, wo, bias, bias_t, w_sem,
    corners, corners_g, corner_in, corner_in_g, edges, edges_g, rows_in, cols_in, rows_in_g, cols_in_g, halo_s, halo_r, halo_gs, halo_gr,
    shifted, hid, xhat, rstd, work, work2, normed_w,
    perm_out, perm_home, perm_swap, perm_pos, perm_arr,
    c0, c1, c2, c3, n0, n1, n2, n3, g0, g1, g2, g3, m0, m1, m2, m3, a2a_s, a2a_r,
    probs, cot_g, nrm_g, qkv, grad_att, att, gqkv,
    gp0, gp1, gp2, gp3, gp4, gp5, gp6, gp7, gp_s, gp_r,
    acc, s0, s1, s2, s3, s4, s5, sum_s, sum_r,
):
    a = lax.axis_index("lat")
    b = lax.axis_index("lon")
    x, zh = div(a, 2), rem(a, 2)
    zl, y, c = div(b, 8), rem(div(b, 2), 4), rem(b, 2)
    z = zh * 4 + zl
    me_b = x * 4 + y
    me_a = z * 2 + c

    def peer_b(k):
        return device(div(k, 4), rem(k, 4), z, c)

    def peer_a(k):
        return device(x, y, div(k, 2), rem(k, 2))

    def neighbour(da, db):
        return (rem(a + da + 8, 8), rem(b + db + 32, 32))

    loads = {}
    for i, (name, src, dst) in enumerate(
        (
            ("fields", fields_hbm, fields), ("pat", pat_hbm, pat), ("cot", cot_hbm, cot),
            ("bias", bias_hbm, bias), ("taps", taps_hbm, taps), ("gain", gain_hbm, gain),
            ("wqkv", wqkv_hbm, wqkv), ("wo", wo_hbm, wo),
        )
    ):
        loads[name] = pltpu.make_async_copy(src, dst, w_sem.at[i])
        loads[name].start()

    bar = pltpu.get_barrier_semaphore()

    def greet(d, carry):
        pl.semaphore_signal(bar, inc=1, device_id=peer_b(rem(me_b + d, 16)), device_id_type=MESH)
        pl.semaphore_signal(bar, inc=1, device_id=peer_a(rem(me_a + d, 16)), device_id_type=MESH)
        return carry

    offsets = [(-1, 0), (1, 0), (0, -1), (0, 1), (-1, -1), (-1, 1), (1, -1), (1, 1)]
    for da, db in offsets:
        pl.semaphore_signal(bar, inc=1, device_id=neighbour(da, db), device_id_type=MESH)
    for d in range(1, 4):
        pl.semaphore_signal(
            bar, inc=1, device_id=device(rem(x + d, 4), y, rem(z + 4, 8), c), device_id_type=MESH
        )
    lax.fori_loop(1, 16, greet, 0)

    row8 = lax.broadcasted_iota(jnp.int32, (8, D), 0)
    row32 = lax.broadcasted_iota(jnp.int32, (32, D), 0)

    def fill_edges(source, dest, corner):
        left = jnp.zeros((8, D), F32)
        right = jnp.zeros((8, D), F32)
        for l in range(8):
            row = source[l].astype(F32)
            left = jnp.where(row8 == l, row[0:1, :], left)
            right = jnp.where(row8 == l, row[31:32, :], right)
        dest[0] = left.astype(BF)
        dest[1] = right.astype(BF)
        corner[0] = left[0:1].astype(BF)
        corner[1] = right[0:1].astype(BF)
        corner[2] = left[7:8].astype(BF)
        corner[3] = right[7:8].astype(BF)

    def arrived(ref, sem):
        pltpu.make_async_copy(ref, ref, sem).wait()

    def halo_start(source, edge, corner, rows, cols, corner_to, ss, rs):
        routes = [
            (source.at[0], rows.at[1], 0), (source.at[7], rows.at[0], 0),
            (edge.at[0], cols.at[1], 1), (edge.at[1], cols.at[0], 1),
            (corner.at[0], corner_to.at[3], 2), (corner.at[1], corner_to.at[2], 2),
            (corner.at[2], corner_to.at[1], 2), (corner.at[3], corner_to.at[0], 2),
        ]
        for m, (src, dst, kind) in enumerate(routes):
            pltpu.make_async_remote_copy(
                src_ref=src, dst_ref=dst, send_sem=ss.at[kind], recv_sem=rs.at[kind],
                device_id=neighbour(*offsets[m]), device_id_type=MESH,
            ).start()

    def halo_wait(rows, cols, corner_to, ss, rs):
        for kind, ref in enumerate((rows, cols, corner_to)):
            arrived(ref, ss.at[kind])
            arrived(ref, rs.at[kind])

    top_mask = (a > 0).astype(F32)
    bottom_mask = (a < 7).astype(F32)

    def fill_shifted(source, rows, cols, corner):
        for r in range(10):
            if r == 0:
                f = rows[0].astype(F32) * top_mask
                le = corner[0].astype(F32) * top_mask
                ri = corner[1].astype(F32) * top_mask
            elif r == 9:
                f = rows[1].astype(F32) * bottom_mask
                le = corner[2].astype(F32) * bottom_mask
                ri = corner[3].astype(F32) * bottom_mask
            else:
                f = source[r - 1].astype(F32)
                le = cols[0].astype(F32)[r - 1 : r, :]
                ri = cols[1].astype(F32)[r - 1 : r, :]
            shifted[0, r] = jnp.where(row32 == 0, le, pltpu.roll(f, 1, 0))
            shifted[1, r] = f
            shifted[2, r] = jnp.where(row32 == 31, ri, pltpu.roll(f, 31, 0))

    def exchange(peer, me, src, dst, slot, sends):
        if not sends:
            arrived(src.at[pl.ds(0, 15)], a2a_s.at[slot])
            arrived(dst.at[pl.ds(0, 15)], a2a_r.at[slot])
            return

        def step(d, carry):
            k = rem(me + d, 16)
            pltpu.make_async_remote_copy(
                src_ref=src.at[k], dst_ref=dst.at[me],
                send_sem=a2a_s.at[slot], recv_sem=a2a_r.at[slot],
                device_id=peer(k), device_id_type=MESH,
            ).start()
            return carry

        lax.fori_loop(1, 16, step, 0)
        dst[me] = src[me]

    def permute(perm, src, dst):
        for n in range(3):
            cols = slice(n * 256, (n + 1) * 256)
            rows = src[..., cols].reshape(256, 256)
            got = nn(perm[...], rows).astype(BF)
            dst[..., cols] = got.reshape(dst.shape[:-1] + (256,))

    def permute_out(perm, src, dst, half):
        rows = src[..., half * 384 : (half + 1) * 384].reshape(256, 384)
        dst[half] = nn(perm[half], rows).astype(BF).reshape(16, 16, 384)

    def permute_mid(src, dst, half):
        dst[half] = nn(perm_swap[...], src[half].reshape(256, 384)).astype(BF).reshape(16, 16, 384)

    def permute_in(perm, src, dst, half):
        got = nn(perm[half], src[half].reshape(256, 384)).astype(BF)
        dst[:, half * 384 : (half + 1) * 384] = got

    loads["fields"].wait()
    fill_edges(fields, edges, corners)
    pl.semaphore_wait(bar, 41)
    halo_start(fields, edges, corners, rows_in, cols_in, corner_in, halo_s, halo_r)

    loads["pat"].wait()
    pat_hot = one_hot(iota2(0) == pat[...])
    for half, first, second in ((0, slot_order, arrival_order), (1, arrival_order, slot_order)):
        order_hot = one_hot(iota2(0) == first(iota2(1)))
        perm_out[half] = nt(order_hot, pat_hot).astype(BF)
        perm_home[half] = nt(pat_hot, order_hot).astype(BF)
        perm_pos[half] = one_hot(iota2(1) == second(iota2(0)))
        perm_arr[half] = one_hot(iota2(0) == second(iota2(1)))
    perm_swap[...] = one_hot(iota2(1) == (iota2(0) & 15) * 16 + (iota2(0) >> 4))
    first_peer = ((peer_b, me_b), (peer_a, me_a))
    second_peer = ((peer_a, me_a), (peer_b, me_b))

    loads["cot"].wait()
    permute_out(perm_out, cot, c0, 0)
    exchange(*first_peer[0], c0.at[0], c1.at[0], 4, True)
    permute_out(perm_out, cot, c0, 1)

    loads["bias"].wait()
    for q in range(6):
        bias_t[q] = jnp.transpose(bias[4 * q : 4 * q + 4].reshape(256, 64))

    halo_wait(rows_in, cols_in, corner_in, halo_s, halo_r)
    exchange(*first_peer[1], c0.at[1], c1.at[1], 5, True)
    fill_shifted(fields, rows_in, cols_in, corner_in)
    loads["taps"].wait()
    loads["gain"].wait()
    gain_row = gain[...].reshape(1, D)

    def conv_row(l, flip):
        out = shifted[1, l + 1]
        for i in range(3):
            for j in range(3):
                ti, tj = (2 - i, 2 - j) if flip else (i, j)
                out = out + taps[ti, tj : tj + 1, :] * shifted[j, l + i]
        return out

    def norm_row(l, carry):
        h = conv_row(l, False).astype(BF)
        hid[l] = h
        hf = h.astype(F32)
        mean = jnp.mean(hf, axis=-1, keepdims=True)
        rem = hf - mean
        var = jnp.mean(rem * rem, axis=-1, keepdims=True)
        inv = lax.rsqrt(var + EPS)
        xh = rem * inv
        xhat[l] = xh
        rstd[l] = inv
        normed_w[l] = (xh * gain_row).astype(BF)
        return carry

    lax.fori_loop(0, 8, norm_row, 0)
    for h in range(2):
        permute_out(perm_out, normed_w, n0, h)
        exchange(*first_peer[h], n0.at[h], n1.at[h], h, True)
    for h in range(2):
        exchange(*first_peer[h], c0.at[h], c1.at[h], 4 + h, False)
        permute_mid(c1, c2, h)
    for h in range(2):
        exchange(*first_peer[h], n0.at[h], n1.at[h], h, False)
        permute_mid(n1, n2, h)
        exchange(*second_peer[h], n2.at[h], n3.at[h], 2 + h, True)
    for h in range(2):
        exchange(*second_peer[h], c2.at[h], c3.at[h], 6 + h, True)

    for h in (1, 0):
        exchange(*second_peer[h], n2.at[h], n3.at[h], 2 + h, False)
        permute_in(perm_pos, n3, nrm_g, h)
    loads["wqkv"].wait()

    for n in range(6):
        cols = slice(n * 384, (n + 1) * 384)
        qkv[:, cols] = nn(nrm_g[...], wqkv[:, cols]).astype(BF)

    lane_head = lax.broadcasted_iota(jnp.int32, (64, 128), 1) >> 5

    def spread(v):
        vf = v.astype(F32)
        return jnp.concatenate(
            [jnp.where(lane_head == e, vf, 0.0).astype(BF) for e in range(4)], axis=0
        )

    def gather(v):
        out = jnp.zeros((64, 128), F32)
        for e in range(4):
            out = jnp.where(lane_head == e, v[e * 64 : (e + 1) * 64, :], out)
        return out

    def columns(q, part):
        return pl.ds(pl.multiple_of(q * 128 + part * D, 128), 128)

    def attend(q, carry):
        for g in range(4):
            rows = slice(g * 64, (g + 1) * 64)
            q_bd = spread(qkv[rows, columns(q, 0)])
            st = nt(qkv[rows, columns(q, 1)], q_bd) * HEAD_SCALE + bias_t[q]
            e = jnp.exp(st - jnp.max(st, axis=0, keepdims=True))
            p = e * (1.0 / jnp.sum(e, axis=0, keepdims=True))
            probs[q, g] = p
            att[rows, columns(q, 0)] = gather(tn(p.astype(BF), qkv[rows, columns(q, 2)])).astype(BF)
        return carry

    def attend_back(q, carry):
        for g in range(4):
            rows = slice(g * 64, (g + 1) * 64)
            q_bd = spread(qkv[rows, columns(q, 0)])
            g_bd = spread(grad_att[rows, columns(q, 0)])
            p = probs[q, g]
            dp = nt(qkv[rows, columns(q, 2)], g_bd)
            ds = (p * (dp - jnp.sum(p * dp, axis=0, keepdims=True))).astype(BF)
            dq = gather(tn(ds, qkv[rows, columns(q, 1)])) * HEAD_SCALE
            gqkv[rows, columns(q, 0)] = dq.astype(BF)
            gqkv[rows, columns(q, 1)] = (nn(ds, q_bd) * HEAD_SCALE).astype(BF)
            gqkv[rows, columns(q, 2)] = nn(p.astype(BF), g_bd).astype(BF)
        return carry

    lax.fori_loop(0, 6, attend, 0)

    loads["wo"].wait()
    for n in range(3):
        cols = slice(n * 256, (n + 1) * 256)
        work2[:, cols] = nn(att[...], wo[:, cols]).astype(BF)
    permute(perm_arr.at[0], work2, m0)
    exchange(peer_a, me_a, m0, m1, 8, True)

    for h in range(2):
        exchange(*second_peer[h], c2.at[h], c3.at[h], 6 + h, False)
        permute_in(perm_pos, c3, cot_g, h)

    def outer(n, carry):
        cols = pl.ds(pl.multiple_of(n * 384, 128), 384)
        got = tn(cot_g[:, cols], att[...]).astype(BF)
        gp0[pl.ds(2 * n, 2)] = got.reshape(2, 4, 48, D)
        return carry

    lax.fori_loop(0, 2, outer, 0)

    def gp_y(d):
        k = rem(y + d, 4)
        pltpu.make_async_remote_copy(
            src_ref=gp0.at[:, k], dst_ref=gp1.at[y], send_sem=gp_s.at[0], recv_sem=gp_r.at[0],
            device_id=device(x, k, z, c), device_id_type=MESH,
        ).start()

    def gp_z(d):
        k = rem(zl + d, 4)
        pltpu.make_async_remote_copy(
            src_ref=gp3.at[k], dst_ref=gp4.at[zl], send_sem=gp_s.at[2], recv_sem=gp_r.at[2],
            device_id=device(x, y, zh * 4 + k, c), device_id_type=MESH,
        ).start()

    def gp_l(d):
        k = rem(a + d, 8)
        pltpu.make_async_remote_copy(
            src_ref=gp6.at[k], dst_ref=gp7.at[a], send_sem=gp_s.at[3], recv_sem=gp_r.at[3],
            device_id=(k, b), device_id_type=MESH,
        ).start()

    def gp_arrived(ref, n, stage):
        arrived(ref.at[pl.ds(0, n)], gp_s.at[stage])
        arrived(ref.at[pl.ds(0, n)], gp_r.at[stage])

    for d in range(1, 4):
        gp_y(d)
    for k in range(4):
        gp1[y, k] = gp0[k, y]

    for n in range(3):
        cols = slice(n * 256, (n + 1) * 256)
        grad_att[:, cols] = nt(cot_g[...], wo[cols, :]).astype(BF)

    lax.fori_loop(0, 6, attend_back, 0)

    for half in range(2):
        cols = slice(half * 384, (half + 1) * 384)
        work[:, cols] = nt(gqkv[...], wqkv[cols, :]).astype(BF)
        permute_out(perm_arr, work, g0, half)
        exchange(*second_peer[half], g0.at[half], g1.at[half], 10 + half, True)

    exchange(peer_a, me_a, m0, m1, 8, False)
    permute(perm_swap, m1, m2)
    exchange(peer_b, me_b, m2, m3, 9, True)

    gp_arrived(gp1, 3, 0)
    for k in range(4):
        total = gp1[0, k].astype(F32)
        for i in range(1, 4):
            total = total + gp1[i, k].astype(F32)
        gp2[0, k] = total[0:24]
        gp2[1, k] = total[24:48]
    core = pltpu.make_async_remote_copy(
        src_ref=gp2.at[1 - c], dst_ref=gp5, send_sem=gp_s.at[1], recv_sem=gp_r.at[1],
        device_id=device(x, y, z, 1 - c), device_id_type=MESH,
    )
    core.start()

    for half in range(2):
        exchange(*second_peer[half], g0.at[half], g1.at[half], 10 + half, False)
        permute_mid(g1, g2, half)
        exchange(*first_peer[half], g2.at[half], g3.at[half], 12 + half, True)

    core.wait()
    for k in range(4):
        gp3[k] = (gp2[c, k] + gp5[k]).astype(BF)
    for d in range(1, 4):
        gp_z(d)
    gp4[zl] = gp3[zl]

    exchange(peer_b, me_b, m2, m3, 9, False)
    permute(perm_home.at[0], m3, work2)
    for l in range(8):
        block_out[l] = (hid[l].astype(F32) + work2[l * 32 : (l + 1) * 32, :].astype(F32)).astype(BF)

    for half in range(2):
        exchange(*first_peer[half], g2.at[half], g3.at[half], 12 + half, False)
        permute_in(perm_home, g3, work, half)
    acc[...] = jnp.zeros_like(acc)

    def norm_back(l, carry):
        ng = work[pl.ds(pl.multiple_of(l * 32, 32), 32), :].astype(F32)
        xh = xhat[l]
        prod = ng * xh
        acc[9] += jnp.sum(prod.reshape(4, 8, D), axis=0)
        u = ng * gain_row
        mu = jnp.mean(u, axis=-1, keepdims=True)
        mux = jnp.mean(prod * gain_row, axis=-1, keepdims=True)
        gh = cot[l].astype(F32) + rstd[l] * (u - mu - xh * mux)
        normed_w[l] = gh.astype(BF)
        return carry

    lax.fori_loop(0, 8, norm_back, 0)
    fill_edges(normed_w, edges_g, corners_g)
    halo_start(normed_w, edges_g, corners_g, rows_in_g, cols_in_g, corner_in_g, halo_gs, halo_gr)

    def tap_sums(l, carry):
        gh = normed_w[l].astype(F32)
        for i in range(3):
            for j in range(3):
                acc[3 * i + j] += jnp.sum((shifted[j, l + i] * gh).reshape(4, 8, D), axis=0)
        return carry

    lax.fori_loop(0, 8, tap_sums, 0)
    for k in range(16):
        if k < 10:
            s0[k] = jnp.sum(acc[k], axis=0, keepdims=True)
        else:
            s0[k] = jnp.zeros((1, D), F32)

    def sums(peer, me, src, dst, slot, whole_src, sends):
        if not sends:
            arrived(dst.at[pl.ds(0, 15)], sum_s.at[slot])
            arrived(dst.at[pl.ds(0, 15)], sum_r.at[slot])
            return

        def step(d, carry):
            k = rem(me + d, 16)
            pltpu.make_async_remote_copy(
                src_ref=src if whole_src else src.at[k], dst_ref=dst.at[me],
                send_sem=sum_s.at[slot], recv_sem=sum_r.at[slot],
                device_id=peer(k), device_id_type=MESH,
            ).start()
            return carry

        lax.fori_loop(1, 16, step, 0)
        dst[me] = src[...] if whole_src else src[me]

    sums(peer_a, me_a, s0, s1, 0, False, True)

    sums(peer_a, me_a, s0, s1, 0, False, False)
    s2[...] = jnp.sum(s1[...], axis=0)
    sums(peer_b, me_b, s2, s3, 1, True, True)

    gp_arrived(gp4, 3, 2)
    total = gp4[0].astype(F32)
    for i in range(1, 4):
        total = total + gp4[i].astype(F32)
    for i in range(8):
        gp6[i, :, 0:96] = total[:, i * 96 : (i + 1) * 96]
        gp6[i, :, 96:128] = jnp.zeros((24, 32), F32)
    for d in range(1, 8):
        gp_l(d)
    gp7[a] = gp6[a]

    sums(peer_b, me_b, s2, s3, 1, True, False)
    s4[...] = jnp.sum(s3[...], axis=0) * TOTAL_SCALE
    sums(peer_a, me_a, s4, s5, 2, True, True)

    halo_wait(rows_in_g, cols_in_g, corner_in_g, halo_gs, halo_gr)
    fill_shifted(normed_w, rows_in_g, cols_in_g, corner_in_g)

    def grad_row(l, carry):
        grad_fields[l] = conv_row(l, True).astype(BF)
        return carry

    lax.fori_loop(0, 8, grad_row, 0)

    gp_arrived(gp7, 7, 3)
    gp_out[...] = (jnp.sum(gp7[...], axis=0) * TOTAL_SCALE)[:, 0:96]
    sums(peer_a, me_a, s4, s5, 2, True, False)
    for k in range(9):
        taps_out[k // 3, k % 3 : k % 3 + 1, :] = s5[k]
    gain_out[...] = s5[9].reshape(D)


def hand_over(*refs):
    for k in range(5):
        refs[5 + k][...] = refs[k][...]


def body(
    fields, conv_kernel, layer_norm_gain, qkv_weight, out_weight, score_bias, pattern, cotangent
):
    vm = pl.BlockSpec(memory_space=pltpu.VMEM)
    hbm = pl.BlockSpec(memory_space=pl.ANY)
    dma = pltpu.SemaphoreType.DMA

    def vmem(shape, dtype):
        return pltpu.VMEM(shape, dtype)

    scratch = (
        [vmem((8, 32, D), BF), vmem((8, 32, D), BF), vmem((3, 3, D), F32), vmem((D,), F32), vmem((1, 256), jnp.int32)]
        + [vmem((D, 3 * D), BF), vmem((D, D), BF), vmem((24, 64, 64), F32), vmem((6, 64, 256), F32), dma((8,))]
        + [vmem((4, 1, D), BF)] * 4
        + [vmem((2, 8, D), BF), vmem((2, 8, D), BF)]
        + [vmem((2, 32, D), BF), vmem((2, 8, D), BF)] * 2
        + [dma((3,))] * 4
        + [vmem((3, 10, 32, D), F32), vmem((8, 32, D), BF), vmem((8, 32, D), F32), vmem((8, 32, 1), F32)]
        + [vmem((256, D), BF)] * 2
        + [vmem((8, 32, D), BF)]
        + [vmem((2, 256, 256), BF)] * 2
        + [vmem((256, 256), BF)]
        + [vmem((2, 256, 256), BF)] * 2
        + [vmem((2, 16, 16, D // 2), BF)] * 12
        + [vmem((16, 16, D), BF)] * 4
        + [dma((14,)), dma((14,))]
        + [vmem((6, 4, 64, 256), F32)]
        + [vmem((256, D), BF), vmem((256, D), BF), vmem((256, 3 * D), BF), vmem((256, D), BF), vmem((256, D), BF), vmem((256, 3 * D), BF)]
        + [vmem((4, 4, 48, D), BF), vmem((4, 4, 48, D), BF), vmem((2, 4, 24, D), F32)]
        + [vmem((4, 24, D), BF), vmem((4, 24, D), BF), vmem((4, 24, D), F32)]
        + [vmem((8, 24, 128), F32), vmem((8, 24, 128), F32)]
        + [dma((4,)), dma((4,))]
        + [vmem((10, 8, D), F32), vmem((16, 1, D), F32), vmem((16, 1, D), F32), vmem((1, D), F32), vmem((16, 1, D), F32), vmem((1, D), F32), vmem((16, 1, D), F32)]
        + [dma((3,)), dma((3,))]
    )
    results = (
        jax.ShapeDtypeStruct((8, 32, D), BF),
        jax.ShapeDtypeStruct((8, 32, D), BF),
        jax.ShapeDtypeStruct((24, 96), F32),
        jax.ShapeDtypeStruct((3, 3, D), F32),
        jax.ShapeDtypeStruct((D,), F32),
    )
    out = pl.pallas_call(
        kernel,
        out_shape=results,
        in_specs=[hbm] * 8,
        out_specs=(vm,) * 5,
        scratch_shapes=scratch,
        name="section",
        compiler_params=pltpu.CompilerParams(
            collective_id=0, has_side_effects=True, vmem_limit_bytes=60 << 20
        ),
    )(
        fields, cotangent, conv_kernel, layer_norm_gain,
        pattern.reshape(1, 256), qkv_weight, out_weight, score_bias,
    )
    block_out, grad_fields, gp, taps, gain = pl.pallas_call(
        hand_over, out_shape=results, in_specs=[vm] * 5, out_specs=(vm,) * 5, name="results"
    )(*out)
    return (block_out, grad_fields, jnp.transpose(gp), taps, gain)


def solution(mesh):
    split = P("lat", "lon", None)
    return jax.shard_map(
        body,
        mesh=mesh,
        in_specs=(split, P(), P(), P(), P(), P(), split, split),
        out_specs=(split, split, P("lat", "lon"), P(), P()),
        check_vma=False,
    )
```

```python
import math

import jax
import jax.numpy as jnp
from jax import lax
from jax.experimental import pallas as pl
from jax.experimental.pallas import tpu as pltpu
from jax.sharding import PartitionSpec as P

MESH = pl.DeviceIdType.MESH
BF = jnp.bfloat16
F32 = jnp.float32
D = 768
EPS = 1e-05
HEAD_SCALE = 32 ** (-0.5)
TOTAL_SCALE = 1.0 / math.sqrt(65536)


def nn(a, b):
    return lax.dot_general(a, b, (((1,), (0,)), ((), ())), preferred_element_type=F32)


def nt(a, b):
    return lax.dot_general(a, b, (((1,), (1,)), ((), ())), preferred_element_type=F32)


def tn(a, b):
    return lax.dot_general(a, b, (((0,), (0,)), ((), ())), preferred_element_type=F32)


def div(a, n):
    return lax.div(a, jnp.int32(n))


def rem(a, n):
    return lax.rem(a, jnp.int32(n))


def device(x, y, z, c):
    return (x * 2 + div(z, 4), rem(z, 4) * 8 + y * 2 + c)


def one_hot(cond):
    return jnp.where(cond, 1.0, 0.0).astype(BF)


def iota2(axis):
    return lax.broadcasted_iota(jnp.int32, (256, 256), axis)


def slot_order(s):
    x, zh, zl, y, c = s >> 6, (s >> 5) & 1, (s >> 3) & 3, (s >> 1) & 3, s & 1
    return x * 64 + y * 16 + zh * 8 + zl * 2 + c


def arrival_order(p):
    x, zh, zl, y, c = p >> 6, (p >> 5) & 1, (p >> 3) & 3, (p >> 1) & 3, p & 1
    return zh * 128 + zl * 32 + c * 16 + x * 4 + y


def kernel(
    fields_hbm, cot_hbm, taps_hbm, gain_hbm, pat_hbm, wqkv_hbm, wo_hbm, bias_hbm,
    block_out, grad_fields, gp_out, taps_out, gain_out,
    fields, cot, taps, gain, pat, wqkv, wo, bias, bias_t, w_sem,
    corners, corners_g, corner_in, corner_in_g, edges, edges_g, rows_in, cols_in, rows_in_g, cols_in_g, halo_s, halo_r, halo_gs, halo_gr,
    shifted, hid, xhat, rstd, work, work2, normed_w,
    perm_out, perm_home, perm_swap, perm_pos, perm_arr,
    c0, c1, c2, c3, n0, n1, n2, n3, g0, g1, g2, g3, m0, m1, m2, m3, a2a_s, a2a_r,
    qkv_part, block_v, grad_v, out_sem, probs, cot_g, nrm_g, qkv, grad_att, att, gqkv,
    gp0, gp1, gp2, gp3, gp4, gp5, gp6, gp7, gp_s, gp_r,
    acc, s0, s1, s2, s3, s4, s5, sum_s, sum_r,
):
    a = lax.axis_index("lat")
    b = lax.axis_index("lon")
    x, zh = div(a, 2), rem(a, 2)
    zl, y, c = div(b, 8), rem(div(b, 2), 4), rem(b, 2)
    z = zh * 4 + zl
    me_b = x * 4 + y
    me_a = z * 2 + c

    def peer_b(k):
        return device(div(k, 4), rem(k, 4), z, c)

    def peer_a(k):
        return device(x, y, div(k, 2), rem(k, 2))

    def neighbour(da, db):
        return (rem(a + da + 8, 8), rem(b + db + 32, 32))

    loads = {}
    for i, (name, src, dst) in enumerate(
        (
            ("fields", fields_hbm, fields), ("pat", pat_hbm, pat), ("cot", cot_hbm, cot),
            ("bias", bias_hbm, bias), ("taps", taps_hbm, taps), ("gain", gain_hbm, gain),
            ("wqkv", wqkv_hbm, wqkv), ("wo", wo_hbm, wo),
        )
    ):
        loads[name] = pltpu.make_async_copy(src, dst, w_sem.at[i])
        loads[name].start()

    bar = pltpu.get_barrier_semaphore()

    def greet(d, carry):
        pl.semaphore_signal(bar, inc=1, device_id=peer_b(rem(me_b + d, 16)), device_id_type=MESH)
        pl.semaphore_signal(bar, inc=1, device_id=peer_a(rem(me_a + d, 16)), device_id_type=MESH)
        return carry

    offsets = [(-1, 0), (1, 0), (0, -1), (0, 1), (-1, -1), (-1, 1), (1, -1), (1, 1)]
    for da, db in offsets:
        pl.semaphore_signal(bar, inc=1, device_id=neighbour(da, db), device_id_type=MESH)
    for d in range(1, 4):
        pl.semaphore_signal(
            bar, inc=1, device_id=device(rem(x + d, 4), y, rem(z + 4, 8), c), device_id_type=MESH
        )
    lax.fori_loop(1, 16, greet, 0)

    row8 = lax.broadcasted_iota(jnp.int32, (8, D), 0)
    row32 = lax.broadcasted_iota(jnp.int32, (32, D), 0)

    def fill_edges(source, dest, corner):
        left = jnp.zeros((8, D), F32)
        right = jnp.zeros((8, D), F32)
        for l in range(8):
            row = source[l].astype(F32)
            left = jnp.where(row8 == l, row[0:1, :], left)
            right = jnp.where(row8 == l, row[31:32, :], right)
        dest[0] = left.astype(BF)
        dest[1] = right.astype(BF)
        corner[0] = left[0:1].astype(BF)
        corner[1] = right[0:1].astype(BF)
        corner[2] = left[7:8].astype(BF)
        corner[3] = right[7:8].astype(BF)

    def arrived(ref, sem):
        pltpu.make_async_copy(ref, ref, sem).wait()

    def halo_start(kinds, source, edge, corner, rows, cols, corner_to, ss, rs):
        routes = [
            (source.at[0], rows.at[1], 0), (source.at[7], rows.at[0], 0),
            (edge.at[0], cols.at[1], 1), (edge.at[1], cols.at[0], 1),
            (corner.at[0], corner_to.at[3], 2), (corner.at[1], corner_to.at[2], 2),
            (corner.at[2], corner_to.at[1], 2), (corner.at[3], corner_to.at[0], 2),
        ]
        for m, (src, dst, kind) in enumerate(routes):
            if kind not in kinds:
                continue
            pltpu.make_async_remote_copy(
                src_ref=src, dst_ref=dst, send_sem=ss.at[kind], recv_sem=rs.at[kind],
                device_id=neighbour(*offsets[m]), device_id_type=MESH,
            ).start()

    def halo_wait(rows, cols, corner_to, ss, rs):
        for kind, ref in enumerate((rows, cols, corner_to)):
            arrived(ref, ss.at[kind])
            arrived(ref, rs.at[kind])

    top_mask = (a > 0).astype(F32)
    bottom_mask = (a < 7).astype(F32)

    def fill_inside(source):
        for r in range(1, 9):
            f = source[r - 1].astype(F32)
            shifted[0, r] = pltpu.roll(f, 1, 0)
            shifted[1, r] = f
            shifted[2, r] = pltpu.roll(f, 31, 0)

    def fill_rim(rows, cols, corner):
        for r, n, mask in ((0, 0, top_mask), (9, 1, bottom_mask)):
            f = rows[n].astype(F32) * mask
            le = corner[2 * n].astype(F32) * mask
            ri = corner[2 * n + 1].astype(F32) * mask
            shifted[0, r] = jnp.where(row32 == 0, le, pltpu.roll(f, 1, 0))
            shifted[1, r] = f
            shifted[2, r] = jnp.where(row32 == 31, ri, pltpu.roll(f, 31, 0))
        le = cols[0].astype(F32)
        ri = cols[1].astype(F32)
        for r in range(1, 9):
            shifted[0, r, 0:1, :] = le[r - 1 : r, :]
            shifted[2, r, 31:32, :] = ri[r - 1 : r, :]

    def exchange(peer, me, src, dst, slot, sends):
        if not sends:
            arrived(src.at[pl.ds(0, 15)], a2a_s.at[slot])
            arrived(dst.at[pl.ds(0, 15)], a2a_r.at[slot])
            return

        def step(d, carry):
            k = rem(me + d, 16)
            pltpu.make_async_remote_copy(
                src_ref=src.at[k], dst_ref=dst.at[me],
                send_sem=a2a_s.at[slot], recv_sem=a2a_r.at[slot],
                device_id=peer(k), device_id_type=MESH,
            ).start()
            return carry

        lax.fori_loop(1, 16, step, 0, unroll=15)
        dst[me] = src[me]

    def permute(perm, src, dst):
        for n in range(3):
            cols = slice(n * 256, (n + 1) * 256)
            rows = src[..., cols].reshape(256, 256)
            got = nn(perm[...], rows).astype(BF)
            dst[..., cols] = got.reshape(dst.shape[:-1] + (256,))

    def permute_out(perm, src, dst, half):
        rows = src[..., half * 384 : (half + 1) * 384].reshape(256, 384)
        dst[half] = nn(perm[half], rows).astype(BF).reshape(16, 16, 384)

    def permute_mid(src, dst, half):
        dst[half] = nn(perm_swap[...], src[half].reshape(256, 384)).astype(BF).reshape(16, 16, 384)

    def permute_in(perm, src, dst, half):
        got = nn(perm[half], src[half].reshape(256, 384)).astype(BF)
        dst[:, half * 384 : (half + 1) * 384] = got

    loads["fields"].wait()
    fill_edges(fields, edges, corners)
    pl.semaphore_wait(bar, 41)
    halo_start((0, 1, 2), fields, edges, corners, rows_in, cols_in, corner_in, halo_s, halo_r)

    loads["pat"].wait()
    pat_hot = one_hot(iota2(0) == pat[...])
    for half, first, second in ((0, slot_order, arrival_order), (1, arrival_order, slot_order)):
        order_hot = one_hot(iota2(0) == first(iota2(1)))
        perm_out[half] = nt(order_hot, pat_hot).astype(BF)
        perm_home[half] = nt(pat_hot, order_hot).astype(BF)
        perm_pos[half] = one_hot(iota2(1) == second(iota2(0)))
        perm_arr[half] = one_hot(iota2(0) == second(iota2(1)))
    perm_swap[...] = one_hot(iota2(1) == (iota2(0) & 15) * 16 + (iota2(0) >> 4))
    first_peer = ((peer_b, me_b), (peer_a, me_a))
    second_peer = ((peer_a, me_a), (peer_b, me_b))

    loads["cot"].wait()
    permute_out(perm_out, cot, c0, 0)
    exchange(*first_peer[0], c0.at[0], c1.at[0], 4, True)
    permute_out(perm_out, cot, c0, 1)

    loads["bias"].wait()
    for q in range(6):
        bias_t[q] = jnp.transpose(bias[4 * q : 4 * q + 4].reshape(256, 64))

    fill_inside(fields)
    halo_wait(rows_in, cols_in, corner_in, halo_s, halo_r)
    exchange(*first_peer[1], c0.at[1], c1.at[1], 5, True)
    fill_rim(rows_in, cols_in, corner_in)
    loads["taps"].wait()
    loads["gain"].wait()
    gain_row = gain[...].reshape(1, D)

    def conv_row(l, flip):
        out = shifted[1, l + 1]
        for i in range(3):
            for j in range(3):
                ti, tj = (2 - i, 2 - j) if flip else (i, j)
                out = out + taps[ti, tj : tj + 1, :] * shifted[j, l + i]
        return out

    def norm_row(l, carry):
        h = conv_row(l, False).astype(BF)
        hid[l] = h
        hf = h.astype(F32)
        mean = jnp.mean(hf, axis=-1, keepdims=True)
        rem = hf - mean
        var = jnp.mean(rem * rem, axis=-1, keepdims=True)
        inv = lax.rsqrt(var + EPS)
        xh = rem * inv
        xhat[l] = xh
        rstd[l] = inv
        normed_w[l] = (xh * gain_row).astype(BF)
        return carry

    lax.fori_loop(0, 8, norm_row, 0, unroll=2)
    for h in range(2):
        permute_out(perm_out, normed_w, n0, h)
        exchange(*first_peer[h], n0.at[h], n1.at[h], h, True)
    for h in range(2):
        exchange(*first_peer[h], c0.at[h], c1.at[h], 4 + h, False)
        permute_mid(c1, c2, h)
    for h in range(2):
        exchange(*first_peer[h], n0.at[h], n1.at[h], h, False)
        permute_mid(n1, n2, h)
        exchange(*second_peer[h], n2.at[h], n3.at[h], 2 + h, True)
    for h in range(2):
        exchange(*second_peer[h], c2.at[h], c3.at[h], 6 + h, True)

    exchange(*second_peer[1], n2.at[1], n3.at[1], 3, False)
    permute_in(perm_pos, n3, nrm_g, 1)
    loads["wqkv"].wait()
    for n in range(6):
        cols = slice(n * 384, (n + 1) * 384)
        qkv_part[:, cols] = nn(nrm_g[:, 384:], wqkv[384:, cols])
    exchange(*second_peer[0], n2.at[0], n3.at[0], 2, False)
    permute_in(perm_pos, n3, nrm_g, 0)
    for n in range(6):
        cols = slice(n * 384, (n + 1) * 384)
        qkv[:, cols] = (nn(nrm_g[:, :384], wqkv[:384, cols]) + qkv_part[:, cols]).astype(BF)

    lane_head = lax.broadcasted_iota(jnp.int32, (64, 128), 1) >> 5

    def spread(v):
        vf = v.astype(F32)
        return jnp.concatenate(
            [jnp.where(lane_head == e, vf, 0.0).astype(BF) for e in range(4)], axis=0
        )

    def gather(v):
        out = jnp.zeros((64, 128), F32)
        for e in range(4):
            out = jnp.where(lane_head == e, v[e * 64 : (e + 1) * 64, :], out)
        return out

    def columns(q, part):
        return pl.ds(pl.multiple_of(q * 128 + part * D, 128), 128)

    def attend(q, carry):
        for g in range(4):
            rows = slice(g * 64, (g + 1) * 64)
            q_bd = spread(qkv[rows, columns(q, 0)])
            st = nt(qkv[rows, columns(q, 1)], q_bd) * HEAD_SCALE + bias_t[q]
            e = jnp.exp(st - jnp.max(st, axis=0, keepdims=True))
            p = e * (1.0 / jnp.sum(e, axis=0, keepdims=True))
            probs[q, g] = p
            att[rows, columns(q, 0)] = gather(tn(p.astype(BF), qkv[rows, columns(q, 2)])).astype(BF)
        return carry

    def attend_back(q, carry):
        for g in range(4):
            rows = slice(g * 64, (g + 1) * 64)
            q_bd = spread(qkv[rows, columns(q, 0)])
            g_bd = spread(grad_att[rows, columns(q, 0)])
            p = probs[q, g]
            dp = nt(qkv[rows, columns(q, 2)], g_bd)
            ds = (p * (dp - jnp.sum(p * dp, axis=0, keepdims=True))).astype(BF)
            dq = gather(tn(ds, qkv[rows, columns(q, 1)])) * HEAD_SCALE
            gqkv[rows, columns(q, 0)] = dq.astype(BF)
            gqkv[rows, columns(q, 1)] = (nn(ds, q_bd) * HEAD_SCALE).astype(BF)
            gqkv[rows, columns(q, 2)] = nn(p.astype(BF), g_bd).astype(BF)
        return carry

    lax.fori_loop(0, 6, attend, 0)

    loads["wo"].wait()
    for n in range(3):
        cols = slice(n * 256, (n + 1) * 256)
        work2[:, cols] = nn(att[...], wo[:, cols]).astype(BF)
    permute(perm_arr.at[0], work2, m0)
    exchange(peer_a, me_a, m0, m1, 8, True)

    for h in range(2):
        exchange(*second_peer[h], c2.at[h], c3.at[h], 6 + h, False)
        permute_in(perm_pos, c3, cot_g, h)

    def outer(n, carry):
        cols = pl.ds(pl.multiple_of(n * 384, 128), 384)
        got = tn(cot_g[:, cols], att[...]).astype(BF)
        gp0[pl.ds(2 * n, 2)] = got.reshape(2, 4, 48, D)
        return carry

    lax.fori_loop(0, 2, outer, 0)

    def gp_y(d):
        k = rem(y + d, 4)
        pltpu.make_async_remote_copy(
            src_ref=gp0.at[:, k], dst_ref=gp1.at[y], send_sem=gp_s.at[0], recv_sem=gp_r.at[0],
            device_id=device(x, k, z, c), device_id_type=MESH,
        ).start()

    def gp_z(d):
        k = rem(zl + d, 4)
        pltpu.make_async_remote_copy(
            src_ref=gp3.at[k], dst_ref=gp4.at[zl], send_sem=gp_s.at[2], recv_sem=gp_r.at[2],
            device_id=device(x, y, zh * 4 + k, c), device_id_type=MESH,
        ).start()

    def gp_l(d):
        k = rem(a + d, 8)
        pltpu.make_async_remote_copy(
            src_ref=gp6.at[k], dst_ref=gp7.at[a], send_sem=gp_s.at[3], recv_sem=gp_r.at[3],
            device_id=(k, b), device_id_type=MESH,
        ).start()

    def gp_arrived(ref, n, stage):
        arrived(ref.at[pl.ds(0, n)], gp_s.at[stage])
        arrived(ref.at[pl.ds(0, n)], gp_r.at[stage])

    for d in range(1, 4):
        gp_y(d)
    for k in range(4):
        gp1[y, k] = gp0[k, y]

    for n in range(3):
        cols = slice(n * 256, (n + 1) * 256)
        grad_att[:, cols] = nt(cot_g[...], wo[cols, :]).astype(BF)

    lax.fori_loop(0, 6, attend_back, 0)

    for half in range(2):
        cols = slice(half * 384, (half + 1) * 384)
        work[:, cols] = nt(gqkv[...], wqkv[cols, :]).astype(BF)
        permute_out(perm_arr, work, g0, half)
        exchange(*second_peer[half], g0.at[half], g1.at[half], 10 + half, True)

    exchange(peer_a, me_a, m0, m1, 8, False)
    permute(perm_swap, m1, m2)
    exchange(peer_b, me_b, m2, m3, 9, True)

    for half in range(2):
        exchange(*second_peer[half], g0.at[half], g1.at[half], 10 + half, False)
        permute_mid(g1, g2, half)
        exchange(*first_peer[half], g2.at[half], g3.at[half], 12 + half, True)

    gp_arrived(gp1, 3, 0)
    for k in range(4):
        total = gp1[0, k].astype(F32)
        for i in range(1, 4):
            total = total + gp1[i, k].astype(F32)
        gp2[0, k] = total[0:24]
        gp2[1, k] = total[24:48]
    core = pltpu.make_async_remote_copy(
        src_ref=gp2.at[1 - c], dst_ref=gp5, send_sem=gp_s.at[1], recv_sem=gp_r.at[1],
        device_id=device(x, y, z, 1 - c), device_id_type=MESH,
    )
    core.start()

    exchange(peer_b, me_b, m2, m3, 9, False)
    permute(perm_home.at[0], m3, work2)
    for l in range(8):
        block_v[l] = (hid[l].astype(F32) + work2[l * 32 : (l + 1) * 32, :].astype(F32)).astype(BF)
    block_copy = pltpu.make_async_copy(block_v, block_out, out_sem.at[8])
    block_copy.start()

    core.wait()
    for k in range(4):
        gp3[k] = (gp2[c, k] + gp5[k]).astype(BF)
    for d in range(1, 4):
        gp_z(d)
    gp4[zl] = gp3[zl]

    for half in range(2):
        exchange(*first_peer[half], g2.at[half], g3.at[half], 12 + half, False)
        permute_in(perm_home, g3, work, half)
    acc[...] = jnp.zeros_like(acc)

    def norm_back(l, carry):
        at = l * 32 if isinstance(l, int) else pl.multiple_of(l * 32, 32)
        ng = work[pl.ds(at, 32), :].astype(F32)
        xh = xhat[l]
        prod = ng * xh
        acc[9] += jnp.sum(prod.reshape(4, 8, D), axis=0)
        u = ng * gain_row
        mu = jnp.mean(u, axis=-1, keepdims=True)
        mux = jnp.mean(prod * gain_row, axis=-1, keepdims=True)
        gh = cot[l].astype(F32) + rstd[l] * (u - mu - xh * mux)
        normed_w[l] = gh.astype(BF)
        return carry

    halo_g = (normed_w, edges_g, corners_g, rows_in_g, cols_in_g, corner_in_g, halo_gs, halo_gr)
    norm_back(0, 0)
    norm_back(7, 0)
    halo_start((0,), *halo_g)
    lax.fori_loop(1, 7, norm_back, 0, unroll=2)
    fill_edges(normed_w, edges_g, corners_g)
    halo_start((1, 2), *halo_g)

    def tap_sums(l, carry):
        gh = normed_w[l].astype(F32)
        for i in range(3):
            for j in range(3):
                acc[3 * i + j] += jnp.sum((shifted[j, l + i] * gh).reshape(4, 8, D), axis=0)
        return carry

    lax.fori_loop(0, 8, tap_sums, 0, unroll=2)
    for k in range(16):
        if k < 10:
            s0[k] = jnp.sum(acc[k], axis=0, keepdims=True)
        else:
            s0[k] = jnp.zeros((1, D), F32)

    def sums(peer, me, src, dst, slot, whole_src, sends):
        if not sends:
            arrived(dst.at[pl.ds(0, 15)], sum_s.at[slot])
            arrived(dst.at[pl.ds(0, 15)], sum_r.at[slot])
            return

        def step(d, carry):
            k = rem(me + d, 16)
            pltpu.make_async_remote_copy(
                src_ref=src if whole_src else src.at[k], dst_ref=dst.at[me],
                send_sem=sum_s.at[slot], recv_sem=sum_r.at[slot],
                device_id=peer(k), device_id_type=MESH,
            ).start()
            return carry

        lax.fori_loop(1, 16, step, 0, unroll=15)
        dst[me] = src[...] if whole_src else src[me]

    sums(peer_b, me_b, s0, s1, 0, False, True)
    fill_inside(normed_w)

    sums(peer_b, me_b, s0, s1, 0, False, False)
    s2[...] = jnp.sum(s1[...], axis=0)
    sums(peer_a, me_a, s2, s3, 1, True, True)

    gp_arrived(gp4, 3, 2)
    total = gp4[0].astype(F32)
    for i in range(1, 4):
        total = total + gp4[i].astype(F32)
    for i in range(8):
        gp6[i, :, 0:96] = total[:, i * 96 : (i + 1) * 96]
        gp6[i, :, 96:128] = jnp.zeros((24, 32), F32)
    for d in range(1, 8):
        gp_l(d)
    gp7[a] = gp6[a]

    sums(peer_a, me_a, s2, s3, 1, True, False)
    s4[...] = jnp.sum(s3[...], axis=0) * TOTAL_SCALE
    sums(peer_b, me_b, s4, s5, 2, True, True)

    halo_wait(rows_in_g, cols_in_g, corner_in_g, halo_gs, halo_gr)
    fill_rim(rows_in_g, cols_in_g, corner_in_g)

    def grad_row(l, carry):
        grad_v[l] = conv_row(l, True).astype(BF)
        pltpu.make_async_copy(grad_v.at[l], grad_fields.at[l], out_sem.at[l]).start()
        return carry

    lax.fori_loop(0, 8, grad_row, 0, unroll=2)

    gp_arrived(gp7, 7, 3)
    gp_out[...] = (jnp.sum(gp7[...], axis=0) * TOTAL_SCALE)[:, 0:96]
    sums(peer_b, me_b, s4, s5, 2, True, False)
    for k in range(9):
        taps_out[k // 3, k % 3 : k % 3 + 1, :] = s5[k]
    gain_out[...] = s5[9].reshape(D)
    block_copy.wait()
    for l in range(8):
        pltpu.make_async_copy(grad_v.at[l], grad_fields.at[l], out_sem.at[l]).wait()


def hand_over(*refs):
    sems = refs[10]
    copies = []
    for k in range(5):
        if k < 2:
            for l in range(8):
                copies.append((refs[k].at[l], refs[5 + k].at[l]))
        else:
            copies.append((refs[k], refs[5 + k]))
    copies = [pltpu.make_async_copy(src, dst, sems.at[i]) for i, (src, dst) in enumerate(copies)]
    for copy in copies:
        copy.start()
    for copy in copies:
        copy.wait()


def body(
    fields, conv_kernel, layer_norm_gain, qkv_weight, out_weight, score_bias, pattern, cotangent
):
    vm = pl.BlockSpec(memory_space=pltpu.VMEM)
    hbm = pl.BlockSpec(memory_space=pl.ANY)
    dma = pltpu.SemaphoreType.DMA

    def vmem(shape, dtype):
        return pltpu.VMEM(shape, dtype)

    scratch = (
        [vmem((8, 32, D), BF), vmem((8, 32, D), BF), vmem((3, 3, D), F32), vmem((D,), F32), vmem((1, 256), jnp.int32)]
        + [vmem((D, 3 * D), BF), vmem((D, D), BF), vmem((24, 64, 64), F32), vmem((6, 64, 256), F32), dma((8,))]
        + [vmem((4, 1, D), BF)] * 4
        + [vmem((2, 8, D), BF), vmem((2, 8, D), BF)]
        + [vmem((2, 32, D), BF), vmem((2, 8, D), BF)] * 2
        + [dma((3,))] * 4
        + [vmem((3, 10, 32, D), F32), vmem((8, 32, D), BF), vmem((8, 32, D), F32), vmem((8, 32, 1), F32)]
        + [vmem((256, D), BF)] * 2
        + [vmem((8, 32, D), BF)]
        + [vmem((2, 256, 256), BF)] * 2
        + [vmem((256, 256), BF)]
        + [vmem((2, 256, 256), BF)] * 2
        + [vmem((2, 16, 16, D // 2), BF)] * 12
        + [vmem((16, 16, D), BF)] * 4
        + [dma((14,)), dma((14,))]
        + [vmem((256, 3 * D), F32), vmem((8, 32, D), BF), vmem((8, 32, D), BF), dma((9,))]
        + [vmem((6, 4, 64, 256), F32)]
        + [vmem((256, D), BF), vmem((256, D), BF), vmem((256, 3 * D), BF), vmem((256, D), BF), vmem((256, D), BF), vmem((256, 3 * D), BF)]
        + [vmem((4, 4, 48, D), BF), vmem((4, 4, 48, D), BF), vmem((2, 4, 24, D), F32)]
        + [vmem((4, 24, D), BF), vmem((4, 24, D), BF), vmem((4, 24, D), F32)]
        + [vmem((8, 24, 128), F32), vmem((8, 24, 128), F32)]
        + [dma((4,)), dma((4,))]
        + [vmem((10, 8, D), F32), vmem((16, 1, D), F32), vmem((16, 1, D), F32), vmem((1, D), F32), vmem((16, 1, D), F32), vmem((1, D), F32), vmem((16, 1, D), F32)]
        + [dma((3,)), dma((3,))]
    )
    results = (
        jax.ShapeDtypeStruct((8, 32, D), BF),
        jax.ShapeDtypeStruct((8, 32, D), BF),
        jax.ShapeDtypeStruct((24, 96), F32),
        jax.ShapeDtypeStruct((3, 3, D), F32),
        jax.ShapeDtypeStruct((D,), F32),
    )
    out = pl.pallas_call(
        kernel,
        out_shape=results,
        in_specs=[hbm] * 8,
        out_specs=(hbm,) * 2 + (vm,) * 3,
        scratch_shapes=scratch,
        name="section",
        compiler_params=pltpu.CompilerParams(
            collective_id=0, has_side_effects=True, vmem_limit_bytes=60 << 20
        ),
    )(
        fields, cotangent, conv_kernel, layer_norm_gain,
        pattern.reshape(1, 256), qkv_weight, out_weight, score_bias,
    )
    block_out, grad_fields, gp, taps, gain = pl.pallas_call(
        hand_over, out_shape=results, in_specs=[hbm] * 5, out_specs=(hbm,) * 5,
        scratch_shapes=[dma((19,))], name="results",
    )(*out)
    return (block_out, grad_fields, jnp.transpose(gp), taps, gain)


def solution(mesh):
    split = P("lat", "lon", None)
    return jax.shard_map(
        body,
        mesh=mesh,
        in_specs=(split, P(), P(), P(), P(), P(), split, split),
        out_specs=(split, split, P("lat", "lon"), P(), P()),
        check_vma=False,
    )
```

```python
import math

import jax
import jax.numpy as jnp
from jax import lax
from jax.experimental import pallas as pl
from jax.experimental.pallas import tpu as pltpu
from jax.sharding import PartitionSpec as P

MESH = pl.DeviceIdType.MESH
BF = jnp.bfloat16
F32 = jnp.float32
D = 768
EPS = 1e-05
HEAD_SCALE = 32 ** (-0.5)
TOTAL_SCALE = 1.0 / math.sqrt(65536)


def nn(a, b):
    return lax.dot_general(a, b, (((1,), (0,)), ((), ())), preferred_element_type=F32)


def nt(a, b):
    return lax.dot_general(a, b, (((1,), (1,)), ((), ())), preferred_element_type=F32)


def tn(a, b):
    return lax.dot_general(a, b, (((0,), (0,)), ((), ())), preferred_element_type=F32)


def div(a, n):
    return lax.div(a, jnp.int32(n))


def rem(a, n):
    return lax.rem(a, jnp.int32(n))


def device(x, y, z, c):
    return (x * 2 + div(z, 4), rem(z, 4) * 8 + y * 2 + c)


def one_hot(cond):
    return jnp.where(cond, 1.0, 0.0).astype(BF)


def iota2(axis):
    return lax.broadcasted_iota(jnp.int32, (256, 256), axis)


def slot_order(s):
    x, zh, zl, y, c = s >> 6, (s >> 5) & 1, (s >> 3) & 3, (s >> 1) & 3, s & 1
    return x * 64 + y * 16 + zh * 8 + zl * 2 + c


def arrival_order(p):
    x, zh, zl, y, c = p >> 6, (p >> 5) & 1, (p >> 3) & 3, (p >> 1) & 3, p & 1
    return zh * 128 + zl * 32 + c * 16 + x * 4 + y


def kernel(
    fields_hbm, cot_hbm, taps_hbm, gain_hbm, pat_hbm, wqkv_hbm, wo_hbm, bias_hbm,
    block_out, grad_fields, gp_out, taps_out, gain_out,
    fields, cot, taps, gain, pat, wqkv, wo, bias, bias_t, w_sem,
    corners, corners_g, corner_in, corner_in_g, edges, edges_g, rows_in, cols_in, rows_in_g, cols_in_g, halo_s, halo_r, halo_gs, halo_gr,
    shifted, hid, xhat, rstd, work, work2, normed_w,
    perm_out, perm_home, perm_swap, perm_pos, perm_arr,
    c0, c1, c2, c3, n0, n1, n2, n3, g0, g1, g2, g3, m0, m1, m2, m3, a2a_s, a2a_r,
    qkv_part, block_v, grad_v, out_sem, probs, cot_g, nrm_g, qkv, grad_att, att, gqkv,
    gp0, gpx, gpa, gp1, gp3, gp4, gp6, gp7, gp_s, gp_r,
    acc, s0, s1, s2, s3, s4, s5, sum_s, sum_r,
):
    a = lax.axis_index("lat")
    b = lax.axis_index("lon")
    x, zh = div(a, 2), rem(a, 2)
    zl, y, c = div(b, 8), rem(div(b, 2), 4), rem(b, 2)
    z = zh * 4 + zl
    me_b = x * 4 + y
    me_a = z * 2 + c

    def peer_b(k):
        return device(div(k, 4), rem(k, 4), z, c)

    def peer_a(k):
        return device(x, y, div(k, 2), rem(k, 2))

    def neighbour(da, db):
        return (rem(a + da + 8, 8), rem(b + db + 32, 32))

    loads = {}
    for i, (name, src, dst) in enumerate(
        (
            ("fields", fields_hbm, fields), ("pat", pat_hbm, pat), ("cot", cot_hbm, cot),
            ("bias", bias_hbm, bias), ("taps", taps_hbm, taps), ("gain", gain_hbm, gain),
            ("wqkv", wqkv_hbm, wqkv), ("wo", wo_hbm, wo),
        )
    ):
        loads[name] = pltpu.make_async_copy(src, dst, w_sem.at[i])
        loads[name].start()

    bar = pltpu.get_barrier_semaphore()

    def greet(d, carry):
        pl.semaphore_signal(bar, inc=1, device_id=peer_b(rem(me_b + d, 16)), device_id_type=MESH)
        pl.semaphore_signal(bar, inc=1, device_id=peer_a(rem(me_a + d, 16)), device_id_type=MESH)
        return carry

    offsets = [(-1, 0), (1, 0), (0, -1), (0, 1), (-1, -1), (-1, 1), (1, -1), (1, 1)]
    for da, db in offsets:
        pl.semaphore_signal(bar, inc=1, device_id=neighbour(da, db), device_id_type=MESH)
    for d in range(1, 4):
        pl.semaphore_signal(
            bar, inc=1, device_id=device(rem(x + d, 4), y, rem(z + 4, 8), c), device_id_type=MESH
        )
    lax.fori_loop(1, 16, greet, 0)

    row8 = lax.broadcasted_iota(jnp.int32, (8, D), 0)
    row32 = lax.broadcasted_iota(jnp.int32, (32, D), 0)

    def fill_edges(source, dest, corner):
        left = jnp.zeros((8, D), F32)
        right = jnp.zeros((8, D), F32)
        for l in range(8):
            row = source[l].astype(F32)
            left = jnp.where(row8 == l, row[0:1, :], left)
            right = jnp.where(row8 == l, row[31:32, :], right)
        dest[0] = left.astype(BF)
        dest[1] = right.astype(BF)
        corner[0] = left[0:1].astype(BF)
        corner[1] = right[0:1].astype(BF)
        corner[2] = left[7:8].astype(BF)
        corner[3] = right[7:8].astype(BF)

    def arrived(ref, sem):
        pltpu.make_async_copy(ref, ref, sem).wait()

    def halo_start(kinds, source, edge, corner, rows, cols, corner_to, ss, rs):
        routes = [
            (source.at[0], rows.at[1], 0), (source.at[7], rows.at[0], 0),
            (edge.at[0], cols.at[1], 1), (edge.at[1], cols.at[0], 1),
            (corner.at[0], corner_to.at[3], 2), (corner.at[1], corner_to.at[2], 2),
            (corner.at[2], corner_to.at[1], 2), (corner.at[3], corner_to.at[0], 2),
        ]
        for m, (src, dst, kind) in enumerate(routes):
            if kind not in kinds:
                continue
            pltpu.make_async_remote_copy(
                src_ref=src, dst_ref=dst, send_sem=ss.at[kind], recv_sem=rs.at[kind],
                device_id=neighbour(*offsets[m]), device_id_type=MESH,
            ).start()

    def halo_wait(rows, cols, corner_to, ss, rs):
        for kind, ref in enumerate((rows, cols, corner_to)):
            arrived(ref, ss.at[kind])
            arrived(ref, rs.at[kind])

    top_mask = (a > 0).astype(F32)
    bottom_mask = (a < 7).astype(F32)

    def fill_inside(source):
        for r in range(1, 9):
            f = source[r - 1].astype(F32)
            shifted[0, r] = pltpu.roll(f, 1, 0)
            shifted[1, r] = f
            shifted[2, r] = pltpu.roll(f, 31, 0)

    def fill_rim(rows, cols, corner):
        for r, n, mask in ((0, 0, top_mask), (9, 1, bottom_mask)):
            f = rows[n].astype(F32) * mask
            le = corner[2 * n].astype(F32) * mask
            ri = corner[2 * n + 1].astype(F32) * mask
            shifted[0, r] = jnp.where(row32 == 0, le, pltpu.roll(f, 1, 0))
            shifted[1, r] = f
            shifted[2, r] = jnp.where(row32 == 31, ri, pltpu.roll(f, 31, 0))
        le = cols[0].astype(F32)
        ri = cols[1].astype(F32)
        for r in range(1, 9):
            shifted[0, r, 0:1, :] = le[r - 1 : r, :]
            shifted[2, r, 31:32, :] = ri[r - 1 : r, :]

    def exchange(peer, me, src, dst, slot, sends):
        if not sends:
            arrived(src.at[pl.ds(0, 15)], a2a_s.at[slot])
            arrived(dst.at[pl.ds(0, 15)], a2a_r.at[slot])
            return

        def step(d, carry):
            k = rem(me + d, 16)
            pltpu.make_async_remote_copy(
                src_ref=src.at[k], dst_ref=dst.at[me],
                send_sem=a2a_s.at[slot], recv_sem=a2a_r.at[slot],
                device_id=peer(k), device_id_type=MESH,
            ).start()
            return carry

        lax.fori_loop(1, 16, step, 0, unroll=15)
        dst[me] = src[me]

    def permute(perm, src, dst):
        for n in range(3):
            cols = slice(n * 256, (n + 1) * 256)
            rows = src[..., cols].reshape(256, 256)
            got = nn(perm[...], rows).astype(BF)
            dst[..., cols] = got.reshape(dst.shape[:-1] + (256,))

    def permute_out(perm, src, dst, half):
        rows = src[..., half * 384 : (half + 1) * 384].reshape(256, 384)
        dst[half] = nn(perm[half], rows).astype(BF).reshape(16, 16, 384)

    def permute_mid(src, dst, half):
        dst[half] = nn(perm_swap[...], src[half].reshape(256, 384)).astype(BF).reshape(16, 16, 384)

    def permute_in(perm, src, dst, half):
        got = nn(perm[half], src[half].reshape(256, 384)).astype(BF)
        dst[:, half * 384 : (half + 1) * 384] = got

    loads["fields"].wait()
    fill_edges(fields, edges, corners)
    pl.semaphore_wait(bar, 41)
    halo_start((0, 1, 2), fields, edges, corners, rows_in, cols_in, corner_in, halo_s, halo_r)

    loads["pat"].wait()
    pat_hot = one_hot(iota2(0) == pat[...])
    for half, first, second in ((0, slot_order, arrival_order), (1, arrival_order, slot_order)):
        order_hot = one_hot(iota2(0) == first(iota2(1)))
        perm_out[half] = nt(order_hot, pat_hot).astype(BF)
        perm_home[half] = nt(pat_hot, order_hot).astype(BF)
        perm_pos[half] = one_hot(iota2(1) == second(iota2(0)))
        perm_arr[half] = one_hot(iota2(0) == second(iota2(1)))
    perm_swap[...] = one_hot(iota2(1) == (iota2(0) & 15) * 16 + (iota2(0) >> 4))
    first_peer = ((peer_b, me_b), (peer_a, me_a))
    second_peer = ((peer_a, me_a), (peer_b, me_b))

    loads["cot"].wait()
    permute_out(perm_out, cot, c0, 0)
    exchange(*first_peer[0], c0.at[0], c1.at[0], 4, True)
    permute_out(perm_out, cot, c0, 1)

    loads["bias"].wait()
    for q in range(6):
        bias_t[q] = jnp.transpose(bias[4 * q : 4 * q + 4].reshape(256, 64))

    fill_inside(fields)
    halo_wait(rows_in, cols_in, corner_in, halo_s, halo_r)
    exchange(*first_peer[1], c0.at[1], c1.at[1], 5, True)
    fill_rim(rows_in, cols_in, corner_in)
    loads["taps"].wait()
    loads["gain"].wait()
    gain_row = gain[...].reshape(1, D)

    def conv_row(l, flip):
        out = shifted[1, l + 1]
        for i in range(3):
            for j in range(3):
                ti, tj = (2 - i, 2 - j) if flip else (i, j)
                out = out + taps[ti, tj : tj + 1, :] * shifted[j, l + i]
        return out

    def norm_row(l, carry):
        h = conv_row(l, False).astype(BF)
        hid[l] = h
        hf = h.astype(F32)
        mean = jnp.mean(hf, axis=-1, keepdims=True)
        rem = hf - mean
        var = jnp.mean(rem * rem, axis=-1, keepdims=True)
        inv = lax.rsqrt(var + EPS)
        xh = rem * inv
        xhat[l] = xh
        rstd[l] = inv
        normed_w[l] = (xh * gain_row).astype(BF)
        return carry

    lax.fori_loop(0, 8, norm_row, 0, unroll=2)
    for h in range(2):
        permute_out(perm_out, normed_w, n0, h)
        exchange(*first_peer[h], n0.at[h], n1.at[h], h, True)
    for h in range(2):
        exchange(*first_peer[h], c0.at[h], c1.at[h], 4 + h, False)
        permute_mid(c1, c2, h)
    for h in range(2):
        exchange(*first_peer[h], n0.at[h], n1.at[h], h, False)
        permute_mid(n1, n2, h)
        exchange(*second_peer[h], n2.at[h], n3.at[h], 2 + h, True)
    for h in range(2):
        exchange(*second_peer[h], c2.at[h], c3.at[h], 6 + h, True)

    exchange(*second_peer[1], n2.at[1], n3.at[1], 3, False)
    permute_in(perm_pos, n3, nrm_g, 1)
    loads["wqkv"].wait()
    for n in range(6):
        cols = slice(n * 384, (n + 1) * 384)
        qkv_part[:, cols] = nn(nrm_g[:, 384:], wqkv[384:, cols])
    exchange(*second_peer[0], n2.at[0], n3.at[0], 2, False)
    permute_in(perm_pos, n3, nrm_g, 0)
    for n in range(6):
        cols = slice(n * 384, (n + 1) * 384)
        qkv[:, cols] = (nn(nrm_g[:, :384], wqkv[:384, cols]) + qkv_part[:, cols]).astype(BF)

    lane_head = lax.broadcasted_iota(jnp.int32, (64, 128), 1) >> 5

    def spread(v):
        vf = v.astype(F32)
        return jnp.concatenate(
            [jnp.where(lane_head == e, vf, 0.0).astype(BF) for e in range(4)], axis=0
        )

    def gather(v):
        out = jnp.zeros((64, 128), F32)
        for e in range(4):
            out = jnp.where(lane_head == e, v[e * 64 : (e + 1) * 64, :], out)
        return out

    def columns(q, part):
        return pl.ds(pl.multiple_of(q * 128 + part * D, 128), 128)

    def attend(q, carry):
        for g in range(4):
            rows = slice(g * 64, (g + 1) * 64)
            q_bd = spread(qkv[rows, columns(q, 0)])
            st = nt(qkv[rows, columns(q, 1)], q_bd) * HEAD_SCALE + bias_t[q]
            e = jnp.exp(st - jnp.max(st, axis=0, keepdims=True))
            p = e * (1.0 / jnp.sum(e, axis=0, keepdims=True))
            probs[q, g] = p
            att[rows, columns(q, 0)] = gather(tn(p.astype(BF), qkv[rows, columns(q, 2)])).astype(BF)
        return carry

    def attend_back(q, carry):
        for g in range(4):
            rows = slice(g * 64, (g + 1) * 64)
            q_bd = spread(qkv[rows, columns(q, 0)])
            g_bd = spread(grad_att[rows, columns(q, 0)])
            p = probs[q, g]
            dp = nt(qkv[rows, columns(q, 2)], g_bd)
            ds = (p * (dp - jnp.sum(p * dp, axis=0, keepdims=True))).astype(BF)
            dq = gather(tn(ds, qkv[rows, columns(q, 1)])) * HEAD_SCALE
            gqkv[rows, columns(q, 0)] = dq.astype(BF)
            gqkv[rows, columns(q, 1)] = (nn(ds, q_bd) * HEAD_SCALE).astype(BF)
            gqkv[rows, columns(q, 2)] = nn(p.astype(BF), g_bd).astype(BF)
        return carry

    lax.fori_loop(0, 6, attend, 0)

    loads["wo"].wait()
    for n in range(3):
        cols = slice(n * 256, (n + 1) * 256)
        work2[:, cols] = nn(att[...], wo[:, cols]).astype(BF)
    permute(perm_arr.at[0], work2, m0)
    exchange(peer_a, me_a, m0, m1, 8, True)

    for h in range(2):
        exchange(*second_peer[h], c2.at[h], c3.at[h], 6 + h, False)
        permute_in(perm_pos, c3, cot_g, h)

    def outer(n, carry):
        cols = pl.ds(pl.multiple_of(n * 384, 128), 384)
        got = tn(cot_g[:, cols], att[...])
        gp0[pl.ds(2 * n, 2)] = got.reshape(2, 4, 2, 24, D).astype(BF)
        return carry

    lax.fori_loop(0, 2, outer, 0)
    core = pltpu.make_async_remote_copy(
        src_ref=gp0.at[:, :, 1 - c], dst_ref=gpx, send_sem=gp_s.at[1], recv_sem=gp_r.at[1],
        device_id=device(x, y, z, 1 - c), device_id_type=MESH,
    )
    core.start()

    def gp_y(d):
        k = rem(y + d, 4)
        pltpu.make_async_remote_copy(
            src_ref=gpa.at[:, k], dst_ref=gp1.at[y], send_sem=gp_s.at[0], recv_sem=gp_r.at[0],
            device_id=device(x, k, z, c), device_id_type=MESH,
        ).start()

    def gp_z(d):
        k = rem(zl + d, 4)
        pltpu.make_async_remote_copy(
            src_ref=gp3.at[k], dst_ref=gp4.at[zl], send_sem=gp_s.at[2], recv_sem=gp_r.at[2],
            device_id=device(x, y, zh * 4 + k, c), device_id_type=MESH,
        ).start()

    def gp_l(d):
        k = rem(a + d, 8)
        pltpu.make_async_remote_copy(
            src_ref=gp6.at[k], dst_ref=gp7.at[a], send_sem=gp_s.at[3], recv_sem=gp_r.at[3],
            device_id=(k, b), device_id_type=MESH,
        ).start()

    def gp_arrived(ref, n, stage):
        arrived(ref.at[pl.ds(0, n)], gp_s.at[stage])
        arrived(ref.at[pl.ds(0, n)], gp_r.at[stage])

    for n in range(3):
        cols = slice(n * 256, (n + 1) * 256)
        grad_att[:, cols] = nt(cot_g[...], wo[cols, :]).astype(BF)

    lax.fori_loop(0, 3, attend_back, 0)
    core.wait()
    for k in range(4):
        gpa[k] = (gp0[k, :, c].astype(F32) + gpx[k].astype(F32)).astype(BF)
    for d in range(1, 4):
        gp_y(d)
    for k in range(4):
        gp1[y, k] = gpa[k, y]
    lax.fori_loop(3, 6, attend_back, 0)

    for half in range(2):
        cols = slice(half * 384, (half + 1) * 384)
        work[:, cols] = nt(gqkv[...], wqkv[cols, :]).astype(BF)
        permute_out(perm_arr, work, g0, half)
        exchange(*second_peer[half], g0.at[half], g1.at[half], 10 + half, True)

    exchange(peer_a, me_a, m0, m1, 8, False)
    permute(perm_swap, m1, m2)
    exchange(peer_b, me_b, m2, m3, 9, True)

    for half in range(2):
        exchange(*second_peer[half], g0.at[half], g1.at[half], 10 + half, False)
        permute_mid(g1, g2, half)
        exchange(*first_peer[half], g2.at[half], g3.at[half], 12 + half, True)

    gp_arrived(gp1, 3, 0)
    for k in range(4):
        total = gp1[0, k].astype(F32)
        for i in range(1, 4):
            total = total + gp1[i, k].astype(F32)
        gp3[k] = total.astype(BF)
    for d in range(1, 4):
        gp_z(d)
    gp4[zl] = gp3[zl]

    exchange(peer_b, me_b, m2, m3, 9, False)
    permute(perm_home.at[0], m3, work2)
    for l in range(8):
        block_v[l] = (hid[l].astype(F32) + work2[l * 32 : (l + 1) * 32, :].astype(F32)).astype(BF)
    block_copy = pltpu.make_async_copy(block_v, block_out, out_sem.at[8])
    block_copy.start()

    for half in range(2):
        exchange(*first_peer[half], g2.at[half], g3.at[half], 12 + half, False)
        permute_in(perm_home, g3, work, half)
    acc[...] = jnp.zeros_like(acc)

    def norm_back(l, carry):
        at = l * 32 if isinstance(l, int) else pl.multiple_of(l * 32, 32)
        ng = work[pl.ds(at, 32), :].astype(F32)
        xh = xhat[l]
        prod = ng * xh
        acc[9] += jnp.sum(prod.reshape(4, 8, D), axis=0)
        u = ng * gain_row
        mu = jnp.mean(u, axis=-1, keepdims=True)
        mux = jnp.mean(prod * gain_row, axis=-1, keepdims=True)
        gh = cot[l].astype(F32) + rstd[l] * (u - mu - xh * mux)
        normed_w[l] = gh.astype(BF)
        return carry

    halo_g = (normed_w, edges_g, corners_g, rows_in_g, cols_in_g, corner_in_g, halo_gs, halo_gr)
    norm_back(0, 0)
    norm_back(7, 0)
    halo_start((0,), *halo_g)
    lax.fori_loop(1, 7, norm_back, 0, unroll=2)
    fill_edges(normed_w, edges_g, corners_g)
    halo_start((1, 2), *halo_g)

    def tap_sums(l, carry):
        gh = normed_w[l].astype(F32)
        for i in range(3):
            for j in range(3):
                acc[3 * i + j] += jnp.sum((shifted[j, l + i] * gh).reshape(4, 8, D), axis=0)
        return carry

    lax.fori_loop(0, 8, tap_sums, 0, unroll=2)
    for k in range(16):
        if k < 10:
            s0[k] = jnp.sum(acc[k], axis=0, keepdims=True)
        else:
            s0[k] = jnp.zeros((1, D), F32)

    def sums(peer, me, src, dst, slot, whole_src, sends):
        if not sends:
            arrived(dst.at[pl.ds(0, 15)], sum_s.at[slot])
            arrived(dst.at[pl.ds(0, 15)], sum_r.at[slot])
            return

        def step(d, carry):
            k = rem(me + d, 16)
            pltpu.make_async_remote_copy(
                src_ref=src if whole_src else src.at[k], dst_ref=dst.at[me],
                send_sem=sum_s.at[slot], recv_sem=sum_r.at[slot],
                device_id=peer(k), device_id_type=MESH,
            ).start()
            return carry

        lax.fori_loop(1, 16, step, 0, unroll=15)
        dst[me] = src[...] if whole_src else src[me]

    sums(peer_b, me_b, s0, s1, 0, False, True)
    fill_inside(normed_w)

    sums(peer_b, me_b, s0, s1, 0, False, False)
    s2[...] = jnp.sum(s1[...], axis=0)
    sums(peer_a, me_a, s2, s3, 1, True, True)

    gp_arrived(gp4, 3, 2)
    total = gp4[0].astype(F32)
    for i in range(1, 4):
        total = total + gp4[i].astype(F32)
    for i in range(8):
        gp6[i, :, 0:96] = total[:, i * 96 : (i + 1) * 96]
        gp6[i, :, 96:128] = jnp.zeros((24, 32), F32)
    for d in range(1, 8):
        gp_l(d)
    gp7[a] = gp6[a]

    sums(peer_a, me_a, s2, s3, 1, True, False)
    s4[...] = jnp.sum(s3[...], axis=0) * TOTAL_SCALE
    sums(peer_b, me_b, s4, s5, 2, True, True)

    halo_wait(rows_in_g, cols_in_g, corner_in_g, halo_gs, halo_gr)
    fill_rim(rows_in_g, cols_in_g, corner_in_g)

    def grad_row(l, carry):
        grad_v[l] = conv_row(l, True).astype(BF)
        pltpu.make_async_copy(grad_v.at[l], grad_fields.at[l], out_sem.at[l]).start()
        return carry

    lax.fori_loop(0, 8, grad_row, 0, unroll=2)

    gp_arrived(gp7, 7, 3)
    gp_out[...] = (jnp.sum(gp7[...], axis=0) * TOTAL_SCALE)[:, 0:96]
    sums(peer_b, me_b, s4, s5, 2, True, False)
    for k in range(9):
        taps_out[k // 3, k % 3 : k % 3 + 1, :] = s5[k]
    gain_out[...] = s5[9].reshape(D)
    block_copy.wait()
    for l in range(8):
        pltpu.make_async_copy(grad_v.at[l], grad_fields.at[l], out_sem.at[l]).wait()


def hand_over(*refs):
    for k in range(5):
        refs[5 + k][...] = refs[k][...]


def body(
    fields, conv_kernel, layer_norm_gain, qkv_weight, out_weight, score_bias, pattern, cotangent
):
    vm = pl.BlockSpec(memory_space=pltpu.VMEM)
    hbm = pl.BlockSpec(memory_space=pl.ANY)
    dma = pltpu.SemaphoreType.DMA

    def vmem(shape, dtype):
        return pltpu.VMEM(shape, dtype)

    scratch = (
        [vmem((8, 32, D), BF), vmem((8, 32, D), BF), vmem((3, 3, D), F32), vmem((D,), F32), vmem((1, 256), jnp.int32)]
        + [vmem((D, 3 * D), BF), vmem((D, D), BF), vmem((24, 64, 64), F32), vmem((6, 64, 256), F32), dma((8,))]
        + [vmem((4, 1, D), BF)] * 4
        + [vmem((2, 8, D), BF), vmem((2, 8, D), BF)]
        + [vmem((2, 32, D), BF), vmem((2, 8, D), BF)] * 2
        + [dma((3,))] * 4
        + [vmem((3, 10, 32, D), F32), vmem((8, 32, D), BF), vmem((8, 32, D), F32), vmem((8, 32, 1), F32)]
        + [vmem((256, D), BF)] * 2
        + [vmem((8, 32, D), BF)]
        + [vmem((2, 256, 256), BF)] * 2
        + [vmem((256, 256), BF)]
        + [vmem((2, 256, 256), BF)] * 2
        + [vmem((2, 16, 16, D // 2), BF)] * 12
        + [vmem((16, 16, D), BF)] * 4
        + [dma((14,)), dma((14,))]
        + [vmem((256, 3 * D), F32), vmem((8, 32, D), BF), vmem((8, 32, D), BF), dma((9,))]
        + [vmem((6, 4, 64, 256), F32)]
        + [vmem((256, D), BF), vmem((256, D), BF), vmem((256, 3 * D), BF), vmem((256, D), BF), vmem((256, D), BF), vmem((256, 3 * D), BF)]
        + [vmem((4, 4, 2, 24, D), BF)]
        + [vmem((4, 4, 24, D), BF)] * 3
        + [vmem((4, 24, D), BF)] * 2
        + [vmem((8, 24, 128), F32), vmem((8, 24, 128), F32)]
        + [dma((4,)), dma((4,))]
        + [vmem((10, 8, D), F32), vmem((16, 1, D), F32), vmem((16, 1, D), F32), vmem((1, D), F32), vmem((16, 1, D), F32), vmem((1, D), F32), vmem((16, 1, D), F32)]
        + [dma((3,)), dma((3,))]
    )
    results = (
        jax.ShapeDtypeStruct((8, 32, D), BF),
        jax.ShapeDtypeStruct((8, 32, D), BF),
        jax.ShapeDtypeStruct((24, 96), F32),
        jax.ShapeDtypeStruct((3, 3, D), F32),
        jax.ShapeDtypeStruct((D,), F32),
    )
    out = pl.pallas_call(
        kernel,
        out_shape=results,
        in_specs=[hbm] * 8,
        out_specs=(hbm,) * 2 + (vm,) * 3,
        scratch_shapes=scratch,
        name="section",
        compiler_params=pltpu.CompilerParams(
            collective_id=0, has_side_effects=True, vmem_limit_bytes=60 << 20
        ),
    )(
        fields, cotangent, conv_kernel, layer_norm_gain,
        pattern.reshape(1, 256), qkv_weight, out_weight, score_bias,
    )
    block_out, grad_fields, gp, taps, gain = pl.pallas_call(
        hand_over, out_shape=results, in_specs=[vm] * 5, out_specs=(vm,) * 5,
        name="results",
    )(*out)
    return (block_out, grad_fields, jnp.transpose(gp), taps, gain)


def solution(mesh):
    split = P("lat", "lon", None)
    return jax.shard_map(
        body,
        mesh=mesh,
        in_specs=(split, P(), P(), P(), P(), P(), split, split),
        out_specs=(split, split, P("lat", "lon"), P(), P()),
        check_vma=False,
    )
```

```python
import math

import jax
import jax.numpy as jnp
from jax import lax
from jax.experimental import pallas as pl
from jax.experimental.pallas import tpu as pltpu
from jax.sharding import PartitionSpec as P

MESH = pl.DeviceIdType.MESH
BF = jnp.bfloat16
F32 = jnp.float32
D = 768
EPS = 1e-05
HEAD_SCALE = 32 ** (-0.5)
TOTAL_SCALE = 1.0 / math.sqrt(65536)


def nn(a, b):
    return lax.dot_general(a, b, (((1,), (0,)), ((), ())), preferred_element_type=F32)


def nt(a, b):
    return lax.dot_general(a, b, (((1,), (1,)), ((), ())), preferred_element_type=F32)


def tn(a, b):
    return lax.dot_general(a, b, (((0,), (0,)), ((), ())), preferred_element_type=F32)


def div(a, n):
    return lax.div(a, jnp.int32(n))


def rem(a, n):
    return lax.rem(a, jnp.int32(n))


def device(x, y, z, c):
    return (x * 2 + div(z, 4), rem(z, 4) * 8 + y * 2 + c)


def one_hot(cond):
    return jnp.where(cond, 1.0, 0.0).astype(BF)


def iota2(axis):
    return lax.broadcasted_iota(jnp.int32, (256, 256), axis)


def slot_order(s):
    x, zh, zl, y, c = s >> 6, (s >> 5) & 1, (s >> 3) & 3, (s >> 1) & 3, s & 1
    return x * 64 + y * 16 + zh * 8 + zl * 2 + c


def arrival_order(p):
    x, zh, zl, y, c = p >> 6, (p >> 5) & 1, (p >> 3) & 3, (p >> 1) & 3, p & 1
    return zh * 128 + zl * 32 + c * 16 + x * 4 + y


def kernel(
    fields_hbm, cot_hbm, taps_hbm, gain_hbm, pat_hbm, wqkv_hbm, wo_hbm, bias_hbm,
    block_out, grad_fields, gp_out, taps_out, gain_out,
    fields, cot, taps, gain, pat, wqkv, wo, bias, bias_t, w_sem,
    corners, corners_g, corner_in, corner_in_g, edges, edges_g, rows_in, cols_in, rows_in_g, cols_in_g, halo_s, halo_r, halo_gs, halo_gr,
    shifted, hid, xhat, rstd, work, work2, normed_w,
    perm_out, perm_home, perm_swap, perm_pos, perm_arr,
    c0, c1, c2, c3, n0, n1, n2, n3, g0, g1, g2, g3, m0, m1, m2, m3, a2a_s, a2a_r,
    qkv_part, block_v, grad_v, out_sem, probs, cot_g, nrm_g, qkv, grad_att, att, gqkv,
    gp0, gpx, gpa, gp1, gp3, gp4, gp6, gp7, gp_s, gp_r,
    acc, s0, s1, s2, s3, s4, s5, sum_s, sum_r,
):
    a = lax.axis_index("lat")
    b = lax.axis_index("lon")
    x, zh = div(a, 2), rem(a, 2)
    zl, y, c = div(b, 8), rem(div(b, 2), 4), rem(b, 2)
    z = zh * 4 + zl
    me_b = x * 4 + y
    me_a = z * 2 + c

    def peer_b(k):
        return device(div(k, 4), rem(k, 4), z, c)

    def peer_a(k):
        return device(x, y, div(k, 2), rem(k, 2))

    def neighbour(da, db):
        return (rem(a + da + 8, 8), rem(b + db + 32, 32))

    loads = {}
    for i, (name, src, dst) in enumerate(
        (
            ("fields", fields_hbm, fields), ("pat", pat_hbm, pat), ("cot", cot_hbm, cot),
            ("bias", bias_hbm, bias), ("taps", taps_hbm, taps), ("gain", gain_hbm, gain),
            ("wqkv", wqkv_hbm, wqkv), ("wo", wo_hbm, wo),
        )
    ):
        loads[name] = pltpu.make_async_copy(src, dst, w_sem.at[i])
        if i < 3:
            loads[name].start()

    bar = pltpu.get_barrier_semaphore()

    def greet(d, carry):
        pl.semaphore_signal(bar, inc=1, device_id=peer_b(rem(me_b + d, 16)), device_id_type=MESH)
        pl.semaphore_signal(bar, inc=1, device_id=peer_a(rem(me_a + d, 16)), device_id_type=MESH)
        return carry

    offsets = [(-1, 0), (1, 0), (0, -1), (0, 1), (-1, -1), (-1, 1), (1, -1), (1, 1)]
    for da, db in offsets:
        pl.semaphore_signal(bar, inc=1, device_id=neighbour(da, db), device_id_type=MESH)
    for d in range(1, 4):
        pl.semaphore_signal(
            bar, inc=1, device_id=device(rem(x + d, 4), y, rem(z + 4, 8), c), device_id_type=MESH
        )
    lax.fori_loop(1, 16, greet, 0)

    row8 = lax.broadcasted_iota(jnp.int32, (8, D), 0)
    row32 = lax.broadcasted_iota(jnp.int32, (32, D), 0)

    def fill_edges(source, dest, corner):
        left = jnp.zeros((8, D), F32)
        right = jnp.zeros((8, D), F32)
        for l in range(8):
            row = source[l].astype(F32)
            left = jnp.where(row8 == l, row[0:1, :], left)
            right = jnp.where(row8 == l, row[31:32, :], right)
        dest[0] = left.astype(BF)
        dest[1] = right.astype(BF)
        corner[0] = left[0:1].astype(BF)
        corner[1] = right[0:1].astype(BF)
        corner[2] = left[7:8].astype(BF)
        corner[3] = right[7:8].astype(BF)

    def arrived(ref, sem):
        pltpu.make_async_copy(ref, ref, sem).wait()

    def halo_start(kinds, source, edge, corner, rows, cols, corner_to, ss, rs):
        routes = [
            (source.at[0], rows.at[1], 0), (source.at[7], rows.at[0], 0),
            (edge.at[0], cols.at[1], 1), (edge.at[1], cols.at[0], 1),
            (corner.at[0], corner_to.at[3], 2), (corner.at[1], corner_to.at[2], 2),
            (corner.at[2], corner_to.at[1], 2), (corner.at[3], corner_to.at[0], 2),
        ]
        for m, (src, dst, kind) in enumerate(routes):
            if kind not in kinds:
                continue
            pltpu.make_async_remote_copy(
                src_ref=src, dst_ref=dst, send_sem=ss.at[kind], recv_sem=rs.at[kind],
                device_id=neighbour(*offsets[m]), device_id_type=MESH,
            ).start()

    def halo_wait(kinds, rows, cols, corner_to, ss, rs):
        for kind in kinds:
            ref = (rows, cols, corner_to)[kind]
            arrived(ref, ss.at[kind])
            arrived(ref, rs.at[kind])

    top_mask = (a > 0).astype(F32)
    bottom_mask = (a < 7).astype(F32)

    def fill_inside(source):
        for r in range(1, 9):
            f = source[r - 1].astype(F32)
            shifted[0, r] = pltpu.roll(f, 1, 0)
            shifted[1, r] = f
            shifted[2, r] = pltpu.roll(f, 31, 0)

    def fill_rows(rows, corner):
        for r, n, mask in ((0, 0, top_mask), (9, 1, bottom_mask)):
            f = rows[n].astype(F32) * mask
            le = corner[2 * n].astype(F32) * mask
            ri = corner[2 * n + 1].astype(F32) * mask
            shifted[0, r] = jnp.where(row32 == 0, le, pltpu.roll(f, 1, 0))
            shifted[1, r] = f
            shifted[2, r] = jnp.where(row32 == 31, ri, pltpu.roll(f, 31, 0))

    def fill_cols(cols):
        le = cols[0].astype(F32)
        ri = cols[1].astype(F32)
        for r in range(1, 9):
            shifted[0, r, 0:1, :] = le[r - 1 : r, :]
            shifted[2, r, 31:32, :] = ri[r - 1 : r, :]

    def exchange(peer, me, src, dst, slot, sends):
        if not sends:
            arrived(src.at[pl.ds(0, 15)], a2a_s.at[slot])
            arrived(dst.at[pl.ds(0, 15)], a2a_r.at[slot])
            return

        def step(d, carry):
            k = rem(me + d, 16)
            pltpu.make_async_remote_copy(
                src_ref=src.at[k], dst_ref=dst.at[me],
                send_sem=a2a_s.at[slot], recv_sem=a2a_r.at[slot],
                device_id=peer(k), device_id_type=MESH,
            ).start()
            return carry

        lax.fori_loop(1, 16, step, 0, unroll=15)
        dst[me] = src[me]

    def permute(perm, src, dst):
        for n in range(3):
            cols = slice(n * 256, (n + 1) * 256)
            rows = src[..., cols].reshape(256, 256)
            got = nn(perm[...], rows).astype(BF)
            dst[..., cols] = got.reshape(dst.shape[:-1] + (256,))

    def permute_out(perm, src, dst, half):
        rows = src[..., half * 384 : (half + 1) * 384].reshape(256, 384)
        dst[half] = nn(perm[half], rows).astype(BF).reshape(16, 16, 384)

    def permute_mid(src, dst, half):
        dst[half] = nn(perm_swap[...], src[half].reshape(256, 384)).astype(BF).reshape(16, 16, 384)

    def permute_in(perm, src, dst, half):
        got = nn(perm[half], src[half].reshape(256, 384)).astype(BF)
        dst[:, half * 384 : (half + 1) * 384] = got

    loads["fields"].wait()
    fill_edges(fields, edges, corners)
    pl.semaphore_wait(bar, 41)
    halo_start((0, 1, 2), fields, edges, corners, rows_in, cols_in, corner_in, halo_s, halo_r)

    for name in ("bias", "taps", "gain", "wqkv", "wo"):
        loads[name].start()

    loads["pat"].wait()
    pat_hot = one_hot(iota2(0) == pat[...])
    for half, first, second in ((0, slot_order, arrival_order), (1, arrival_order, slot_order)):
        order_hot = one_hot(iota2(0) == first(iota2(1)))
        perm_out[half] = nt(order_hot, pat_hot).astype(BF)
        perm_home[half] = nt(pat_hot, order_hot).astype(BF)
        perm_pos[half] = one_hot(iota2(1) == second(iota2(0)))
        perm_arr[half] = one_hot(iota2(0) == second(iota2(1)))
    perm_swap[...] = one_hot(iota2(1) == (iota2(0) & 15) * 16 + (iota2(0) >> 4))
    first_peer = ((peer_b, me_b), (peer_a, me_a))
    second_peer = ((peer_a, me_a), (peer_b, me_b))

    loads["cot"].wait()
    permute_out(perm_out, cot, c0, 0)
    exchange(*first_peer[0], c0.at[0], c1.at[0], 4, True)
    permute_out(perm_out, cot, c0, 1)

    loads["bias"].wait()
    for q in range(6):
        bias_t[q] = jnp.transpose(bias[4 * q : 4 * q + 4].reshape(256, 64))

    fill_inside(fields)
    loads["taps"].wait()
    loads["gain"].wait()
    gain_row = gain[...].reshape(1, D)
    halo_f = (rows_in, cols_in, corner_in, halo_s, halo_r)
    halo_wait((1,), *halo_f)
    exchange(*first_peer[1], c0.at[1], c1.at[1], 5, True)
    fill_cols(cols_in)

    def conv_row(l, flip):
        out = shifted[1, l + 1]
        for i in range(3):
            for j in range(3):
                ti, tj = (2 - i, 2 - j) if flip else (i, j)
                out = out + taps[ti, tj : tj + 1, :] * shifted[j, l + i]
        return out

    def norm_row(l, carry):
        h = conv_row(l, False).astype(BF)
        hid[l] = h
        hf = h.astype(F32)
        mean = jnp.mean(hf, axis=-1, keepdims=True)
        rem = hf - mean
        var = jnp.mean(rem * rem, axis=-1, keepdims=True)
        inv = lax.rsqrt(var + EPS)
        xh = rem * inv
        xhat[l] = xh
        rstd[l] = inv
        normed_w[l] = (xh * gain_row).astype(BF)
        return carry

    lax.fori_loop(1, 7, norm_row, 0, unroll=2)
    halo_wait((0, 2), *halo_f)
    fill_rows(rows_in, corner_in)
    norm_row(0, 0)
    norm_row(7, 0)
    for h in range(2):
        permute_out(perm_out, normed_w, n0, h)
        exchange(*first_peer[h], n0.at[h], n1.at[h], h, True)
    for h in range(2):
        exchange(*first_peer[h], n0.at[h], n1.at[h], h, False)
        permute_mid(n1, n2, h)
        exchange(*second_peer[h], n2.at[h], n3.at[h], 2 + h, True)
    for h in range(2):
        exchange(*first_peer[h], c0.at[h], c1.at[h], 4 + h, False)
        permute_mid(c1, c2, h)
        exchange(*second_peer[h], c2.at[h], c3.at[h], 6 + h, True)

    exchange(*second_peer[1], n2.at[1], n3.at[1], 3, False)
    permute_in(perm_pos, n3, nrm_g, 1)
    loads["wqkv"].wait()
    for n in range(6):
        cols = slice(n * 384, (n + 1) * 384)
        qkv_part[:, cols] = nn(nrm_g[:, 384:], wqkv[384:, cols])
    exchange(*second_peer[0], n2.at[0], n3.at[0], 2, False)
    permute_in(perm_pos, n3, nrm_g, 0)
    for n in range(6):
        cols = slice(n * 384, (n + 1) * 384)
        qkv[:, cols] = (nn(nrm_g[:, :384], wqkv[:384, cols]) + qkv_part[:, cols]).astype(BF)

    lane_head = lax.broadcasted_iota(jnp.int32, (64, 128), 1) >> 5

    def spread(v):
        vf = v.astype(F32)
        return jnp.concatenate(
            [jnp.where(lane_head == e, vf, 0.0).astype(BF) for e in range(4)], axis=0
        )

    def gather(v):
        out = jnp.zeros((64, 128), F32)
        for e in range(4):
            out = jnp.where(lane_head == e, v[e * 64 : (e + 1) * 64, :], out)
        return out

    def columns(q, part):
        return pl.ds(pl.multiple_of(q * 128 + part * D, 128), 128)

    def attend(q, carry):
        for g in range(4):
            rows = slice(g * 64, (g + 1) * 64)
            q_bd = spread(qkv[rows, columns(q, 0)])
            st = nt(qkv[rows, columns(q, 1)], q_bd) * HEAD_SCALE + bias_t[q]
            e = jnp.exp(st - jnp.max(st, axis=0, keepdims=True))
            p = e * (1.0 / jnp.sum(e, axis=0, keepdims=True))
            probs[q, g] = p
            att[rows, columns(q, 0)] = gather(tn(p.astype(BF), qkv[rows, columns(q, 2)])).astype(BF)
        return carry

    def attend_back(q, carry):
        for g in range(4):
            rows = slice(g * 64, (g + 1) * 64)
            q_bd = spread(qkv[rows, columns(q, 0)])
            g_bd = spread(grad_att[rows, columns(q, 0)])
            p = probs[q, g]
            dp = nt(qkv[rows, columns(q, 2)], g_bd)
            ds = (p * (dp - jnp.sum(p * dp, axis=0, keepdims=True))).astype(BF)
            dq = gather(tn(ds, qkv[rows, columns(q, 1)])) * HEAD_SCALE
            gqkv[rows, columns(q, 0)] = dq.astype(BF)
            gqkv[rows, columns(q, 1)] = (nn(ds, q_bd) * HEAD_SCALE).astype(BF)
            gqkv[rows, columns(q, 2)] = nn(p.astype(BF), g_bd).astype(BF)
        return carry

    lax.fori_loop(0, 6, attend, 0, unroll=2)

    loads["wo"].wait()
    for n in range(3):
        cols = slice(n * 256, (n + 1) * 256)
        work2[:, cols] = nn(att[...], wo[:, cols]).astype(BF)
    permute(perm_arr.at[0], work2, m0)
    exchange(peer_a, me_a, m0, m1, 8, True)

    for h in range(2):
        exchange(*second_peer[h], c2.at[h], c3.at[h], 6 + h, False)
        permute_in(perm_pos, c3, cot_g, h)

    def outer(n, carry):
        cols = pl.ds(pl.multiple_of(n * 384, 128), 384)
        got = tn(cot_g[:, cols], att[...])
        gp0[pl.ds(2 * n, 2)] = got.reshape(2, 4, 2, 24, D).astype(BF)
        return carry

    lax.fori_loop(0, 2, outer, 0)
    core = pltpu.make_async_remote_copy(
        src_ref=gp0.at[:, :, 1 - c], dst_ref=gpx, send_sem=gp_s.at[1], recv_sem=gp_r.at[1],
        device_id=device(x, y, z, 1 - c), device_id_type=MESH,
    )
    core.start()

    def gp_y(d):
        k = rem(y + d, 4)
        pltpu.make_async_remote_copy(
            src_ref=gpa.at[:, k], dst_ref=gp1.at[y], send_sem=gp_s.at[0], recv_sem=gp_r.at[0],
            device_id=device(x, k, z, c), device_id_type=MESH,
        ).start()

    def gp_z(d):
        k = rem(zl + d, 4)
        pltpu.make_async_remote_copy(
            src_ref=gp3.at[k], dst_ref=gp4.at[zl], send_sem=gp_s.at[2], recv_sem=gp_r.at[2],
            device_id=device(x, y, zh * 4 + k, c), device_id_type=MESH,
        ).start()

    def gp_l(d):
        k = rem(a + d, 8)
        pltpu.make_async_remote_copy(
            src_ref=gp6.at[k], dst_ref=gp7.at[a], send_sem=gp_s.at[3], recv_sem=gp_r.at[3],
            device_id=(k, b), device_id_type=MESH,
        ).start()

    def gp_arrived(ref, n, stage):
        arrived(ref.at[pl.ds(0, n)], gp_s.at[stage])
        arrived(ref.at[pl.ds(0, n)], gp_r.at[stage])

    for n in range(3):
        cols = slice(n * 256, (n + 1) * 256)
        grad_att[:, cols] = nt(cot_g[...], wo[cols, :]).astype(BF)

    lax.fori_loop(0, 3, attend_back, 0, unroll=3)
    core.wait()
    for k in range(4):
        gpa[k] = (gp0[k, :, c].astype(F32) + gpx[k].astype(F32)).astype(BF)
    for d in range(1, 4):
        gp_y(d)
    for k in range(4):
        gp1[y, k] = gpa[k, y]
    lax.fori_loop(3, 6, attend_back, 0, unroll=3)

    for half in range(2):
        cols = slice(half * 384, (half + 1) * 384)
        work[:, cols] = nt(gqkv[...], wqkv[cols, :]).astype(BF)
        permute_out(perm_arr, work, g0, half)
        exchange(*second_peer[half], g0.at[half], g1.at[half], 10 + half, True)

    for half in (1, 0):
        exchange(*second_peer[half], g0.at[half], g1.at[half], 10 + half, False)
        permute_mid(g1, g2, half)
        exchange(*first_peer[half], g2.at[half], g3.at[half], 12 + half, True)

    exchange(peer_a, me_a, m0, m1, 8, False)
    permute(perm_swap, m1, m2)
    exchange(peer_b, me_b, m2, m3, 9, True)

    gp_arrived(gp1, 3, 0)
    for k in range(4):
        total = gp1[0, k].astype(F32)
        for i in range(1, 4):
            total = total + gp1[i, k].astype(F32)
        gp3[k] = total.astype(BF)
    for d in range(1, 4):
        gp_z(d)
    gp4[zl] = gp3[zl]

    for half in range(2):
        exchange(*first_peer[half], g2.at[half], g3.at[half], 12 + half, False)
        permute_in(perm_home, g3, work, half)
    acc[...] = jnp.zeros_like(acc)

    def norm_back(l, carry):
        at = l * 32 if isinstance(l, int) else pl.multiple_of(l * 32, 32)
        ng = work[pl.ds(at, 32), :].astype(F32)
        xh = xhat[l]
        prod = ng * xh
        acc[9] += jnp.sum(prod.reshape(4, 8, D), axis=0)
        u = ng * gain_row
        mu = jnp.mean(u, axis=-1, keepdims=True)
        mux = jnp.mean(prod * gain_row, axis=-1, keepdims=True)
        gh = cot[l].astype(F32) + rstd[l] * (u - mu - xh * mux)
        ghb = gh.astype(BF)
        normed_w[l] = ghb
        ghf = ghb.astype(F32)
        for i in range(3):
            for j in range(3):
                acc[3 * i + j] += jnp.sum((shifted[j, l + i] * ghf).reshape(4, 8, D), axis=0)
        return carry

    halo_g = (normed_w, edges_g, corners_g, rows_in_g, cols_in_g, corner_in_g, halo_gs, halo_gr)
    norm_back(0, 0)
    norm_back(7, 0)
    halo_start((0,), *halo_g)
    lax.fori_loop(1, 7, norm_back, 0, unroll=2)
    fill_edges(normed_w, edges_g, corners_g)
    halo_start((1, 2), *halo_g)

    for k in range(16):
        if k < 10:
            s0[k] = jnp.sum(acc[k], axis=0, keepdims=True)
        else:
            s0[k] = jnp.zeros((1, D), F32)

    def sums(peer, me, src, dst, slot, whole_src, sends):
        if not sends:
            arrived(dst.at[pl.ds(0, 15)], sum_s.at[slot])
            arrived(dst.at[pl.ds(0, 15)], sum_r.at[slot])
            return

        def step(d, carry):
            k = rem(me + d, 16)
            pltpu.make_async_remote_copy(
                src_ref=src if whole_src else src.at[k], dst_ref=dst.at[me],
                send_sem=sum_s.at[slot], recv_sem=sum_r.at[slot],
                device_id=peer(k), device_id_type=MESH,
            ).start()
            return carry

        lax.fori_loop(1, 16, step, 0, unroll=15)
        dst[me] = src[...] if whole_src else src[me]

    sums(peer_b, me_b, s0, s1, 0, False, True)
    fill_inside(normed_w)
    exchange(peer_b, me_b, m2, m3, 9, False)
    permute(perm_home.at[0], m3, work2)
    for l in range(8):
        block_v[l] = (hid[l].astype(F32) + work2[l * 32 : (l + 1) * 32, :].astype(F32)).astype(BF)
    block_copy = pltpu.make_async_copy(block_v, block_out, out_sem.at[8])
    block_copy.start()

    sums(peer_b, me_b, s0, s1, 0, False, False)
    s2[...] = jnp.sum(s1[...], axis=0)
    sums(peer_a, me_a, s2, s3, 1, True, True)

    def grad_row(l, carry):
        grad_v[l] = conv_row(l, True).astype(BF)
        pltpu.make_async_copy(grad_v.at[l], grad_fields.at[l], out_sem.at[l]).start()
        return carry

    halo_b = (rows_in_g, cols_in_g, corner_in_g, halo_gs, halo_gr)
    halo_wait((1,), *halo_b)
    fill_cols(cols_in_g)
    lax.fori_loop(1, 7, grad_row, 0, unroll=2)

    gp_arrived(gp4, 3, 2)
    total = gp4[0].astype(F32)
    for i in range(1, 4):
        total = total + gp4[i].astype(F32)
    for i in range(8):
        gp6[i, :, 0:96] = total[:, i * 96 : (i + 1) * 96]
        gp6[i, :, 96:128] = jnp.zeros((24, 32), F32)
    for d in range(1, 8):
        gp_l(d)
    gp7[a] = gp6[a]

    sums(peer_a, me_a, s2, s3, 1, True, False)
    s4[...] = jnp.sum(s3[...], axis=0) * TOTAL_SCALE
    sums(peer_b, me_b, s4, s5, 2, True, True)

    halo_wait((0, 2), *halo_b)
    fill_rows(rows_in_g, corner_in_g)
    grad_row(0, 0)
    grad_row(7, 0)

    gp_arrived(gp7, 7, 3)
    gp_out[...] = (jnp.sum(gp7[...], axis=0) * TOTAL_SCALE)[:, 0:96]
    sums(peer_b, me_b, s4, s5, 2, True, False)
    for k in range(9):
        taps_out[k // 3, k % 3 : k % 3 + 1, :] = s5[k]
    gain_out[...] = s5[9].reshape(D)
    block_copy.wait()
    for l in range(8):
        pltpu.make_async_copy(grad_v.at[l], grad_fields.at[l], out_sem.at[l]).wait()


def hand_over(*refs):
    for k in range(5):
        refs[5 + k][...] = refs[k][...]


def body(
    fields, conv_kernel, layer_norm_gain, qkv_weight, out_weight, score_bias, pattern, cotangent
):
    vm = pl.BlockSpec(memory_space=pltpu.VMEM)
    hbm = pl.BlockSpec(memory_space=pl.ANY)
    dma = pltpu.SemaphoreType.DMA

    def vmem(shape, dtype):
        return pltpu.VMEM(shape, dtype)

    scratch = (
        [vmem((8, 32, D), BF), vmem((8, 32, D), BF), vmem((3, 3, D), F32), vmem((D,), F32), vmem((1, 256), jnp.int32)]
        + [vmem((D, 3 * D), BF), vmem((D, D), BF), vmem((24, 64, 64), F32), vmem((6, 64, 256), F32), dma((8,))]
        + [vmem((4, 1, D), BF)] * 4
        + [vmem((2, 8, D), BF), vmem((2, 8, D), BF)]
        + [vmem((2, 32, D), BF), vmem((2, 8, D), BF)] * 2
        + [dma((3,))] * 4
        + [vmem((3, 10, 32, D), F32), vmem((8, 32, D), BF), vmem((8, 32, D), F32), vmem((8, 32, 1), F32)]
        + [vmem((256, D), BF)] * 2
        + [vmem((8, 32, D), BF)]
        + [vmem((2, 256, 256), BF)] * 2
        + [vmem((256, 256), BF)]
        + [vmem((2, 256, 256), BF)] * 2
        + [vmem((2, 16, 16, D // 2), BF)] * 12
        + [vmem((16, 16, D), BF)] * 4
        + [dma((14,)), dma((14,))]
        + [vmem((256, 3 * D), F32), vmem((8, 32, D), BF), vmem((8, 32, D), BF), dma((9,))]
        + [vmem((6, 4, 64, 256), F32)]
        + [vmem((256, D), BF), vmem((256, D), BF), vmem((256, 3 * D), BF), vmem((256, D), BF), vmem((256, D), BF), vmem((256, 3 * D), BF)]
        + [vmem((4, 4, 2, 24, D), BF)]
        + [vmem((4, 4, 24, D), BF)] * 3
        + [vmem((4, 24, D), BF)] * 2
        + [vmem((8, 24, 128), F32), vmem((8, 24, 128), F32)]
        + [dma((4,)), dma((4,))]
        + [vmem((10, 8, D), F32), vmem((16, 1, D), F32), vmem((16, 1, D), F32), vmem((1, D), F32), vmem((16, 1, D), F32), vmem((1, D), F32), vmem((16, 1, D), F32)]
        + [dma((3,)), dma((3,))]
    )
    results = (
        jax.ShapeDtypeStruct((8, 32, D), BF),
        jax.ShapeDtypeStruct((8, 32, D), BF),
        jax.ShapeDtypeStruct((24, 96), F32),
        jax.ShapeDtypeStruct((3, 3, D), F32),
        jax.ShapeDtypeStruct((D,), F32),
    )
    out = pl.pallas_call(
        kernel,
        out_shape=results,
        in_specs=[hbm] * 8,
        out_specs=(hbm,) * 2 + (vm,) * 3,
        scratch_shapes=scratch,
        name="section",
        compiler_params=pltpu.CompilerParams(
            collective_id=0, has_side_effects=True, vmem_limit_bytes=60 << 20
        ),
    )(
        fields, cotangent, conv_kernel, layer_norm_gain,
        pattern.reshape(1, 256), qkv_weight, out_weight, score_bias,
    )
    block_out, grad_fields, gp, taps, gain = pl.pallas_call(
        hand_over, out_shape=results, in_specs=[vm] * 5, out_specs=(vm,) * 5,
        name="results",
    )(*out)
    return (block_out, grad_fields, jnp.transpose(gp), taps, gain)


def solution(mesh):
    split = P("lat", "lon", None)
    return jax.shard_map(
        body,
        mesh=mesh,
        in_specs=(split, P(), P(), P(), P(), P(), split, split),
        out_specs=(split, split, P("lat", "lon"), P(), P()),
        check_vma=False,
    )
```

```python
import math

import jax
import jax.numpy as jnp
from jax import lax
from jax.experimental import pallas as pl
from jax.experimental.pallas import tpu as pltpu
from jax.sharding import PartitionSpec as P

MESH = pl.DeviceIdType.MESH
BF = jnp.bfloat16
F32 = jnp.float32
D = 768
EPS = 1e-05
HEAD_SCALE = 32 ** (-0.5)
TOTAL_SCALE = 1.0 / math.sqrt(65536)


def nn(a, b):
    return lax.dot_general(a, b, (((1,), (0,)), ((), ())), preferred_element_type=F32)


def nt(a, b):
    return lax.dot_general(a, b, (((1,), (1,)), ((), ())), preferred_element_type=F32)


def tn(a, b):
    return lax.dot_general(a, b, (((0,), (0,)), ((), ())), preferred_element_type=F32)


def div(a, n):
    return lax.div(a, jnp.int32(n))


def rem(a, n):
    return lax.rem(a, jnp.int32(n))


def device(x, y, z, c):
    return (x * 2 + div(z, 4), rem(z, 4) * 8 + y * 2 + c)


def one_hot(cond):
    return jnp.where(cond, 1.0, 0.0).astype(BF)


def iota2(axis):
    return lax.broadcasted_iota(jnp.int32, (256, 256), axis)


def slot_order(s):
    x, zh, zl, y, c = s >> 6, (s >> 5) & 1, (s >> 3) & 3, (s >> 1) & 3, s & 1
    return x * 64 + y * 16 + zh * 8 + zl * 2 + c


def arrival_order(p):
    x, zh, zl, y, c = p >> 6, (p >> 5) & 1, (p >> 3) & 3, (p >> 1) & 3, p & 1
    return zh * 128 + zl * 32 + c * 16 + x * 4 + y


def kernel(
    fields_hbm, cot_hbm, taps_hbm, gain_hbm, pat_hbm, wqkv_hbm, wo_hbm, bias_hbm,
    block_out, grad_fields, gp_out, taps_out, gain_out,
    fields, cot, taps, gain, pat, wqkv, wo, bias, bias_t, w_sem,
    corners, corners_g, corner_in, corner_in_g, edges, edges_g, rows_in, cols_in, rows_in_g, cols_in_g, halo_s, halo_r, halo_gs, halo_gr,
    shifted, hid, xhat, rstd, work, work2, normed_w,
    perm_out, perm_home, perm_swap, perm_pos, perm_arr,
    c0, c1, c2, c3, n0, n1, n2, n3, g0, g1, g2, g3, m0, m1, m2, m3, a2a_s, a2a_r,
    qkv_part, block_v, grad_v, out_sem, probs, cot_g, nrm_g, qkv, grad_att, att, gqkv,
    gp0, gpx, gpa, gp1, gp3, gp4, gp6, gp7, gp_s, gp_r,
    acc, s0, s1, s2, s3, s4, s5, sum_s, sum_r,
):
    a = lax.axis_index("lat")
    b = lax.axis_index("lon")
    x, zh = div(a, 2), rem(a, 2)
    zl, y, c = div(b, 8), rem(div(b, 2), 4), rem(b, 2)
    z = zh * 4 + zl
    me_b = x * 4 + y
    me_a = z * 2 + c

    def peer_b(k):
        return device(div(k, 4), rem(k, 4), z, c)

    def peer_a(k):
        return device(x, y, div(k, 2), rem(k, 2))

    def neighbour(da, db):
        return (rem(a + da + 8, 8), rem(b + db + 32, 32))

    loads = {}
    for i, (name, src, dst) in enumerate(
        (
            ("fields", fields_hbm, fields), ("pat", pat_hbm, pat), ("cot", cot_hbm, cot),
            ("bias", bias_hbm, bias), ("taps", taps_hbm, taps), ("gain", gain_hbm, gain),
            ("wqkv", wqkv_hbm, wqkv), ("wo", wo_hbm, wo),
        )
    ):
        loads[name] = pltpu.make_async_copy(src, dst, w_sem.at[i])
        if i < 3:
            loads[name].start()

    bar = pltpu.get_barrier_semaphore()

    def greet(d, carry):
        pl.semaphore_signal(bar, inc=1, device_id=peer_b(rem(me_b + d, 16)), device_id_type=MESH)
        pl.semaphore_signal(bar, inc=1, device_id=peer_a(rem(me_a + d, 16)), device_id_type=MESH)
        return carry

    offsets = [(-1, 0), (1, 0), (0, -1), (0, 1), (-1, -1), (-1, 1), (1, -1), (1, 1)]
    for da, db in offsets:
        pl.semaphore_signal(bar, inc=1, device_id=neighbour(da, db), device_id_type=MESH)
    for d in range(1, 4):
        pl.semaphore_signal(
            bar, inc=1, device_id=device(rem(x + d, 4), y, rem(z + 4, 8), c), device_id_type=MESH
        )
    lax.fori_loop(1, 16, greet, 0, unroll=15)

    row8 = lax.broadcasted_iota(jnp.int32, (8, D), 0)
    row32 = lax.broadcasted_iota(jnp.int32, (32, D), 0)

    def fill_edges(source, dest, corner):
        left = jnp.zeros((8, D), F32)
        right = jnp.zeros((8, D), F32)
        for l in range(8):
            row = source[l].astype(F32)
            left = jnp.where(row8 == l, row[0:1, :], left)
            right = jnp.where(row8 == l, row[31:32, :], right)
        dest[0] = left.astype(BF)
        dest[1] = right.astype(BF)
        corner[0] = left[0:1].astype(BF)
        corner[1] = right[0:1].astype(BF)
        corner[2] = left[7:8].astype(BF)
        corner[3] = right[7:8].astype(BF)

    def arrived(ref, sem):
        pltpu.make_async_copy(ref, ref, sem).wait()

    def halo_start(kinds, source, edge, corner, rows, cols, corner_to, ss, rs):
        routes = [
            (source.at[0], rows.at[1], 0), (source.at[7], rows.at[0], 0),
            (edge.at[0], cols.at[1], 1), (edge.at[1], cols.at[0], 1),
            (corner.at[0], corner_to.at[3], 2), (corner.at[1], corner_to.at[2], 2),
            (corner.at[2], corner_to.at[1], 2), (corner.at[3], corner_to.at[0], 2),
        ]
        for m, (src, dst, kind) in enumerate(routes):
            if kind not in kinds:
                continue
            pltpu.make_async_remote_copy(
                src_ref=src, dst_ref=dst, send_sem=ss.at[kind], recv_sem=rs.at[kind],
                device_id=neighbour(*offsets[m]), device_id_type=MESH,
            ).start()

    def halo_wait(kinds, rows, cols, corner_to, ss, rs):
        for kind in kinds:
            ref = (rows, cols, corner_to)[kind]
            arrived(ref, ss.at[kind])
            arrived(ref, rs.at[kind])

    top_mask = (a > 0).astype(F32)
    bottom_mask = (a < 7).astype(F32)

    def fill_inside(source):
        for r in range(1, 9):
            f = source[r - 1].astype(F32)
            shifted[0, r] = pltpu.roll(f, 1, 0)
            shifted[1, r] = f
            shifted[2, r] = pltpu.roll(f, 31, 0)

    def fill_rows(rows, corner):
        for r, n, mask in ((0, 0, top_mask), (9, 1, bottom_mask)):
            f = rows[n].astype(F32) * mask
            le = corner[2 * n].astype(F32) * mask
            ri = corner[2 * n + 1].astype(F32) * mask
            shifted[0, r] = jnp.where(row32 == 0, le, pltpu.roll(f, 1, 0))
            shifted[1, r] = f
            shifted[2, r] = jnp.where(row32 == 31, ri, pltpu.roll(f, 31, 0))

    def fill_cols(cols):
        le = cols[0].astype(F32)
        ri = cols[1].astype(F32)
        for r in range(1, 9):
            shifted[0, r, 0:1, :] = le[r - 1 : r, :]
            shifted[2, r, 31:32, :] = ri[r - 1 : r, :]

    def exchange(peer, me, src, dst, slot, sends):
        if not sends:
            arrived(src.at[pl.ds(0, 15)], a2a_s.at[slot])
            arrived(dst.at[pl.ds(0, 15)], a2a_r.at[slot])
            return

        def step(d, carry):
            k = rem(me + d, 16)
            pltpu.make_async_remote_copy(
                src_ref=src.at[k], dst_ref=dst.at[me],
                send_sem=a2a_s.at[slot], recv_sem=a2a_r.at[slot],
                device_id=peer(k), device_id_type=MESH,
            ).start()
            return carry

        lax.fori_loop(1, 16, step, 0, unroll=15)
        dst[me] = src[me]

    def permute(perm, src, dst):
        for n in range(3):
            cols = slice(n * 256, (n + 1) * 256)
            rows = src[..., cols].reshape(256, 256)
            got = nn(perm[...], rows).astype(BF)
            dst[..., cols] = got.reshape(dst.shape[:-1] + (256,))

    def permute_out(perm, src, dst, half):
        rows = src[..., half * 384 : (half + 1) * 384].reshape(256, 384)
        dst[half] = nn(perm[half], rows).astype(BF).reshape(16, 16, 384)

    def permute_mid(src, dst, half):
        dst[half] = nn(perm_swap[...], src[half].reshape(256, 384)).astype(BF).reshape(16, 16, 384)

    def permute_in(perm, src, dst, half):
        got = nn(perm[half], src[half].reshape(256, 384)).astype(BF)
        dst[:, half * 384 : (half + 1) * 384] = got

    loads["fields"].wait()
    fill_edges(fields, edges, corners)
    pl.semaphore_wait(bar, 41)
    halo_start((0, 1, 2), fields, edges, corners, rows_in, cols_in, corner_in, halo_s, halo_r)

    for name in ("bias", "taps", "gain", "wqkv", "wo"):
        loads[name].start()

    loads["pat"].wait()
    pat_hot = one_hot(iota2(0) == pat[...])
    for half, first, second in ((0, slot_order, arrival_order), (1, arrival_order, slot_order)):
        order_hot = one_hot(iota2(0) == first(iota2(1)))
        perm_out[half] = nt(order_hot, pat_hot).astype(BF)
        perm_home[half] = nt(pat_hot, order_hot).astype(BF)
        perm_pos[half] = one_hot(iota2(1) == second(iota2(0)))
        perm_arr[half] = one_hot(iota2(0) == second(iota2(1)))
    perm_swap[...] = one_hot(iota2(1) == (iota2(0) & 15) * 16 + (iota2(0) >> 4))
    first_peer = ((peer_b, me_b), (peer_a, me_a))
    second_peer = ((peer_a, me_a), (peer_b, me_b))

    loads["cot"].wait()
    permute_out(perm_out, cot, c0, 0)
    exchange(*first_peer[0], c0.at[0], c1.at[0], 4, True)
    permute_out(perm_out, cot, c0, 1)
    exchange(*first_peer[1], c0.at[1], c1.at[1], 5, True)

    loads["bias"].wait()
    for q in range(6):
        bias_t[q] = jnp.transpose(bias[4 * q : 4 * q + 4].reshape(256, 64))

    fill_inside(fields)
    loads["taps"].wait()
    loads["gain"].wait()
    gain_row = gain[...].reshape(1, D)
    halo_f = (rows_in, cols_in, corner_in, halo_s, halo_r)
    halo_wait((1,), *halo_f)
    fill_cols(cols_in)

    def conv_row(l, flip):
        out = shifted[1, l + 1]
        for i in range(3):
            for j in range(3):
                ti, tj = (2 - i, 2 - j) if flip else (i, j)
                out = out + taps[ti, tj : tj + 1, :] * shifted[j, l + i]
        return out

    def norm_row(l, carry):
        h = conv_row(l, False).astype(BF)
        hid[l] = h
        hf = h.astype(F32)
        mean = jnp.mean(hf, axis=-1, keepdims=True)
        rem = hf - mean
        var = jnp.mean(rem * rem, axis=-1, keepdims=True)
        inv = lax.rsqrt(var + EPS)
        xh = rem * inv
        xhat[l] = xh
        rstd[l] = inv
        normed_w[l] = (xh * gain_row).astype(BF)
        return carry

    lax.fori_loop(1, 7, norm_row, 0, unroll=2)
    halo_wait((0, 2), *halo_f)
    fill_rows(rows_in, corner_in)
    norm_row(0, 0)
    norm_row(7, 0)
    for h in range(2):
        permute_out(perm_out, normed_w, n0, h)
        exchange(*first_peer[h], n0.at[h], n1.at[h], h, True)
    for h in range(2):
        exchange(*first_peer[h], n0.at[h], n1.at[h], h, False)
        permute_mid(n1, n2, h)
        exchange(*second_peer[h], n2.at[h], n3.at[h], 2 + h, True)
    for h in range(2):
        exchange(*first_peer[h], c0.at[h], c1.at[h], 4 + h, False)
        permute_mid(c1, c2, h)
        exchange(*second_peer[h], c2.at[h], c3.at[h], 6 + h, True)

    exchange(*second_peer[1], n2.at[1], n3.at[1], 3, False)
    permute_in(perm_pos, n3, nrm_g, 1)
    loads["wqkv"].wait()
    for n in range(6):
        cols = slice(n * 384, (n + 1) * 384)
        qkv_part[:, cols] = nn(nrm_g[:, 384:], wqkv[384:, cols])
    exchange(*second_peer[0], n2.at[0], n3.at[0], 2, False)
    permute_in(perm_pos, n3, nrm_g, 0)
    for n in range(6):
        cols = slice(n * 384, (n + 1) * 384)
        qkv[:, cols] = (nn(nrm_g[:, :384], wqkv[:384, cols]) + qkv_part[:, cols]).astype(BF)

    lane_head = lax.broadcasted_iota(jnp.int32, (64, 128), 1) >> 5

    own_head = [one_hot(lane_head == e) for e in range(4)]

    def spread(v):
        return jnp.concatenate([v * own_head[e] for e in range(4)], axis=0)

    def gather(v):
        out = jnp.zeros((64, 128), F32)
        for e in range(4):
            out = jnp.where(lane_head == e, v[e * 64 : (e + 1) * 64, :], out)
        return out

    def columns(q, part):
        return pl.ds(pl.multiple_of(q * 128 + part * D, 128), 128)

    def attend(q, carry):
        for g in range(4):
            rows = slice(g * 64, (g + 1) * 64)
            q_bd = spread(qkv[rows, columns(q, 0)])
            st = nt(qkv[rows, columns(q, 1)], q_bd) * HEAD_SCALE + bias_t[q]
            e = jnp.exp(st - jnp.max(st, axis=0, keepdims=True))
            p = e * (1.0 / jnp.sum(e, axis=0, keepdims=True))
            probs[q, g] = p
            att[rows, columns(q, 0)] = gather(tn(p.astype(BF), qkv[rows, columns(q, 2)])).astype(BF)
        return carry

    def attend_back(q, carry):
        for g in range(4):
            rows = slice(g * 64, (g + 1) * 64)
            q_bd = spread(qkv[rows, columns(q, 0)])
            g_bd = spread(grad_att[rows, columns(q, 0)])
            p = probs[q, g]
            dp = nt(qkv[rows, columns(q, 2)], g_bd)
            ds = (p * (dp - jnp.sum(p * dp, axis=0, keepdims=True))).astype(BF)
            dq = gather(tn(ds, qkv[rows, columns(q, 1)])) * HEAD_SCALE
            gqkv[rows, columns(q, 0)] = dq.astype(BF)
            gqkv[rows, columns(q, 1)] = (nn(ds, q_bd) * HEAD_SCALE).astype(BF)
            gqkv[rows, columns(q, 2)] = nn(p.astype(BF), g_bd).astype(BF)
        return carry

    lax.fori_loop(0, 6, attend, 0, unroll=2)

    loads["wo"].wait()
    for n in range(3):
        cols = slice(n * 256, (n + 1) * 256)
        work2[:, cols] = nn(att[...], wo[:, cols]).astype(BF)
    permute(perm_arr.at[0], work2, m0)
    exchange(peer_a, me_a, m0, m1, 8, True)

    for h in range(2):
        exchange(*second_peer[h], c2.at[h], c3.at[h], 6 + h, False)
        permute_in(perm_pos, c3, cot_g, h)

    def outer(n, carry):
        cols = pl.ds(pl.multiple_of(n * 384, 128), 384)
        got = tn(cot_g[:, cols], att[...])
        gp0[pl.ds(2 * n, 2)] = got.reshape(2, 4, 2, 24, D).astype(BF)
        return carry

    lax.fori_loop(0, 2, outer, 0)
    core = pltpu.make_async_remote_copy(
        src_ref=gp0.at[:, :, 1 - c], dst_ref=gpx, send_sem=gp_s.at[1], recv_sem=gp_r.at[1],
        device_id=device(x, y, z, 1 - c), device_id_type=MESH,
    )
    core.start()

    def gp_y(d):
        k = rem(y + d, 4)
        pltpu.make_async_remote_copy(
            src_ref=gpa.at[:, k], dst_ref=gp1.at[y], send_sem=gp_s.at[0], recv_sem=gp_r.at[0],
            device_id=device(x, k, z, c), device_id_type=MESH,
        ).start()

    def gp_z(d):
        k = rem(zl + d, 4)
        pltpu.make_async_remote_copy(
            src_ref=gp3.at[k], dst_ref=gp4.at[zl], send_sem=gp_s.at[2], recv_sem=gp_r.at[2],
            device_id=device(x, y, zh * 4 + k, c), device_id_type=MESH,
        ).start()

    def gp_l(d):
        k = rem(a + d, 8)
        pltpu.make_async_remote_copy(
            src_ref=gp6.at[k], dst_ref=gp7.at[a], send_sem=gp_s.at[3], recv_sem=gp_r.at[3],
            device_id=(k, b), device_id_type=MESH,
        ).start()

    def gp_arrived(ref, n, stage):
        arrived(ref.at[pl.ds(0, n)], gp_s.at[stage])
        arrived(ref.at[pl.ds(0, n)], gp_r.at[stage])

    for n in range(3):
        cols = slice(n * 256, (n + 1) * 256)
        grad_att[:, cols] = nt(cot_g[...], wo[cols, :]).astype(BF)

    lax.fori_loop(0, 3, attend_back, 0, unroll=3)
    core.wait()
    for k in range(4):
        gpa[k] = (gp0[k, :, c].astype(F32) + gpx[k].astype(F32)).astype(BF)
    for d in range(1, 4):
        gp_y(d)
    for k in range(4):
        gp1[y, k] = gpa[k, y]
    lax.fori_loop(3, 6, attend_back, 0, unroll=3)

    for half in range(2):
        cols = slice(half * 384, (half + 1) * 384)
        work[:, cols] = nt(gqkv[...], wqkv[cols, :]).astype(BF)
        permute_out(perm_arr, work, g0, half)
        exchange(*second_peer[half], g0.at[half], g1.at[half], 10 + half, True)

    for half in (1, 0):
        exchange(*second_peer[half], g0.at[half], g1.at[half], 10 + half, False)
        permute_mid(g1, g2, half)
        exchange(*first_peer[half], g2.at[half], g3.at[half], 12 + half, True)

    exchange(peer_a, me_a, m0, m1, 8, False)
    permute(perm_swap, m1, m2)
    exchange(peer_b, me_b, m2, m3, 9, True)

    gp_arrived(gp1, 3, 0)
    for k in range(4):
        total = gp1[0, k].astype(F32)
        for i in range(1, 4):
            total = total + gp1[i, k].astype(F32)
        gp3[k] = total.astype(BF)
    for d in range(1, 4):
        gp_z(d)
    gp4[zl] = gp3[zl]

    for half in range(2):
        exchange(*first_peer[half], g2.at[half], g3.at[half], 12 + half, False)
        permute_in(perm_home, g3, work, half)
    acc[...] = jnp.zeros_like(acc)

    def norm_back(l, carry):
        at = l * 32 if isinstance(l, int) else pl.multiple_of(l * 32, 32)
        ng = work[pl.ds(at, 32), :].astype(F32)
        xh = xhat[l]
        prod = ng * xh
        acc[9] += jnp.sum(prod.reshape(4, 8, D), axis=0)
        u = ng * gain_row
        mu = jnp.mean(u, axis=-1, keepdims=True)
        mux = jnp.mean(prod * gain_row, axis=-1, keepdims=True)
        gh = cot[l].astype(F32) + rstd[l] * (u - mu - xh * mux)
        ghb = gh.astype(BF)
        normed_w[l] = ghb
        ghf = ghb.astype(F32)
        for i in range(3):
            for j in range(3):
                acc[3 * i + j] += jnp.sum((shifted[j, l + i] * ghf).reshape(4, 8, D), axis=0)
        return carry

    halo_g = (normed_w, edges_g, corners_g, rows_in_g, cols_in_g, corner_in_g, halo_gs, halo_gr)
    norm_back(0, 0)
    norm_back(7, 0)
    halo_start((0,), *halo_g)
    lax.fori_loop(1, 7, norm_back, 0, unroll=2)
    fill_edges(normed_w, edges_g, corners_g)
    halo_start((1, 2), *halo_g)

    for k in range(16):
        if k < 10:
            s0[k] = jnp.sum(acc[k], axis=0, keepdims=True)
        else:
            s0[k] = jnp.zeros((1, D), F32)

    def sums(peer, me, src, dst, slot, whole_src, sends):
        if not sends:
            arrived(dst.at[pl.ds(0, 15)], sum_s.at[slot])
            arrived(dst.at[pl.ds(0, 15)], sum_r.at[slot])
            return

        def step(d, carry):
            k = rem(me + d, 16)
            pltpu.make_async_remote_copy(
                src_ref=src if whole_src else src.at[k], dst_ref=dst.at[me],
                send_sem=sum_s.at[slot], recv_sem=sum_r.at[slot],
                device_id=peer(k), device_id_type=MESH,
            ).start()
            return carry

        lax.fori_loop(1, 16, step, 0, unroll=15)
        dst[me] = src[...] if whole_src else src[me]

    sums(peer_b, me_b, s0, s1, 0, False, True)
    fill_inside(normed_w)
    exchange(peer_b, me_b, m2, m3, 9, False)
    permute(perm_home.at[0], m3, work2)
    for l in range(8):
        block_v[l] = (hid[l].astype(F32) + work2[l * 32 : (l + 1) * 32, :].astype(F32)).astype(BF)
    block_copy = pltpu.make_async_copy(block_v, block_out, out_sem.at[8])
    block_copy.start()

    sums(peer_b, me_b, s0, s1, 0, False, False)
    s2[...] = jnp.sum(s1[...], axis=0)
    sums(peer_a, me_a, s2, s3, 1, True, True)

    def grad_row(l, carry):
        grad_v[l] = conv_row(l, True).astype(BF)
        pltpu.make_async_copy(grad_v.at[l], grad_fields.at[l], out_sem.at[l]).start()
        return carry

    halo_b = (rows_in_g, cols_in_g, corner_in_g, halo_gs, halo_gr)
    halo_wait((1,), *halo_b)
    fill_cols(cols_in_g)
    lax.fori_loop(1, 7, grad_row, 0, unroll=2)

    gp_arrived(gp4, 3, 2)
    total = gp4[0].astype(F32)
    for i in range(1, 4):
        total = total + gp4[i].astype(F32)
    for i in range(8):
        gp6[i, :, 0:96] = total[:, i * 96 : (i + 1) * 96]
        gp6[i, :, 96:128] = jnp.zeros((24, 32), F32)
    for d in range(1, 8):
        gp_l(d)
    gp7[a] = gp6[a]

    sums(peer_a, me_a, s2, s3, 1, True, False)
    s4[...] = jnp.sum(s3[...], axis=0) * TOTAL_SCALE
    sums(peer_b, me_b, s4, s5, 2, True, True)

    halo_wait((0, 2), *halo_b)
    fill_rows(rows_in_g, corner_in_g)
    grad_row(0, 0)
    grad_row(7, 0)

    gp_arrived(gp7, 7, 3)
    gp_out[...] = (jnp.sum(gp7[...], axis=0) * TOTAL_SCALE)[:, 0:96]
    sums(peer_b, me_b, s4, s5, 2, True, False)
    for k in range(9):
        taps_out[k // 3, k % 3 : k % 3 + 1, :] = s5[k]
    gain_out[...] = s5[9].reshape(D)
    block_copy.wait()
    for l in range(8):
        pltpu.make_async_copy(grad_v.at[l], grad_fields.at[l], out_sem.at[l]).wait()


def hand_over(*refs):
    for k in range(5):
        refs[5 + k][...] = refs[k][...]


def body(
    fields, conv_kernel, layer_norm_gain, qkv_weight, out_weight, score_bias, pattern, cotangent
):
    vm = pl.BlockSpec(memory_space=pltpu.VMEM)
    hbm = pl.BlockSpec(memory_space=pl.ANY)
    dma = pltpu.SemaphoreType.DMA

    def vmem(shape, dtype):
        return pltpu.VMEM(shape, dtype)

    scratch = (
        [vmem((8, 32, D), BF), vmem((8, 32, D), BF), vmem((3, 3, D), F32), vmem((D,), F32), vmem((1, 256), jnp.int32)]
        + [vmem((D, 3 * D), BF), vmem((D, D), BF), vmem((24, 64, 64), F32), vmem((6, 64, 256), F32), dma((8,))]
        + [vmem((4, 1, D), BF)] * 4
        + [vmem((2, 8, D), BF), vmem((2, 8, D), BF)]
        + [vmem((2, 32, D), BF), vmem((2, 8, D), BF)] * 2
        + [dma((3,))] * 4
        + [vmem((3, 10, 32, D), F32), vmem((8, 32, D), BF), vmem((8, 32, D), F32), vmem((8, 32, 1), F32)]
        + [vmem((256, D), BF)] * 2
        + [vmem((8, 32, D), BF)]
        + [vmem((2, 256, 256), BF)] * 2
        + [vmem((256, 256), BF)]
        + [vmem((2, 256, 256), BF)] * 2
        + [vmem((2, 16, 16, D // 2), BF)] * 12
        + [vmem((16, 16, D), BF)] * 4
        + [dma((14,)), dma((14,))]
        + [vmem((256, 3 * D), F32), vmem((8, 32, D), BF), vmem((8, 32, D), BF), dma((9,))]
        + [vmem((6, 4, 64, 256), F32)]
        + [vmem((256, D), BF), vmem((256, D), BF), vmem((256, 3 * D), BF), vmem((256, D), BF), vmem((256, D), BF), vmem((256, 3 * D), BF)]
        + [vmem((4, 4, 2, 24, D), BF)]
        + [vmem((4, 4, 24, D), BF)] * 3
        + [vmem((4, 24, D), BF)] * 2
        + [vmem((8, 24, 128), F32), vmem((8, 24, 128), F32)]
        + [dma((4,)), dma((4,))]
        + [vmem((10, 8, D), F32), vmem((16, 1, D), F32), vmem((16, 1, D), F32), vmem((1, D), F32), vmem((16, 1, D), F32), vmem((1, D), F32), vmem((16, 1, D), F32)]
        + [dma((3,)), dma((3,))]
    )
    results = (
        jax.ShapeDtypeStruct((8, 32, D), BF),
        jax.ShapeDtypeStruct((8, 32, D), BF),
        jax.ShapeDtypeStruct((24, 96), F32),
        jax.ShapeDtypeStruct((3, 3, D), F32),
        jax.ShapeDtypeStruct((D,), F32),
    )
    out = pl.pallas_call(
        kernel,
        out_shape=results,
        in_specs=[hbm] * 8,
        out_specs=(hbm,) * 2 + (vm,) * 3,
        scratch_shapes=scratch,
        name="section",
        compiler_params=pltpu.CompilerParams(
            collective_id=0, has_side_effects=True, vmem_limit_bytes=60 << 20
        ),
    )(
        fields, cotangent, conv_kernel, layer_norm_gain,
        pattern.reshape(1, 256), qkv_weight, out_weight, score_bias,
    )
    block_out, grad_fields, gp, taps, gain = pl.pallas_call(
        hand_over, out_shape=results, in_specs=[vm] * 5, out_specs=(vm,) * 5,
        name="results",
    )(*out)
    return (block_out, grad_fields, jnp.transpose(gp), taps, gain)


def solution(mesh):
    split = P("lat", "lon", None)
    return jax.shard_map(
        body,
        mesh=mesh,
        in_specs=(split, P(), P(), P(), P(), P(), split, split),
        out_specs=(split, split, P("lat", "lon"), P(), P()),
        check_vma=False,
    )
```

```python
import math

import jax
import jax.numpy as jnp
from jax import lax
from jax.experimental import pallas as pl
from jax.experimental.pallas import tpu as pltpu
from jax.sharding import PartitionSpec as P

MESH = pl.DeviceIdType.MESH
BF = jnp.bfloat16
F32 = jnp.float32
D = 768
EPS = 1e-05
HEAD_SCALE = 32 ** (-0.5)
TOTAL_SCALE = 1.0 / math.sqrt(65536)


def nn(a, b):
    return lax.dot_general(a, b, (((1,), (0,)), ((), ())), preferred_element_type=F32)


def nt(a, b):
    return lax.dot_general(a, b, (((1,), (1,)), ((), ())), preferred_element_type=F32)


def tn(a, b):
    return lax.dot_general(a, b, (((0,), (0,)), ((), ())), preferred_element_type=F32)


def div(a, n):
    return lax.div(a, jnp.int32(n))


def rem(a, n):
    return lax.rem(a, jnp.int32(n))


def device(x, y, z, c):
    return (x * 2 + div(z, 4), rem(z, 4) * 8 + y * 2 + c)


def one_hot(cond):
    return jnp.where(cond, 1.0, 0.0).astype(BF)


def iota2(axis):
    return lax.broadcasted_iota(jnp.int32, (256, 256), axis)


def slot_order(s):
    x, zh, zl, y, c = s >> 6, (s >> 5) & 1, (s >> 3) & 3, (s >> 1) & 3, s & 1
    return x * 64 + y * 16 + zh * 8 + zl * 2 + c


def arrival_order(p):
    x, zh, zl, y, c = p >> 6, (p >> 5) & 1, (p >> 3) & 3, (p >> 1) & 3, p & 1
    return zh * 128 + zl * 32 + c * 16 + x * 4 + y


def kernel(
    fields_hbm, cot_hbm, taps_hbm, gain_hbm, pat_hbm, wqkv_hbm, wo_hbm, bias_hbm,
    block_out, grad_fields, gp_out, taps_out, gain_out,
    fields, cot, taps, gain, pat, wqkv, wo, bias, bias_t, w_sem,
    corners, corners_g, corner_in, corner_in_g, edges, edges_g, rows_in, cols_in, rows_in_g, cols_in_g, halo_s, halo_r, halo_gs, halo_gr,
    shifted, hid, xhat, rstd, work, work2, normed_w,
    perm_out, perm_home, perm_swap, perm_pos, perm_arr,
    c0, c1, c2, c3, n0, n1, n2, n3, g0, g1, g2, g3, m0, m1, m2, m3, a2a_s, a2a_r,
    qkv_part, block_v, grad_v, out_sem, probs, cot_g, nrm_g, qkv, grad_att, att, gqkv,
    gp0, gpx, gpa, gp1, gp3, gp4, gp6, gp7, gp_s, gp_r,
    acc, s0, s1, s2, s3, s4, s5, sum_s, sum_r,
):
    a = lax.axis_index("lat")
    b = lax.axis_index("lon")
    x, zh = div(a, 2), rem(a, 2)
    zl, y, c = div(b, 8), rem(div(b, 2), 4), rem(b, 2)
    z = zh * 4 + zl
    me_b = x * 4 + y
    me_a = z * 2 + c

    def peer_b(k):
        return device(div(k, 4), rem(k, 4), z, c)

    def peer_a(k):
        return device(x, y, div(k, 2), rem(k, 2))

    def neighbour(da, db):
        return (rem(a + da + 8, 8), rem(b + db + 32, 32))

    loads = {}
    for i, (name, src, dst) in enumerate(
        (
            ("fields", fields_hbm, fields), ("pat", pat_hbm, pat), ("cot", cot_hbm, cot),
            ("bias", bias_hbm, bias), ("taps", taps_hbm, taps), ("gain", gain_hbm, gain),
            ("wqkv", wqkv_hbm, wqkv), ("wo", wo_hbm, wo),
        )
    ):
        loads[name] = pltpu.make_async_copy(src, dst, w_sem.at[i])
        if i < 3:
            loads[name].start()

    bar = pltpu.get_barrier_semaphore()

    def greet(d, carry):
        pl.semaphore_signal(bar, inc=1, device_id=peer_b(rem(me_b + d, 16)), device_id_type=MESH)
        pl.semaphore_signal(bar, inc=1, device_id=peer_a(rem(me_a + d, 16)), device_id_type=MESH)
        return carry

    offsets = [(-1, 0), (1, 0), (0, -1), (0, 1), (-1, -1), (-1, 1), (1, -1), (1, 1)]
    for da, db in offsets:
        pl.semaphore_signal(bar, inc=1, device_id=neighbour(da, db), device_id_type=MESH)
    for d in range(1, 4):
        pl.semaphore_signal(
            bar, inc=1, device_id=device(rem(x + d, 4), y, rem(z + 4, 8), c), device_id_type=MESH
        )
    lax.fori_loop(1, 16, greet, 0, unroll=15)

    row8 = lax.broadcasted_iota(jnp.int32, (8, D), 0)
    row32 = lax.broadcasted_iota(jnp.int32, (32, D), 0)

    def fill_edges(source, dest, corner):
        left = jnp.zeros((8, D), F32)
        right = jnp.zeros((8, D), F32)
        for l in range(8):
            row = source[l].astype(F32)
            left = jnp.where(row8 == l, row[0:1, :], left)
            right = jnp.where(row8 == l, row[31:32, :], right)
        dest[0] = left.astype(BF)
        dest[1] = right.astype(BF)
        corner[0] = left[0:1].astype(BF)
        corner[1] = right[0:1].astype(BF)
        corner[2] = left[7:8].astype(BF)
        corner[3] = right[7:8].astype(BF)

    def arrived(ref, sem):
        pltpu.make_async_copy(ref, ref, sem).wait()

    def halo_start(kinds, source, edge, corner, rows, cols, corner_to, ss, rs):
        routes = [
            (source.at[0], rows.at[1], 0), (source.at[7], rows.at[0], 0),
            (edge.at[0], cols.at[1], 1), (edge.at[1], cols.at[0], 1),
            (corner.at[0], corner_to.at[3], 2), (corner.at[1], corner_to.at[2], 2),
            (corner.at[2], corner_to.at[1], 2), (corner.at[3], corner_to.at[0], 2),
        ]
        for m, (src, dst, kind) in enumerate(routes):
            if kind not in kinds:
                continue
            pltpu.make_async_remote_copy(
                src_ref=src, dst_ref=dst, send_sem=ss.at[kind], recv_sem=rs.at[kind],
                device_id=neighbour(*offsets[m]), device_id_type=MESH,
            ).start()

    def halo_wait(kinds, rows, cols, corner_to, ss, rs):
        for kind in kinds:
            ref = (rows, cols, corner_to)[kind]
            arrived(ref, ss.at[kind])
            arrived(ref, rs.at[kind])

    top_mask = (a > 0).astype(F32)
    bottom_mask = (a < 7).astype(F32)

    def fill_inside(source):
        for r in range(1, 9):
            f = source[r - 1].astype(F32)
            shifted[0, r] = pltpu.roll(f, 1, 0)
            shifted[1, r] = f
            shifted[2, r] = pltpu.roll(f, 31, 0)

    def fill_rows(rows, corner):
        for r, n, mask in ((0, 0, top_mask), (9, 1, bottom_mask)):
            f = rows[n].astype(F32) * mask
            le = corner[2 * n].astype(F32) * mask
            ri = corner[2 * n + 1].astype(F32) * mask
            shifted[0, r] = jnp.where(row32 == 0, le, pltpu.roll(f, 1, 0))
            shifted[1, r] = f
            shifted[2, r] = jnp.where(row32 == 31, ri, pltpu.roll(f, 31, 0))

    def fill_cols(cols):
        le = cols[0].astype(F32)
        ri = cols[1].astype(F32)
        for r in range(1, 9):
            shifted[0, r, 0:1, :] = le[r - 1 : r, :]
            shifted[2, r, 31:32, :] = ri[r - 1 : r, :]

    def exchange(peer, me, src, dst, slot, sends):
        if not sends:
            arrived(src.at[pl.ds(0, 15)], a2a_s.at[slot])
            arrived(dst.at[pl.ds(0, 15)], a2a_r.at[slot])
            return

        def step(d, carry):
            k = rem(me + d, 16)
            pltpu.make_async_remote_copy(
                src_ref=src.at[k], dst_ref=dst.at[me],
                send_sem=a2a_s.at[slot], recv_sem=a2a_r.at[slot],
                device_id=peer(k), device_id_type=MESH,
            ).start()
            return carry

        lax.fori_loop(1, 16, step, 0, unroll=15)
        dst[me] = src[me]

    def permute(perm, src, dst):
        for n in range(3):
            cols = slice(n * 256, (n + 1) * 256)
            rows = src[..., cols].reshape(256, 256)
            got = nn(perm[...], rows).astype(BF)
            dst[..., cols] = got.reshape(dst.shape[:-1] + (256,))

    def permute_out(perm, src, dst, half):
        rows = src[..., half * 384 : (half + 1) * 384].reshape(256, 384)
        dst[half] = nn(perm[half], rows).astype(BF).reshape(16, 16, 384)

    def permute_mid(src, dst, half):
        dst[half] = nn(perm_swap[...], src[half].reshape(256, 384)).astype(BF).reshape(16, 16, 384)

    def permute_in(perm, src, dst, half):
        got = nn(perm[half], src[half].reshape(256, 384)).astype(BF)
        dst[:, half * 384 : (half + 1) * 384] = got

    loads["fields"].wait()
    fill_edges(fields, edges, corners)
    pl.semaphore_wait(bar, 41)
    halo_start((0, 1, 2), fields, edges, corners, rows_in, cols_in, corner_in, halo_s, halo_r)

    for name in ("bias", "taps", "gain", "wqkv", "wo"):
        loads[name].start()

    loads["pat"].wait()
    pat_hot = one_hot(iota2(0) == pat[...])
    for half, first, second in ((0, slot_order, arrival_order), (1, arrival_order, slot_order)):
        order_hot = one_hot(iota2(0) == first(iota2(1)))
        perm_out[half] = nt(order_hot, pat_hot).astype(BF)
        perm_home[half] = nt(pat_hot, order_hot).astype(BF)
        perm_pos[half] = one_hot(iota2(1) == second(iota2(0)))
        perm_arr[half] = one_hot(iota2(0) == second(iota2(1)))
    perm_swap[...] = one_hot(iota2(1) == (iota2(0) & 15) * 16 + (iota2(0) >> 4))
    first_peer = ((peer_b, me_b), (peer_a, me_a))
    second_peer = ((peer_a, me_a), (peer_b, me_b))

    loads["cot"].wait()
    permute_out(perm_out, cot, c0, 0)
    exchange(*first_peer[0], c0.at[0], c1.at[0], 4, True)
    permute_out(perm_out, cot, c0, 1)
    exchange(*first_peer[1], c0.at[1], c1.at[1], 5, True)

    loads["bias"].wait()
    for q in range(6):
        bias_t[q] = jnp.transpose(bias[4 * q : 4 * q + 4].reshape(256, 64))

    fill_inside(fields)
    loads["taps"].wait()
    loads["gain"].wait()
    gain_row = gain[...].reshape(1, D)
    halo_f = (rows_in, cols_in, corner_in, halo_s, halo_r)
    halo_wait((1,), *halo_f)
    fill_cols(cols_in)

    def conv_row(l, flip):
        out = shifted[1, l + 1]
        for i in range(3):
            for j in range(3):
                ti, tj = (2 - i, 2 - j) if flip else (i, j)
                out = out + taps[ti, tj : tj + 1, :] * shifted[j, l + i]
        return out

    def norm_row(l, carry):
        h = conv_row(l, False).astype(BF)
        hid[l] = h
        hf = h.astype(F32)
        mean = jnp.mean(hf, axis=-1, keepdims=True)
        rem = hf - mean
        var = jnp.mean(rem * rem, axis=-1, keepdims=True)
        inv = lax.rsqrt(var + EPS)
        xh = rem * inv
        xhat[l] = xh
        rstd[l] = inv
        normed_w[l] = (xh * gain_row).astype(BF)
        return carry

    lax.fori_loop(1, 7, norm_row, 0, unroll=2)
    halo_wait((0, 2), *halo_f)
    fill_rows(rows_in, corner_in)
    norm_row(0, 0)
    norm_row(7, 0)
    for h in range(2):
        permute_out(perm_out, normed_w, n0, h)
        exchange(*first_peer[h], n0.at[h], n1.at[h], h, True)
    for h in range(2):
        exchange(*first_peer[h], n0.at[h], n1.at[h], h, False)
        permute_mid(n1, n2, h)
        exchange(*second_peer[h], n2.at[h], n3.at[h], 2 + h, True)
    for h in range(2):
        exchange(*first_peer[h], c0.at[h], c1.at[h], 4 + h, False)
        permute_mid(c1, c2, h)
        exchange(*second_peer[h], c2.at[h], c3.at[h], 6 + h, True)

    exchange(*second_peer[1], n2.at[1], n3.at[1], 3, False)
    permute_in(perm_pos, n3, nrm_g, 1)
    loads["wqkv"].wait()
    for n in range(6):
        cols = slice(n * 384, (n + 1) * 384)
        qkv_part[:, cols] = nn(nrm_g[:, 384:], wqkv[384:, cols])
    exchange(*second_peer[0], n2.at[0], n3.at[0], 2, False)
    permute_in(perm_pos, n3, nrm_g, 0)
    for n in range(6):
        cols = slice(n * 384, (n + 1) * 384)
        qkv[:, cols] = (nn(nrm_g[:, :384], wqkv[:384, cols]) + qkv_part[:, cols]).astype(BF)

    lane_head = lax.broadcasted_iota(jnp.int32, (64, 128), 1) >> 5

    own_head = [one_hot(lane_head == e) for e in range(4)]

    def spread(v):
        return jnp.concatenate([v * own_head[e] for e in range(4)], axis=0)

    def gather(v):
        out = jnp.zeros((64, 128), F32)
        for e in range(4):
            out = jnp.where(lane_head == e, v[e * 64 : (e + 1) * 64, :], out)
        return out

    def columns(q, part):
        return pl.ds(pl.multiple_of(q * 128 + part * D, 128), 128)

    def attend(q, carry):
        for g in range(4):
            rows = slice(g * 64, (g + 1) * 64)
            q_bd = spread(qkv[rows, columns(q, 0)])
            st = nt(qkv[rows, columns(q, 1)], q_bd) * HEAD_SCALE + bias_t[q]
            e = jnp.exp(st - jnp.max(st, axis=0, keepdims=True))
            p = e * (1.0 / jnp.sum(e, axis=0, keepdims=True))
            probs[q, g] = p
            att[rows, columns(q, 0)] = gather(tn(p.astype(BF), qkv[rows, columns(q, 2)])).astype(BF)
        return carry

    def attend_back(q, carry):
        for g in range(4):
            rows = slice(g * 64, (g + 1) * 64)
            q_bd = spread(qkv[rows, columns(q, 0)])
            g_bd = spread(grad_att[rows, columns(q, 0)])
            p = probs[q, g]
            dp = nt(qkv[rows, columns(q, 2)], g_bd)
            ds = (p * (dp - jnp.sum(p * dp, axis=0, keepdims=True))).astype(BF)
            dq = gather(tn(ds, qkv[rows, columns(q, 1)])) * HEAD_SCALE
            gqkv[rows, columns(q, 0)] = dq.astype(BF)
            gqkv[rows, columns(q, 1)] = (nn(ds, q_bd) * HEAD_SCALE).astype(BF)
            gqkv[rows, columns(q, 2)] = nn(p.astype(BF), g_bd).astype(BF)
        return carry

    lax.fori_loop(0, 6, attend, 0, unroll=2)

    loads["wo"].wait()
    for n in range(3):
        cols = slice(n * 256, (n + 1) * 256)
        work2[:, cols] = nn(att[...], wo[:, cols]).astype(BF)
    permute(perm_arr.at[0], work2, m0)
    exchange(peer_a, me_a, m0, m1, 8, True)

    for h in range(2):
        exchange(*second_peer[h], c2.at[h], c3.at[h], 6 + h, False)
        permute_in(perm_pos, c3, cot_g, h)

    def gp_y(d):
        k = rem(y + d, 4)
        pltpu.make_async_remote_copy(
            src_ref=gpa.at[:, k], dst_ref=gp1.at[y], send_sem=gp_s.at[0], recv_sem=gp_r.at[0],
            device_id=device(x, k, z, c), device_id_type=MESH,
        ).start()

    def gp_z(d):
        k = rem(zl + d, 4)
        pltpu.make_async_remote_copy(
            src_ref=gp3.at[k], dst_ref=gp4.at[zl], send_sem=gp_s.at[2], recv_sem=gp_r.at[2],
            device_id=device(x, y, zh * 4 + k, c), device_id_type=MESH,
        ).start()

    def gp_l(d):
        k = rem(a + d, 8)
        pltpu.make_async_remote_copy(
            src_ref=gp6.at[k], dst_ref=gp7.at[a], send_sem=gp_s.at[3], recv_sem=gp_r.at[3],
            device_id=(k, b), device_id_type=MESH,
        ).start()

    def gp_arrived(ref, n, stage):
        arrived(ref.at[pl.ds(0, n)], gp_s.at[stage])
        arrived(ref.at[pl.ds(0, n)], gp_r.at[stage])

    for n in range(3):
        cols = slice(n * 256, (n + 1) * 256)
        grad_att[:, cols] = nt(cot_g[...], wo[cols, :]).astype(BF)

    lax.fori_loop(0, 6, attend_back, 0, unroll=3)

    for half in range(2):
        cols = slice(half * 384, (half + 1) * 384)
        work[:, cols] = nt(gqkv[...], wqkv[cols, :]).astype(BF)
        permute_out(perm_arr, work, g0, half)
        exchange(*second_peer[half], g0.at[half], g1.at[half], 10 + half, True)

    def outer(n, carry):
        cols = pl.ds(pl.multiple_of(n * 384, 128), 384)
        got = tn(cot_g[:, cols], att[...])
        gp0[pl.ds(2 * n, 2)] = got.reshape(2, 4, 2, 24, D).astype(BF)
        return carry

    lax.fori_loop(0, 2, outer, 0)
    core = pltpu.make_async_remote_copy(
        src_ref=gp0.at[:, :, 1 - c], dst_ref=gpx, send_sem=gp_s.at[1], recv_sem=gp_r.at[1],
        device_id=device(x, y, z, 1 - c), device_id_type=MESH,
    )
    core.start()

    def forward_half(half):
        exchange(*second_peer[half], g0.at[half], g1.at[half], 10 + half, False)
        permute_mid(g1, g2, half)
        exchange(*first_peer[half], g2.at[half], g3.at[half], 12 + half, True)

    forward_half(1)
    core.wait()
    for k in range(4):
        gpa[k] = (gp0[k, :, c].astype(F32) + gpx[k].astype(F32)).astype(BF)
    for d in range(1, 4):
        gp_y(d)
    for k in range(4):
        gp1[y, k] = gpa[k, y]
    forward_half(0)

    exchange(peer_a, me_a, m0, m1, 8, False)
    permute(perm_swap, m1, m2)
    exchange(peer_b, me_b, m2, m3, 9, True)

    gp_arrived(gp1, 3, 0)
    for k in range(4):
        total = gp1[0, k].astype(F32)
        for i in range(1, 4):
            total = total + gp1[i, k].astype(F32)
        gp3[k] = total.astype(BF)
    for d in range(1, 4):
        gp_z(d)
    gp4[zl] = gp3[zl]

    for half in range(2):
        exchange(*first_peer[half], g2.at[half], g3.at[half], 12 + half, False)
        permute_in(perm_home, g3, work, half)
    acc[...] = jnp.zeros_like(acc)

    def norm_back(l, carry):
        at = l * 32 if isinstance(l, int) else pl.multiple_of(l * 32, 32)
        ng = work[pl.ds(at, 32), :].astype(F32)
        xh = xhat[l]
        prod = ng * xh
        acc[9] += jnp.sum(prod.reshape(4, 8, D), axis=0)
        u = ng * gain_row
        mu = jnp.mean(u, axis=-1, keepdims=True)
        mux = jnp.mean(prod * gain_row, axis=-1, keepdims=True)
        gh = cot[l].astype(F32) + rstd[l] * (u - mu - xh * mux)
        ghb = gh.astype(BF)
        normed_w[l] = ghb
        ghf = ghb.astype(F32)
        for i in range(3):
            for j in range(3):
                acc[3 * i + j] += jnp.sum((shifted[j, l + i] * ghf).reshape(4, 8, D), axis=0)
        return carry

    halo_g = (normed_w, edges_g, corners_g, rows_in_g, cols_in_g, corner_in_g, halo_gs, halo_gr)
    norm_back(0, 0)
    norm_back(7, 0)
    halo_start((0,), *halo_g)
    lax.fori_loop(1, 7, norm_back, 0, unroll=2)
    fill_edges(normed_w, edges_g, corners_g)
    halo_start((1, 2), *halo_g)

    for k in range(16):
        if k < 10:
            s0[k] = jnp.sum(acc[k], axis=0, keepdims=True)
        else:
            s0[k] = jnp.zeros((1, D), F32)

    def sums(peer, me, src, dst, slot, whole_src, sends):
        if not sends:
            arrived(dst.at[pl.ds(0, 15)], sum_s.at[slot])
            arrived(dst.at[pl.ds(0, 15)], sum_r.at[slot])
            return

        def step(d, carry):
            k = rem(me + d, 16)
            pltpu.make_async_remote_copy(
                src_ref=src if whole_src else src.at[k], dst_ref=dst.at[me],
                send_sem=sum_s.at[slot], recv_sem=sum_r.at[slot],
                device_id=peer(k), device_id_type=MESH,
            ).start()
            return carry

        lax.fori_loop(1, 16, step, 0, unroll=15)
        dst[me] = src[...] if whole_src else src[me]

    sums(peer_b, me_b, s0, s1, 0, False, True)
    fill_inside(normed_w)
    exchange(peer_b, me_b, m2, m3, 9, False)
    permute(perm_home.at[0], m3, work2)
    for l in range(8):
        block_v[l] = (hid[l].astype(F32) + work2[l * 32 : (l + 1) * 32, :].astype(F32)).astype(BF)
    block_copy = pltpu.make_async_copy(block_v, block_out, out_sem.at[8])
    block_copy.start()

    sums(peer_b, me_b, s0, s1, 0, False, False)
    s2[...] = jnp.sum(s1[...], axis=0)
    sums(peer_a, me_a, s2, s3, 1, True, True)

    def grad_row(l, carry):
        grad_v[l] = conv_row(l, True).astype(BF)
        pltpu.make_async_copy(grad_v.at[l], grad_fields.at[l], out_sem.at[l]).start()
        return carry

    halo_b = (rows_in_g, cols_in_g, corner_in_g, halo_gs, halo_gr)
    halo_wait((1,), *halo_b)
    fill_cols(cols_in_g)
    lax.fori_loop(1, 7, grad_row, 0, unroll=2)

    gp_arrived(gp4, 3, 2)
    total = gp4[0].astype(F32)
    for i in range(1, 4):
        total = total + gp4[i].astype(F32)
    for i in range(8):
        gp6[i, :, 0:96] = total[:, i * 96 : (i + 1) * 96]
        gp6[i, :, 96:128] = jnp.zeros((24, 32), F32)
    for d in range(1, 8):
        gp_l(d)
    gp7[a] = gp6[a]

    sums(peer_a, me_a, s2, s3, 1, True, False)
    s4[...] = jnp.sum(s3[...], axis=0) * TOTAL_SCALE
    sums(peer_b, me_b, s4, s5, 2, True, True)

    halo_wait((0, 2), *halo_b)
    fill_rows(rows_in_g, corner_in_g)
    grad_row(0, 0)
    grad_row(7, 0)

    gp_arrived(gp7, 7, 3)
    gp_out[...] = (jnp.sum(gp7[...], axis=0) * TOTAL_SCALE)[:, 0:96]
    sums(peer_b, me_b, s4, s5, 2, True, False)
    for k in range(9):
        taps_out[k // 3, k % 3 : k % 3 + 1, :] = s5[k]
    gain_out[...] = s5[9].reshape(D)
    block_copy.wait()
    for l in range(8):
        pltpu.make_async_copy(grad_v.at[l], grad_fields.at[l], out_sem.at[l]).wait()


def hand_over(*refs):
    for k in range(5):
        refs[5 + k][...] = refs[k][...]


def body(
    fields, conv_kernel, layer_norm_gain, qkv_weight, out_weight, score_bias, pattern, cotangent
):
    vm = pl.BlockSpec(memory_space=pltpu.VMEM)
    hbm = pl.BlockSpec(memory_space=pl.ANY)
    dma = pltpu.SemaphoreType.DMA

    def vmem(shape, dtype):
        return pltpu.VMEM(shape, dtype)

    scratch = (
        [vmem((8, 32, D), BF), vmem((8, 32, D), BF), vmem((3, 3, D), F32), vmem((D,), F32), vmem((1, 256), jnp.int32)]
        + [vmem((D, 3 * D), BF), vmem((D, D), BF), vmem((24, 64, 64), F32), vmem((6, 64, 256), F32), dma((8,))]
        + [vmem((4, 1, D), BF)] * 4
        + [vmem((2, 8, D), BF), vmem((2, 8, D), BF)]
        + [vmem((2, 32, D), BF), vmem((2, 8, D), BF)] * 2
        + [dma((3,))] * 4
        + [vmem((3, 10, 32, D), F32), vmem((8, 32, D), BF), vmem((8, 32, D), F32), vmem((8, 32, 1), F32)]
        + [vmem((256, D), BF)] * 2
        + [vmem((8, 32, D), BF)]
        + [vmem((2, 256, 256), BF)] * 2
        + [vmem((256, 256), BF)]
        + [vmem((2, 256, 256), BF)] * 2
        + [vmem((2, 16, 16, D // 2), BF)] * 12
        + [vmem((16, 16, D), BF)] * 4
        + [dma((14,)), dma((14,))]
        + [vmem((256, 3 * D), F32), vmem((8, 32, D), BF), vmem((8, 32, D), BF), dma((9,))]
        + [vmem((6, 4, 64, 256), F32)]
        + [vmem((256, D), BF), vmem((256, D), BF), vmem((256, 3 * D), BF), vmem((256, D), BF), vmem((256, D), BF), vmem((256, 3 * D), BF)]
        + [vmem((4, 4, 2, 24, D), BF)]
        + [vmem((4, 4, 24, D), BF)] * 3
        + [vmem((4, 24, D), BF)] * 2
        + [vmem((8, 24, 128), F32), vmem((8, 24, 128), F32)]
        + [dma((4,)), dma((4,))]
        + [vmem((10, 8, D), F32), vmem((16, 1, D), F32), vmem((16, 1, D), F32), vmem((1, D), F32), vmem((16, 1, D), F32), vmem((1, D), F32), vmem((16, 1, D), F32)]
        + [dma((3,)), dma((3,))]
    )
    results = (
        jax.ShapeDtypeStruct((8, 32, D), BF),
        jax.ShapeDtypeStruct((8, 32, D), BF),
        jax.ShapeDtypeStruct((24, 96), F32),
        jax.ShapeDtypeStruct((3, 3, D), F32),
        jax.ShapeDtypeStruct((D,), F32),
    )
    out = pl.pallas_call(
        kernel,
        out_shape=results,
        in_specs=[hbm] * 8,
        out_specs=(hbm,) * 2 + (vm,) * 3,
        scratch_shapes=scratch,
        name="section",
        compiler_params=pltpu.CompilerParams(
            collective_id=0, has_side_effects=True, vmem_limit_bytes=60 << 20
        ),
    )(
        fields, cotangent, conv_kernel, layer_norm_gain,
        pattern.reshape(1, 256), qkv_weight, out_weight, score_bias,
    )
    block_out, grad_fields, gp, taps, gain = pl.pallas_call(
        hand_over, out_shape=results, in_specs=[vm] * 5, out_specs=(vm,) * 5,
        name="results",
    )(*out)
    return (block_out, grad_fields, jnp.transpose(gp), taps, gain)


def solution(mesh):
    split = P("lat", "lon", None)
    return jax.shard_map(
        body,
        mesh=mesh,
        in_specs=(split, P(), P(), P(), P(), P(), split, split),
        out_specs=(split, split, P("lat", "lon"), P(), P()),
        check_vma=False,
    )
```

```python
import math

import jax
import jax.numpy as jnp
from jax import lax
from jax.experimental import pallas as pl
from jax.experimental.pallas import tpu as pltpu
from jax.sharding import PartitionSpec as P

MESH = pl.DeviceIdType.MESH
BF = jnp.bfloat16
F32 = jnp.float32
D = 768
EPS = 1e-05
HEAD_SCALE = 32 ** (-0.5)
TOTAL_SCALE = 1.0 / math.sqrt(65536)


def nn(a, b):
    return lax.dot_general(a, b, (((1,), (0,)), ((), ())), preferred_element_type=F32)


def nt(a, b):
    return lax.dot_general(a, b, (((1,), (1,)), ((), ())), preferred_element_type=F32)


def tn(a, b):
    return lax.dot_general(a, b, (((0,), (0,)), ((), ())), preferred_element_type=F32)


def div(a, n):
    return lax.div(a, jnp.int32(n))


def rem(a, n):
    return lax.rem(a, jnp.int32(n))


def device(x, y, z, c):
    return (x * 2 + div(z, 4), rem(z, 4) * 8 + y * 2 + c)


def one_hot(cond):
    return jnp.where(cond, 1.0, 0.0).astype(BF)


def iota2(axis):
    return lax.broadcasted_iota(jnp.int32, (256, 256), axis)


def slot_order(s):
    x, zh, zl, y, c = s >> 6, (s >> 5) & 1, (s >> 3) & 3, (s >> 1) & 3, s & 1
    return x * 64 + y * 16 + zh * 8 + zl * 2 + c


def arrival_order(p):
    x, zh, zl, y, c = p >> 6, (p >> 5) & 1, (p >> 3) & 3, (p >> 1) & 3, p & 1
    return zh * 128 + zl * 32 + c * 16 + x * 4 + y


def kernel(
    fields_hbm, cot_hbm, taps_hbm, gain_hbm, pat_hbm, wqkv_hbm, wo_hbm, bias_hbm,
    block_out, grad_fields, gp_out, taps_out, gain_out,
    fields, cot, taps, gain, pat, wqkv, wo, bias, bias_t, w_sem,
    corners, corners_g, corner_in, corner_in_g, edges, edges_g, rows_in, cols_in, rows_in_g, cols_in_g, halo_s, halo_r, halo_gs, halo_gr,
    shifted, hid, xhat, rstd, work, work2, normed_w,
    perm_out, perm_home, perm_swap, perm_pos, perm_arr,
    c0, c1, c2, c3, n0, n1, n2, n3, g0, g1, g2, g3, m0, m1, m2, m3, a2a_s, a2a_r,
    qkv_part, block_v, grad_v, out_sem, probs, cot_g, nrm_g, qkv, grad_att, att, gqkv,
    gp0, gpx, gpa, gp1, gp3, gp4, gp6, gp7, gp_s, gp_r,
    acc, s0, s1, s2, s3, s4, s5, sum_s, sum_r,
):
    a = lax.axis_index("lat")
    b = lax.axis_index("lon")
    x, zh = div(a, 2), rem(a, 2)
    zl, y, c = div(b, 8), rem(div(b, 2), 4), rem(b, 2)
    z = zh * 4 + zl
    me_b = x * 4 + y
    me_a = z * 2 + c

    def peer_b(k):
        return device(div(k, 4), rem(k, 4), z, c)

    def peer_a(k):
        return device(x, y, div(k, 2), rem(k, 2))

    def neighbour(da, db):
        return (rem(a + da + 8, 8), rem(b + db + 32, 32))

    loads = {}
    for i, (name, src, dst) in enumerate(
        (
            ("fields", fields_hbm, fields), ("pat", pat_hbm, pat), ("cot", cot_hbm, cot),
            ("bias", bias_hbm, bias), ("taps", taps_hbm, taps), ("gain", gain_hbm, gain),
            ("wqkv", wqkv_hbm, wqkv), ("wo", wo_hbm, wo),
        )
    ):
        loads[name] = pltpu.make_async_copy(src, dst, w_sem.at[i])
        if i < 3:
            loads[name].start()

    bar = pltpu.get_barrier_semaphore()

    def greet(d, carry):
        pl.semaphore_signal(bar, inc=1, device_id=peer_b(rem(me_b + d, 16)), device_id_type=MESH)
        pl.semaphore_signal(bar, inc=1, device_id=peer_a(rem(me_a + d, 16)), device_id_type=MESH)
        return carry

    offsets = [(-1, 0), (1, 0), (0, -1), (0, 1), (-1, -1), (-1, 1), (1, -1), (1, 1)]
    for da, db in offsets:
        pl.semaphore_signal(bar, inc=1, device_id=neighbour(da, db), device_id_type=MESH)
    for d in range(1, 4):
        pl.semaphore_signal(
            bar, inc=1, device_id=device(rem(x + d, 4), y, rem(z + 4, 8), c), device_id_type=MESH
        )
    lax.fori_loop(1, 16, greet, 0, unroll=15)

    row8 = lax.broadcasted_iota(jnp.int32, (8, D), 0)
    row32 = lax.broadcasted_iota(jnp.int32, (32, D), 0)

    def fill_edges(source, dest, corner):
        left = jnp.zeros((8, D), F32)
        right = jnp.zeros((8, D), F32)
        for l in range(8):
            row = source[l].astype(F32)
            left = jnp.where(row8 == l, row[0:1, :], left)
            right = jnp.where(row8 == l, row[31:32, :], right)
        dest[0] = left.astype(BF)
        dest[1] = right.astype(BF)
        corner[0] = left[0:1].astype(BF)
        corner[1] = right[0:1].astype(BF)
        corner[2] = left[7:8].astype(BF)
        corner[3] = right[7:8].astype(BF)

    def arrived(ref, sem):
        pltpu.make_async_copy(ref, ref, sem).wait()

    def halo_start(kinds, source, edge, corner, rows, cols, corner_to, ss, rs):
        routes = [
            (source.at[0], rows.at[1], 0), (source.at[7], rows.at[0], 0),
            (edge.at[0], cols.at[1], 1), (edge.at[1], cols.at[0], 1),
            (corner.at[0], corner_to.at[3], 2), (corner.at[1], corner_to.at[2], 2),
            (corner.at[2], corner_to.at[1], 2), (corner.at[3], corner_to.at[0], 2),
        ]
        for m, (src, dst, kind) in enumerate(routes):
            if kind not in kinds:
                continue
            pltpu.make_async_remote_copy(
                src_ref=src, dst_ref=dst, send_sem=ss.at[kind], recv_sem=rs.at[kind],
                device_id=neighbour(*offsets[m]), device_id_type=MESH,
            ).start()

    def halo_wait(kinds, rows, cols, corner_to, ss, rs):
        for kind in kinds:
            ref = (rows, cols, corner_to)[kind]
            arrived(ref, ss.at[kind])
            arrived(ref, rs.at[kind])

    top_mask = (a > 0).astype(F32)
    bottom_mask = (a < 7).astype(F32)

    def fill_inside(source):
        for r in range(1, 9):
            f = source[r - 1].astype(F32)
            shifted[0, r] = pltpu.roll(f, 1, 0)
            shifted[1, r] = f
            shifted[2, r] = pltpu.roll(f, 31, 0)

    def fill_rows(rows, corner):
        for r, n, mask in ((0, 0, top_mask), (9, 1, bottom_mask)):
            f = rows[n].astype(F32) * mask
            le = corner[2 * n].astype(F32) * mask
            ri = corner[2 * n + 1].astype(F32) * mask
            shifted[0, r] = jnp.where(row32 == 0, le, pltpu.roll(f, 1, 0))
            shifted[1, r] = f
            shifted[2, r] = jnp.where(row32 == 31, ri, pltpu.roll(f, 31, 0))

    def fill_cols(cols):
        le = cols[0].astype(F32)
        ri = cols[1].astype(F32)
        for r in range(1, 9):
            shifted[0, r, 0:1, :] = le[r - 1 : r, :]
            shifted[2, r, 31:32, :] = ri[r - 1 : r, :]

    def exchange(peer, me, src, dst, slot, sends):
        if not sends:
            arrived(src.at[pl.ds(0, 15)], a2a_s.at[slot])
            arrived(dst.at[pl.ds(0, 15)], a2a_r.at[slot])
            return

        def step(d, carry):
            k = rem(me + d, 16)
            pltpu.make_async_remote_copy(
                src_ref=src.at[k], dst_ref=dst.at[me],
                send_sem=a2a_s.at[slot], recv_sem=a2a_r.at[slot],
                device_id=peer(k), device_id_type=MESH,
            ).start()
            return carry

        lax.fori_loop(1, 16, step, 0, unroll=15)
        dst[me] = src[me]

    def permute(perm, src, dst):
        for n in range(3):
            cols = slice(n * 256, (n + 1) * 256)
            rows = src[..., cols].reshape(256, 256)
            got = nn(perm[...], rows).astype(BF)
            dst[..., cols] = got.reshape(dst.shape[:-1] + (256,))

    def permute_out(perm, src, dst, half):
        rows = src[..., half * 384 : (half + 1) * 384].reshape(256, 384)
        dst[half] = nn(perm[half], rows).astype(BF).reshape(16, 16, 384)

    def permute_mid(src, dst, half):
        dst[half] = nn(perm_swap[...], src[half].reshape(256, 384)).astype(BF).reshape(16, 16, 384)

    def permute_in(perm, src, dst, half):
        got = nn(perm[half], src[half].reshape(256, 384)).astype(BF)
        dst[:, half * 384 : (half + 1) * 384] = got

    loads["fields"].wait()
    fill_edges(fields, edges, corners)
    pl.semaphore_wait(bar, 41)
    halo_start((0, 1, 2), fields, edges, corners, rows_in, cols_in, corner_in, halo_s, halo_r)

    for name in ("bias", "taps", "gain", "wqkv", "wo"):
        loads[name].start()

    loads["pat"].wait()
    pat_hot = one_hot(iota2(0) == pat[...])
    for half, first, second in ((0, slot_order, arrival_order), (1, arrival_order, slot_order)):
        order_hot = one_hot(iota2(0) == first(iota2(1)))
        perm_out[half] = nt(order_hot, pat_hot).astype(BF)
        perm_home[half] = nt(pat_hot, order_hot).astype(BF)
        perm_pos[half] = one_hot(iota2(1) == second(iota2(0)))
        perm_arr[half] = one_hot(iota2(0) == second(iota2(1)))
    perm_swap[...] = one_hot(iota2(1) == (iota2(0) & 15) * 16 + (iota2(0) >> 4))
    first_peer = ((peer_b, me_b), (peer_a, me_a))
    second_peer = ((peer_a, me_a), (peer_b, me_b))

    loads["cot"].wait()
    permute_out(perm_out, cot, c0, 0)
    exchange(*first_peer[0], c0.at[0], c1.at[0], 4, True)
    permute_out(perm_out, cot, c0, 1)
    exchange(*first_peer[1], c0.at[1], c1.at[1], 5, True)

    loads["bias"].wait()
    for q in range(6):
        bias_t[q] = jnp.transpose(bias[4 * q : 4 * q + 4].reshape(256, 64))

    fill_inside(fields)
    loads["taps"].wait()
    loads["gain"].wait()
    gain_row = gain[...].reshape(1, D)
    halo_f = (rows_in, cols_in, corner_in, halo_s, halo_r)
    halo_wait((1,), *halo_f)
    fill_cols(cols_in)

    def conv_row(l, flip):
        out = shifted[1, l + 1]
        for i in range(3):
            for j in range(3):
                ti, tj = (2 - i, 2 - j) if flip else (i, j)
                out = out + taps[ti, tj : tj + 1, :] * shifted[j, l + i]
        return out

    def norm_row(l, carry):
        h = conv_row(l, False).astype(BF)
        hid[l] = h
        hf = h.astype(F32)
        mean = jnp.mean(hf, axis=-1, keepdims=True)
        rem = hf - mean
        var = jnp.mean(rem * rem, axis=-1, keepdims=True)
        inv = lax.rsqrt(var + EPS)
        xh = rem * inv
        xhat[l] = xh
        rstd[l] = inv
        normed_w[l] = (xh * gain_row).astype(BF)
        return carry

    lax.fori_loop(1, 7, norm_row, 0, unroll=2)
    halo_wait((0, 2), *halo_f)
    fill_rows(rows_in, corner_in)
    norm_row(0, 0)
    norm_row(7, 0)
    for h in range(2):
        permute_out(perm_out, normed_w, n0, h)
        exchange(*first_peer[h], n0.at[h], n1.at[h], h, True)
    for h in range(2):
        exchange(*first_peer[h], n0.at[h], n1.at[h], h, False)
        permute_mid(n1, n2, h)
        exchange(*second_peer[h], n2.at[h], n3.at[h], 2 + h, True)
    for h in range(2):
        exchange(*first_peer[h], c0.at[h], c1.at[h], 4 + h, False)
        permute_mid(c1, c2, h)
        exchange(*second_peer[h], c2.at[h], c3.at[h], 6 + h, True)

    exchange(*second_peer[1], n2.at[1], n3.at[1], 3, False)
    permute_in(perm_pos, n3, nrm_g, 1)
    loads["wqkv"].wait()
    for n in range(6):
        cols = slice(n * 384, (n + 1) * 384)
        qkv_part[:, cols] = nn(nrm_g[:, 384:], wqkv[384:, cols])
    exchange(*second_peer[0], n2.at[0], n3.at[0], 2, False)
    permute_in(perm_pos, n3, nrm_g, 0)
    for n in range(6):
        cols = slice(n * 384, (n + 1) * 384)
        qkv[:, cols] = (nn(nrm_g[:, :384], wqkv[:384, cols]) + qkv_part[:, cols]).astype(BF)

    lane_head = lax.broadcasted_iota(jnp.int32, (64, 128), 1) >> 5

    own_head = [one_hot(lane_head == e) for e in range(4)]

    def spread(v):
        return jnp.concatenate([v * own_head[e] for e in range(4)], axis=0)

    def gather(v):
        out = jnp.zeros((64, 128), F32)
        for e in range(4):
            out = jnp.where(lane_head == e, v[e * 64 : (e + 1) * 64, :], out)
        return out

    def columns(q, part):
        return pl.ds(pl.multiple_of(q * 128 + part * D, 128), 128)

    def attend(q, carry):
        for g in range(4):
            rows = slice(g * 64, (g + 1) * 64)
            q_bd = spread(qkv[rows, columns(q, 0)])
            st = nt(qkv[rows, columns(q, 1)], q_bd) * HEAD_SCALE + bias_t[q]
            e = jnp.exp(st - jnp.max(st, axis=0, keepdims=True))
            p = e * (1.0 / jnp.sum(e, axis=0, keepdims=True))
            probs[q, g] = p
            att[rows, columns(q, 0)] = gather(tn(p.astype(BF), qkv[rows, columns(q, 2)])).astype(BF)
        return carry

    def attend_back(q, carry):
        for g in range(4):
            rows = slice(g * 64, (g + 1) * 64)
            q_bd = spread(qkv[rows, columns(q, 0)])
            g_bd = spread(grad_att[rows, columns(q, 0)])
            p = probs[q, g]
            dp = nt(qkv[rows, columns(q, 2)], g_bd)
            ds = (p * (dp - jnp.sum(p * dp, axis=0, keepdims=True))).astype(BF)
            dq = gather(tn(ds, qkv[rows, columns(q, 1)])) * HEAD_SCALE
            gqkv[rows, columns(q, 0)] = dq.astype(BF)
            gqkv[rows, columns(q, 1)] = (nn(ds, q_bd) * HEAD_SCALE).astype(BF)
            gqkv[rows, columns(q, 2)] = nn(p.astype(BF), g_bd).astype(BF)
        return carry

    lax.fori_loop(0, 6, attend, 0, unroll=2)

    loads["wo"].wait()
    for n in range(3):
        cols = slice(n * 256, (n + 1) * 256)
        work2[:, cols] = nn(att[...], wo[:, cols]).astype(BF)
    permute(perm_arr.at[0], work2, m0)
    exchange(peer_a, me_a, m0, m1, 8, True)

    for h in range(2):
        exchange(*second_peer[h], c2.at[h], c3.at[h], 6 + h, False)
        permute_in(perm_pos, c3, cot_g, h)

    def outer(n, carry):
        cols = pl.ds(pl.multiple_of(n * 384, 128), 384)
        got = tn(cot_g[:, cols], att[...])
        gp0[pl.ds(2 * n, 2)] = got.reshape(2, 4, 2, 24, D).astype(BF)
        return carry

    lax.fori_loop(0, 2, outer, 0)
    core = pltpu.make_async_remote_copy(
        src_ref=gp0.at[:, :, 1 - c], dst_ref=gpx, send_sem=gp_s.at[1], recv_sem=gp_r.at[1],
        device_id=device(x, y, z, 1 - c), device_id_type=MESH,
    )
    core.start()

    def gp_y(d):
        k = rem(y + d, 4)
        pltpu.make_async_remote_copy(
            src_ref=gpa.at[:, k], dst_ref=gp1.at[y], send_sem=gp_s.at[0], recv_sem=gp_r.at[0],
            device_id=device(x, k, z, c), device_id_type=MESH,
        ).start()

    def gp_z(d):
        k = rem(zl + d, 4)
        pltpu.make_async_remote_copy(
            src_ref=gp3.at[k], dst_ref=gp4.at[zl], send_sem=gp_s.at[2], recv_sem=gp_r.at[2],
            device_id=device(x, y, zh * 4 + k, c), device_id_type=MESH,
        ).start()

    def gp_l(d):
        k = rem(a + d, 8)
        pltpu.make_async_remote_copy(
            src_ref=gp6.at[k], dst_ref=gp7.at[a], send_sem=gp_s.at[3], recv_sem=gp_r.at[3],
            device_id=(k, b), device_id_type=MESH,
        ).start()

    def gp_arrived(ref, n, stage):
        arrived(ref.at[pl.ds(0, n)], gp_s.at[stage])
        arrived(ref.at[pl.ds(0, n)], gp_r.at[stage])

    for n in range(3):
        cols = slice(n * 256, (n + 1) * 256)
        grad_att[:, cols] = nt(cot_g[...], wo[cols, :]).astype(BF)

    lax.fori_loop(0, 3, attend_back, 0, unroll=3)
    core.wait()
    for k in range(4):
        gpa[k] = (gp0[k, :, c].astype(F32) + gpx[k].astype(F32)).astype(BF)
    for d in range(1, 4):
        gp_y(d)
    for k in range(4):
        gp1[y, k] = gpa[k, y]
    lax.fori_loop(3, 6, attend_back, 0, unroll=3)

    for half in range(2):
        cols = slice(half * 384, (half + 1) * 384)
        work[:, cols] = nt(gqkv[...], wqkv[cols, :]).astype(BF)
        permute_out(perm_arr, work, g0, half)
        exchange(*second_peer[half], g0.at[half], g1.at[half], 10 + half, True)

    for half in (1, 0):
        exchange(*second_peer[half], g0.at[half], g1.at[half], 10 + half, False)
        permute_mid(g1, g2, half)
        exchange(*first_peer[half], g2.at[half], g3.at[half], 12 + half, True)

    exchange(peer_a, me_a, m0, m1, 8, False)
    permute(perm_swap, m1, m2)
    exchange(peer_b, me_b, m2, m3, 9, True)

    gp_arrived(gp1, 3, 0)
    for k in range(4):
        total = gp1[0, k].astype(F32)
        for i in range(1, 4):
            total = total + gp1[i, k].astype(F32)
        gp3[k] = total.astype(BF)
    for d in range(1, 4):
        gp_z(d)
    gp4[zl] = gp3[zl]

    for half in range(2):
        exchange(*first_peer[half], g2.at[half], g3.at[half], 12 + half, False)
        permute_in(perm_home, g3, work, half)
    acc[...] = jnp.zeros_like(acc)

    def norm_back(l, carry):
        at = l * 32 if isinstance(l, int) else pl.multiple_of(l * 32, 32)
        ng = work[pl.ds(at, 32), :].astype(F32)
        xh = xhat[l]
        prod = ng * xh
        acc[9] += jnp.sum(prod.reshape(4, 8, D), axis=0)
        u = ng * gain_row
        mu = jnp.mean(u, axis=-1, keepdims=True)
        mux = jnp.mean(prod * gain_row, axis=-1, keepdims=True)
        gh = cot[l].astype(F32) + rstd[l] * (u - mu - xh * mux)
        ghb = gh.astype(BF)
        normed_w[l] = ghb
        ghf = ghb.astype(F32)
        for i in range(3):
            for j in range(3):
                acc[3 * i + j] += jnp.sum((shifted[j, l + i] * ghf).reshape(4, 8, D), axis=0)
        return carry

    halo_g = (normed_w, edges_g, corners_g, rows_in_g, cols_in_g, corner_in_g, halo_gs, halo_gr)
    norm_back(0, 0)
    norm_back(7, 0)
    halo_start((0,), *halo_g)
    lax.fori_loop(1, 7, norm_back, 0, unroll=2)
    fill_edges(normed_w, edges_g, corners_g)
    halo_start((1, 2), *halo_g)

    for k in range(16):
        if k < 10:
            s0[k] = jnp.sum(acc[k], axis=0, keepdims=True)
        else:
            s0[k] = jnp.zeros((1, D), F32)

    def sums(peer, me, src, dst, slot, whole_src, sends):
        if not sends:
            arrived(dst.at[pl.ds(0, 15)], sum_s.at[slot])
            arrived(dst.at[pl.ds(0, 15)], sum_r.at[slot])
            return

        def step(d, carry):
            k = rem(me + d, 16)
            pltpu.make_async_remote_copy(
                src_ref=src if whole_src else src.at[k], dst_ref=dst.at[me],
                send_sem=sum_s.at[slot], recv_sem=sum_r.at[slot],
                device_id=peer(k), device_id_type=MESH,
            ).start()
            return carry

        lax.fori_loop(1, 16, step, 0, unroll=15)
        dst[me] = src[...] if whole_src else src[me]

    sums(peer_b, me_b, s0, s1, 0, False, True)
    fill_inside(normed_w)
    exchange(peer_b, me_b, m2, m3, 9, False)
    permute(perm_home.at[0], m3, work2)
    for l in range(8):
        block_v[l] = (hid[l].astype(F32) + work2[l * 32 : (l + 1) * 32, :].astype(F32)).astype(BF)
    block_copy = pltpu.make_async_copy(block_v, block_out, out_sem.at[8])
    block_copy.start()

    sums(peer_b, me_b, s0, s1, 0, False, False)
    s2[...] = jnp.sum(s1[...], axis=0)
    sums(peer_a, me_a, s2, s3, 1, True, True)

    def grad_row(l, carry):
        grad_v[l] = conv_row(l, True).astype(BF)
        pltpu.make_async_copy(grad_v.at[l], grad_fields.at[l], out_sem.at[l]).start()
        return carry

    halo_b = (rows_in_g, cols_in_g, corner_in_g, halo_gs, halo_gr)
    halo_wait((1,), *halo_b)
    fill_cols(cols_in_g)
    lax.fori_loop(1, 7, grad_row, 0, unroll=2)

    gp_arrived(gp4, 3, 2)
    total = gp4[0].astype(F32)
    for i in range(1, 4):
        total = total + gp4[i].astype(F32)
    for i in range(8):
        gp6[i, :, 0:96] = total[:, i * 96 : (i + 1) * 96]
        gp6[i, :, 96:128] = jnp.zeros((24, 32), F32)
    for d in range(1, 8):
        gp_l(d)
    gp7[a] = gp6[a]

    sums(peer_a, me_a, s2, s3, 1, True, False)
    s4[...] = jnp.sum(s3[...], axis=0) * TOTAL_SCALE
    sums(peer_b, me_b, s4, s5, 2, True, True)

    halo_wait((0, 2), *halo_b)
    fill_rows(rows_in_g, corner_in_g)
    grad_row(0, 0)
    grad_row(7, 0)

    gp_arrived(gp7, 7, 3)
    gp_out[...] = (jnp.sum(gp7[...], axis=0) * TOTAL_SCALE)[:, 0:96]
    sums(peer_b, me_b, s4, s5, 2, True, False)
    for k in range(9):
        taps_out[k // 3, k % 3 : k % 3 + 1, :] = s5[k]
    gain_out[...] = s5[9].reshape(D)
    block_copy.wait()
    for l in range(8):
        pltpu.make_async_copy(grad_v.at[l], grad_fields.at[l], out_sem.at[l]).wait()


def hand_over(*refs):
    held, sem_in, sem_out = refs[10:15], refs[15], refs[16]
    moves = []
    for k in range(5):
        parts = [slice(0, 4), slice(4, 8)] if k < 2 else [slice(None)]
        for part in parts:
            i = len(moves)
            moves.append(
                (
                    pltpu.make_async_copy(refs[k].at[part], held[k].at[part], sem_in.at[i]),
                    pltpu.make_async_copy(held[k].at[part], refs[5 + k].at[part], sem_out.at[i]),
                )
            )
    for load, store in moves:
        load.start()
    for load, store in moves:
        load.wait()
        store.start()
    for load, store in moves:
        store.wait()


def body(
    fields, conv_kernel, layer_norm_gain, qkv_weight, out_weight, score_bias, pattern, cotangent
):
    vm = pl.BlockSpec(memory_space=pltpu.VMEM)
    hbm = pl.BlockSpec(memory_space=pl.ANY)
    dma = pltpu.SemaphoreType.DMA

    def vmem(shape, dtype):
        return pltpu.VMEM(shape, dtype)

    scratch = (
        [vmem((8, 32, D), BF), vmem((8, 32, D), BF), vmem((3, 3, D), F32), vmem((D,), F32), vmem((1, 256), jnp.int32)]
        + [vmem((D, 3 * D), BF), vmem((D, D), BF), vmem((24, 64, 64), F32), vmem((6, 64, 256), F32), dma((8,))]
        + [vmem((4, 1, D), BF)] * 4
        + [vmem((2, 8, D), BF), vmem((2, 8, D), BF)]
        + [vmem((2, 32, D), BF), vmem((2, 8, D), BF)] * 2
        + [dma((3,))] * 4
        + [vmem((3, 10, 32, D), F32), vmem((8, 32, D), BF), vmem((8, 32, D), F32), vmem((8, 32, 1), F32)]
        + [vmem((256, D), BF)] * 2
        + [vmem((8, 32, D), BF)]
        + [vmem((2, 256, 256), BF)] * 2
        + [vmem((256, 256), BF)]
        + [vmem((2, 256, 256), BF)] * 2
        + [vmem((2, 16, 16, D // 2), BF)] * 12
        + [vmem((16, 16, D), BF)] * 4
        + [dma((14,)), dma((14,))]
        + [vmem((256, 3 * D), F32), vmem((8, 32, D), BF), vmem((8, 32, D), BF), dma((9,))]
        + [vmem((6, 4, 64, 256), F32)]
        + [vmem((256, D), BF), vmem((256, D), BF), vmem((256, 3 * D), BF), vmem((256, D), BF), vmem((256, D), BF), vmem((256, 3 * D), BF)]
        + [vmem((4, 4, 2, 24, D), BF)]
        + [vmem((4, 4, 24, D), BF)] * 3
        + [vmem((4, 24, D), BF)] * 2
        + [vmem((8, 24, 128), F32), vmem((8, 24, 128), F32)]
        + [dma((4,)), dma((4,))]
        + [vmem((10, 8, D), F32), vmem((16, 1, D), F32), vmem((16, 1, D), F32), vmem((1, D), F32), vmem((16, 1, D), F32), vmem((1, D), F32), vmem((16, 1, D), F32)]
        + [dma((3,)), dma((3,))]
    )
    results = (
        jax.ShapeDtypeStruct((8, 32, D), BF),
        jax.ShapeDtypeStruct((8, 32, D), BF),
        jax.ShapeDtypeStruct((24, 96), F32),
        jax.ShapeDtypeStruct((3, 3, D), F32),
        jax.ShapeDtypeStruct((D,), F32),
    )
    out = pl.pallas_call(
        kernel,
        out_shape=results,
        in_specs=[hbm] * 8,
        out_specs=(hbm,) * 2 + (vm,) * 3,
        scratch_shapes=scratch,
        name="section",
        compiler_params=pltpu.CompilerParams(
            collective_id=0, has_side_effects=True, vmem_limit_bytes=60 << 20
        ),
    )(
        fields, cotangent, conv_kernel, layer_norm_gain,
        pattern.reshape(1, 256), qkv_weight, out_weight, score_bias,
    )
    block_out, grad_fields, gp, taps, gain = pl.pallas_call(
        hand_over, out_shape=results, in_specs=[hbm] * 5, out_specs=(hbm,) * 5,
        scratch_shapes=[vmem(r.shape, r.dtype) for r in results] + [dma((7,)), dma((7,))],
        name="results",
    )(*out)
    return (block_out, grad_fields, jnp.transpose(gp), taps, gain)


def solution(mesh):
    split = P("lat", "lon", None)
    return jax.shard_map(
        body,
        mesh=mesh,
        in_specs=(split, P(), P(), P(), P(), P(), split, split),
        out_specs=(split, split, P("lat", "lon"), P(), P()),
        check_vma=False,
    )
```
